512 devices in a mesh: gx: 32 (over y, x), gy: 16 (over z, core).
Axes of the slice: x: 4, y: 8, z: 8, core: 2. Of those that a mesh axis runs over, the one named last changes fastest.
Arguments:
- source: float32 [256, 256, 256], P('gx', 'gy'), may hold values from -6 to 6
- initial: float32 [256, 256, 256], P('gx', 'gy'), may hold values from -6 to 6
- absorption: float32 [256, 256, 256], P('gx', 'gy'), may hold values from 0.01 to 0.2
- beta_x: float32 [256, 256, 256], P('gx', 'gy'), may hold values from 0.4 to 2.5
- beta_y: float32 [256, 256, 256], P('gx', 'gy'), may hold values from 0.4 to 2.5
- beta_z: float32 [256, 256, 256], P('gx', 'gy'), may hold values from 0.4 to 2.5
Outputs:
- solution: float32 [256, 256, 256], P('gx', 'gy')
The draws below stay inside these ranges and needn't reach their ends.
All inputs are finite; a program needn't handle non-finite values.
Results may differ from the reference program's by a relative error of at most 0.00002.
Values sent between devices are 32-bit elements; how exact they have to be, the bound alone decides.
A program may use at most 64 MiB of HBM per device.

```python
import math
import jax
import jax.numpy as jnp

NZ = 256
SWEEPS = 4
COARSE_SWEEPS = 8
NX = 256
NY = 256


def log_spread(key, low, high):
    values = jnp.exp(jax.random.uniform(key, (NX, NY, NZ), jnp.float32, math.log(low), math.log(high)))
    return jnp.clip(values, low, high)


def draw_absorption(key, part):
    own_key = jax.random.fold_in(key, 101)
    return log_spread(own_key, 0.01, 0.2)


def draw_beta_x(key, part):
    own_key = jax.random.fold_in(key, 202)
    return log_spread(own_key, 0.4, 2.5)


def draw_beta_y(key, part):
    own_key = jax.random.fold_in(key, 303)
    return log_spread(own_key, 0.4, 2.5)


def draw_beta_z(key, part):
    own_key = jax.random.fold_in(key, 404)
    return log_spread(own_key, 0.4, 2.5)


def steps_of(key, dims, split, low, high):
    def one(dim, parts):
        heights = jax.random.uniform(jax.random.fold_in(jax.random.fold_in(key, 6), dim), (parts,), jnp.float32, low / len(split), high / len(split))
        return jnp.repeat(jnp.exp(heights), dims[dim] // parts).reshape((-1,) + (1,) * (len(dims) - dim - 1))

    gain = one(*split[0])
    for cut in split[1:]:
        gain = gain * one(*cut)
    return gain


def noise(rng, shape, scale, limit, cuts=(), kind=jnp.bfloat16):
    entries = jax.random.normal(rng, shape, jnp.float32) * scale
    if len(cuts) > 0:
        entries = steps_of(rng, shape, cuts, -0.22, 0.18) * entries
    return jnp.clip(entries, min=-limit, max=limit).astype(kind)


def setup_inputs(seed: int = 0) -> dict:
    key_list = jax.random.split(jax.random.key(seed), 7)
    return {
        "source": noise(key_list[0], (NX, NY, NZ), 1.0, 6.0, ((0, 32), (1, 16)), jnp.float32),
        "initial": noise(key_list[1], (NX, NY, NZ), 1.0, 6.0, ((0, 32), (1, 16)), jnp.float32),
        "absorption": draw_absorption(jax.random.fold_in(key_list[6], 71), 0),
        "beta_x": draw_beta_x(jax.random.fold_in(key_list[6], 71), 0),
        "beta_y": draw_beta_y(jax.random.fold_in(key_list[6], 71), 0),
        "beta_z": draw_beta_z(jax.random.fold_in(key_list[6], 71), 0),
    }


def restrict_cells(field):
    size_x, size_y, size_z = field.shape
    return field.reshape(size_x // 2, 2, size_y // 2, 2, size_z // 2, 2).mean(axis=(1, 3, 5))


def restrict_faces(face_x, face_y, face_z):
    lower_x = face_x[0::2]
    size_x, size_y, size_z = lower_x.shape
    coarse_x = lower_x.reshape(size_x, size_y // 2, 2, size_z // 2, 2).mean(axis=(2, 4))
    lower_y = face_y[:, 0::2]
    size_x, size_y, size_z = lower_y.shape
    coarse_y = lower_y.reshape(size_x // 2, 2, size_y, size_z // 2, 2).mean(axis=(1, 4))
    lower_z = face_z[:, :, 0::2]
    size_x, size_y, size_z = lower_z.shape
    coarse_z = lower_z.reshape(size_x // 2, 2, size_y // 2, 2, size_z).mean(axis=(1, 3))
    return coarse_x, coarse_y, coarse_z


def prolong_cells(field):
    return jnp.repeat(jnp.repeat(jnp.repeat(field, 2, axis=0), 2, axis=1), 2, axis=2)


def level_coeffs(absorb, face_xl, face_yl, face_zl, stencil_scale):
    face_xh = jnp.roll(face_xl, -1, axis=0)
    face_yh = jnp.roll(face_yl, -1, axis=1)
    face_zh = jnp.concatenate([face_zl[:, :, 1:], jnp.zeros_like(face_zl[:, :, :1])], axis=2)
    diagonal = absorb + stencil_scale * (face_xl + face_xh + face_yl + face_yh + face_zl + face_zh)
    return (absorb, face_xl, face_xh, face_yl, face_yh, face_zl, face_zh, diagonal, stencil_scale)


def rolled(field):
    return (jnp.roll(field, 1, axis=0), jnp.roll(field, -1, axis=0),
            jnp.roll(field, 1, axis=1), jnp.roll(field, -1, axis=1))


def apply_operator(field, coeffs, lower_x, upper_x, lower_y, upper_y):
    absorb, face_xl, face_xh, face_yl, face_yh, face_zl, face_zh, diagonal, stencil_scale = coeffs
    zeros_plane = jnp.zeros_like(field[:, :, :1])
    lower_z = jnp.concatenate([zeros_plane, field[:, :, :-1]], axis=2)
    upper_z = jnp.concatenate([field[:, :, 1:], zeros_plane], axis=2)
    flux = (face_xl * (field - lower_x) + face_xh * (field - upper_x)
            + face_yl * (field - lower_y) + face_yh * (field - upper_y)
            + face_zl * (field - lower_z) + face_zh * (field - upper_z))
    return absorb * field + stencil_scale * flux


def chebyshev_weights(sweeps):
    cheb_theta = 1.125
    cheb_delta = 0.875
    cheb_sigma = cheb_theta / cheb_delta
    rho_old = 1.0 / cheb_sigma
    weights = [(0.0, 1.0 / cheb_theta)]
    for sweep in range(1, sweeps):
        rho_new = 1.0 / (2.0 * cheb_sigma - rho_old)
        weights.append((rho_new * rho_old, 2.0 * rho_new / cheb_delta))
        rho_old = rho_new
    return weights


def chebyshev_smooth(iterate, target, coeffs, sweeps, zero_start):
    update = jnp.zeros_like(target)
    for sweep, pair in enumerate(chebyshev_weights(sweeps)):
        if sweep == 0 and zero_start:
            remain = target
        else:
            remain = target - apply_operator(iterate, coeffs, *rolled(iterate))
        update = pair[0] * update + pair[1] * remain / coeffs[7]
        iterate = iterate + update
    return iterate


def reference(source, initial, absorption, beta_x, beta_y, beta_z):
    coeffs_fine = level_coeffs(absorption, beta_x, beta_y, beta_z, 1.0)
    absorb_mid = restrict_cells(absorption)
    face_mid = restrict_faces(beta_x, beta_y, beta_z)
    coeffs_mid = level_coeffs(absorb_mid, face_mid[0], face_mid[1], face_mid[2], 0.25)
    absorb_low = restrict_cells(absorb_mid)
    face_low = restrict_faces(face_mid[0], face_mid[1], face_mid[2])
    coeffs_low = level_coeffs(absorb_low, face_low[0], face_low[1], face_low[2], 0.0625)

    fine_iter = chebyshev_smooth(initial, source, coeffs_fine, SWEEPS, False)
    fine_rest = source - apply_operator(fine_iter, coeffs_fine, *rolled(fine_iter))
    source_mid = restrict_cells(fine_rest)
    mid_iter = chebyshev_smooth(jnp.zeros_like(source_mid), source_mid, coeffs_mid, SWEEPS, True)
    mid_rest = source_mid - apply_operator(mid_iter, coeffs_mid, *rolled(mid_iter))
    source_low = restrict_cells(mid_rest)
    low_iter = chebyshev_smooth(jnp.zeros_like(source_low), source_low, coeffs_low, COARSE_SWEEPS, True)
    mid_iter = mid_iter + prolong_cells(low_iter)
    mid_iter = chebyshev_smooth(mid_iter, source_mid, coeffs_mid, SWEEPS, False)
    fine_iter = fine_iter + prolong_cells(mid_iter)
    return chebyshev_smooth(fine_iter, source, coeffs_fine, SWEEPS, False)
```

```python
import jax
import jax.numpy as jnp
from jax import lax
from jax.experimental import pallas as pl
from jax.experimental.pallas import tpu as pltpu
from jax.sharding import PartitionSpec as P

SWEEPS = 4
COARSE_SWEEPS = 8
LANES = 128
HALF = 64
MESH = pl.DeviceIdType.MESH

NX0, NY0, HX0, HY0, YP0 = 8, 16, 5, 5, 26
NX1, NY1, HX1, HY1, YP1 = 4, 8, 6, 9, 26
NX2, NY2, HX2, HY2, YP2 = 2, 4, 10, 12, 28
ROWS0 = 472
ROWS1 = 416
ROWS2 = 616

DEPTH = 5
NEAR = [(-1, 0), (1, 0), (0, -1), (0, 1), (-1, -1), (-1, 1), (1, -1), (1, 1)]
WIDE = [(-2, 0), (2, 0), (-2, -1), (-2, 1), (2, -1), (2, 1)]
MIDS = NEAR + WIDE


def ball_offsets():
    offsets = []
    for i in range(-5, 6):
        for j in range(-3, 4):
            far_x = 2 * abs(i) - 1 if i else 0
            far_y = 4 * abs(j) - 3 if j else 0
            if (i, j) != (0, 0) and far_x + far_y <= (11 if i and j else 10):
                offsets.append((i, j))
    return offsets


BALL = ball_offsets()


def chebyshev_weights(sweeps):
    cheb_theta = 1.125
    cheb_delta = 0.875
    cheb_sigma = cheb_theta / cheb_delta
    rho_old = 1.0 / cheb_sigma
    weights = [(0.0, 1.0 / cheb_theta)]
    for sweep in range(1, sweeps):
        rho_new = 1.0 / (2.0 * cheb_sigma - rho_old)
        weights.append((rho_new * rho_old, 2.0 * rho_new / cheb_delta))
        rho_old = rho_new
    return weights


def row0(x, y):
    return (x + HX0) * YP0 + y + HY0


def row1(x, y):
    return (x + HX1) * YP1 + y + HY1


def row2(x, y):
    return (x + HX2) * YP2 + y + HY2


def lanes(shape):
    return lax.broadcasted_iota(jnp.int32, shape, len(shape) - 1)


def shift_down(v):
    return jnp.where(lanes(v.shape) < HALF, pltpu.roll(v, HALF + 1, 1), pltpu.roll(v, HALF, 1))


def shift_up(v):
    return jnp.where(lanes(v.shape) < HALF, pltpu.roll(v, HALF, 1), pltpu.roll(v, HALF - 1, 1))


def z_neighbours(values, level):
    if level == 0:
        return (shift_down(values[1]), values[0]), (values[1], shift_up(values[0]))
    if level == 1:
        return (shift_down(values[0]),), (shift_up(values[0]),)
    return (pltpu.roll(values[0], 1, 1),), (pltpu.roll(values[0], LANES - 1, 1),)


def z_ends(shape, level, half):
    at = lanes(shape)
    if level == 0:
        return (at == 0) if half == 0 else None, (at == LANES - 1) if half == 1 else None
    if level == 1:
        return at == 0, at == LANES - 1
    return (at % HALF) == 0, (at % HALF) == HALF - 1


def plane_loop(first, count, body):
    def pair(i, carry):
        body(first + 2 * i)
        body(first + 2 * i + 1)
        return carry

    lax.fori_loop(0, count // 2, pair, 0)


class Level:
    def __init__(self, number, halves, row, pitch, raw, coef, diag, rhs, update):
        self.number, self.halves, self.row, self.pitch = number, halves, row, pitch
        self.raw, self.coef, self.diag, self.rhs, self.update = raw, coef, diag, rhs, update
        self.scale = 0.25**number

    def faces(self, at, rows):
        n, raw = self.halves, self.raw
        take = lambda k, e, shift=0: raw[k * n + e, pl.ds(at + shift, rows), :]
        low_z = [take(3, e) for e in range(n)]
        _, high_z = z_neighbours(low_z, self.number)
        out = []
        for e in range(n):
            _, top = z_ends((rows, LANES), self.number, e)
            upper = high_z[e] if top is None else jnp.where(top, 0.0, high_z[e])
            faces = [take(1, e), take(1, e, self.pitch), take(2, e), take(2, e, 1), low_z[e], upper]
            total = (faces[0] + faces[1]) + (faces[2] + faces[3]) + (faces[4] + faces[5])
            out.append((faces, take(0, e) + self.scale * total))
        return out

    def own_diagonal(self, x, y, rows):
        return [d for _, d in self.faces(self.row(x, y), rows)]

    def build(self, first_x, count, first_y, rows, source=None):
        n = self.halves

        def body(x):
            at = self.row(x, first_y)
            for e, (faces, diagonal) in enumerate(self.faces(at, rows)):
                inverse = 1.0 / diagonal
                low, _ = z_ends((rows, LANES), self.number, e)
                if low is not None:
                    faces[4] = jnp.where(low, 0.0, faces[4])
                scaled = self.scale * inverse
                for c in range(6):
                    self.coef[c * n + e, pl.ds(at, rows), :] = faces[c] * scaled
                self.diag[e, pl.ds(at, rows), :] = diagonal
                if source is not None:
                    ref, base = source
                    self.rhs[e, pl.ds(at, rows), :] = ref[base + e, pl.ds(at, rows), :] * inverse

        plane_loop(first_x, count, body)

    def residual(self, src, at, rows):
        n = self.halves
        ref, base = src
        take = lambda e, shift=0: ref[base + e, pl.ds(at + shift, rows), :]
        centre = [take(e) for e in range(n)]
        below, above = z_neighbours(centre, self.number)
        out = []
        for e in range(n):
            c = lambda k: self.coef[k * n + e, pl.ds(at, rows), :]
            t = self.rhs[e, pl.ds(at, rows), :] - centre[e]
            t_x = c(0) * take(e, -self.pitch) + c(1) * take(e, self.pitch)
            t_y = c(2) * take(e, -1) + c(3) * take(e, 1)
            t_z = c(4) * below[e] + c(5) * above[e]
            out.append(t + (t_x + t_y) + t_z)
        return out, centre

    def sweep(self, pair, src, dst, first_x, count, first_y, rows, last=False, emit=None):
        def body(x):
            at = self.row(x, first_y)
            steps, centre = self.residual(src, at, rows)
            news = []
            for e in range(self.halves):
                new = pair[1] * steps[e]
                if pair[0] != 0.0:
                    new = pair[0] * self.update[e, pl.ds(at, rows), :] + new
                if not last:
                    self.update[e, pl.ds(at, rows), :] = new
                news.append(centre[e] + new)
            if emit is not None:
                emit(x, news)
            else:
                ref, base = dst
                for e in range(self.halves):
                    ref[base + e, pl.ds(at, rows), :] = news[e]

        plane_loop(first_x, count, body)

    def first_from_zero(self, pair, dst, first_x, count, first_y, rows):
        def body(x):
            at = self.row(x, first_y)
            for e in range(self.halves):
                new = pair[1] * self.rhs[e, pl.ds(at, rows), :]
                self.update[e, pl.ds(at, rows), :] = new
                ref, base = dst
                ref[base + e, pl.ds(at, rows), :] = new

        plane_loop(first_x, count, body)


def corner_pieces(sx, sy, depth):
    pieces = []
    for dx in range(1, depth):
        rows = depth - dx
        pieces.append((NX0 - dx if sx > 0 else dx - 1, NY0 - rows if sy > 0 else 0, rows))
    return pieces


def side_plane(sx, dx):
    return NX0 - dx if sx > 0 else dx - 1


def side_row(sy, dy):
    return NY0 - dy if sy > 0 else dy - 1


def corner_rows(depth):
    return depth * (depth - 1) // 2


def kernel(counts, *refs):
    inputs, out_hbm = refs[:6], refs[6]
    (nat, fine, fine_a, fine_b, coef0, diag0, rhs0, upd0, rest0,
     raw1, coef1, diag1, rhs1, upd1, it1_a, it1_b, rest1,
     raw2, coef2, diag2, rhs2, upd2, it2_a, it2_b,
     sxa, sya, sca, rxa, rya, rca, sxb, syb, scb, rxb, ryb, rcb,
     smc, rmc, rmcw, sg1, rg1, rg1w, sx1, rx1, rx1w,
     s2c, r2c, sg2, rg2, sxu, syu, scu, rxu, ryu, rcu, out_v,
     in_sem, out_sem, near_s, near_r, mids_s, mids_r, ball_s, ball_r) = refs[7:]
    count_x, count_y = counts
    me_x, me_y = lax.axis_index("gx"), lax.axis_index("gy")

    def device(offset):
        return (lax.rem(me_x + offset[0] + count_x, count_x), lax.rem(me_y + offset[1] + count_y, count_y))

    loads = [pltpu.make_async_copy(inputs[k], nat.at[k], in_sem.at[k]) for k in range(6)]
    for load in loads:
        load.start()
    barrier = pltpu.get_barrier_semaphore()
    for offset in BALL:
        pl.semaphore_signal(barrier, inc=1, device_id=device(offset), device_id_type=MESH)

    started = []

    def send(src, dst, s_sem, r_sem, offset):
        copy = pltpu.make_async_remote_copy(
            src_ref=src, dst_ref=dst, send_sem=s_sem, recv_sem=r_sem, device_id=device(offset), device_id_type=MESH
        )
        copy.start()
        started.append(copy)
        return copy

    level0 = Level(0, 2, row0, YP0, fine, coef0, diag0, rhs0, upd0)
    level1 = Level(1, 1, row1, YP1, raw1, coef1, diag1, rhs1, upd1)
    level2 = Level(2, 1, row2, YP2, raw2, coef2, diag2, rhs2, upd2)

    at = lanes((NY0, LANES))
    cell = 4 * (at % HALF) + 2 * (at // HALF)
    from_first = (at % HALF) < HALF // 2
    picks = [(cell + e) % LANES for e in range(2)]

    def permute(k):
        def body(x, carry):
            first = nat[k, x, :, 0:LANES]
            second = nat[k, x, :, LANES : 2 * LANES]
            for e in range(2):
                low = jnp.take_along_axis(first, picks[e], axis=1, mode="promise_in_bounds")
                high = jnp.take_along_axis(second, picks[e], axis=1, mode="promise_in_bounds")
                fine[2 * k + e, pl.ds(row0(x, 0), NY0), :] = jnp.where(from_first, low, high)
            return carry

        lax.fori_loop(0, NX0, body, 0)

    def pack(field, first, count, xs, ys, cs, planes, depth):
        def body(i, carry):
            k = first + i
            for side, (sx, _) in enumerate(NEAR[:2]):
                for dx in range(1, planes + 1):
                    dst = pl.multiple_of((i * planes + dx - 1) * NY0, NY0)
                    xs[side, pl.ds(dst, NY0), :] = field[k, pl.ds(row0(side_plane(sx, dx), 0), NY0), :]
            for side, (_, sy) in enumerate(NEAR[2:4]):
                for dy in range(1, depth + 1):
                    dst = pl.multiple_of((i * depth + dy - 1) * NX0, NX0)
                    ys[side, pl.ds(dst, NX0), :] = field[k, pl.ds(row0(0, side_row(sy, dy)), NX0, stride=YP0), :]
            for side, (sx, sy) in enumerate(NEAR[4:8]):
                dst = i * corner_rows(depth)
                for x, y, rows in corner_pieces(sx, sy, depth):
                    cs[side, pl.ds(dst, rows), :] = field[k, pl.ds(row0(x, y), rows), :]
                    dst = dst + rows
            return carry

        lax.fori_loop(0, count, body, 0)

    def unpack(field, first, count, xs, ys, cs, planes, depth):
        def body(i, carry):
            k = first + i
            for side, (sx, _) in enumerate(NEAR[:2]):
                for dx in range(1, planes + 1):
                    src = pl.multiple_of((i * planes + dx - 1) * NY0, NY0)
                    field[k, pl.ds(row0(side_plane(sx, dx) - sx * NX0, 0), NY0), :] = xs[side, pl.ds(src, NY0), :]
            for side, (_, sy) in enumerate(NEAR[2:4]):
                for dy in range(1, depth + 1):
                    src = pl.multiple_of((i * depth + dy - 1) * NX0, NX0)
                    to = pl.ds(row0(0, side_row(sy, dy) - sy * NY0), NX0, stride=YP0)
                    field[k, to, :] = ys[side, pl.ds(src, NX0), :]
            for side, (sx, sy) in enumerate(NEAR[4:8]):
                src = i * corner_rows(depth)
                for x, y, rows in corner_pieces(sx, sy, depth):
                    to = pl.ds(row0(x - sx * NX0, y - sy * NY0), rows)
                    field[k, to, :] = cs[side, pl.ds(src, rows), :]
                    src = src + rows
            return carry

        lax.fori_loop(0, count, body, 0)

    def extra_out(field, k, xs, base, sides):
        for side in sides:
            sx = NEAR[side][0]
            for e in range(2):
                xs[side, pl.ds(base + e * NY0, NY0), :] = field[k + e, pl.ds(row0(side_plane(sx, DEPTH), 0), NY0), :]

    def extra_in(field, k, xs, base, sides):
        for side in sides:
            sx = NEAR[side][0]
            for e in range(2):
                to = pl.ds(row0(side_plane(sx, DEPTH) - sx * NX0, 0), NY0)
                field[k + e, to, :] = xs[side, pl.ds(base + e * NY0, NY0), :]

    def near_sends(group, xs, ys, cs, rx, ry, rc, x_rows):
        waits = []
        for n, offset in enumerate(NEAR):
            s_sem, r_sem = near_s.at[group, n], near_r.at[group, n]
            if n < 2:
                cut = pl.ds(0, x_rows[n])
                waits.append(send(xs.at[n, cut], rx.at[n, cut], s_sem, r_sem, offset))
            elif n < 4:
                waits.append(send(ys.at[n - 2], ry.at[n - 2], s_sem, r_sem, offset))
            else:
                waits.append(send(cs.at[n - 4], rc.at[n - 4], s_sem, r_sem, offset))
        return waits

    for k in range(4):
        loads[k].wait()
        permute(k)
    pack(fine, 0, 8, sxa, sya, sca, 4, DEPTH)
    extra_out(fine, 2, sxa, 512, (0,))
    pl.semaphore_wait(barrier, len(BALL))
    waits_a = near_sends(0, sxa, sya, sca, rxa, rya, rca, (544, 512))
    for k in (4, 5):
        loads[k].wait()
        permute(k)
    pack(fine, 8, 4, sxb, syb, scb, 4, DEPTH)
    extra_out(fine, 10, sxb, 256, (0, 1))
    waits_b = near_sends(1, sxb, syb, scb, rxb, ryb, rcb, (288, 288))

    def children(k, e, x, y_step):
        return fine[2 * k + e, pl.ds(row0(x, y_step), NY1, stride=2), :]

    def coarsen1(big, carry):
        to = pl.ds(row1(big, 0), NY1)
        x = 2 * big
        absorb = sum(children(0, e, x + p, q) for e in range(2) for p in range(2) for q in range(2)) * 0.125
        face_x = sum(children(1, e, x, q) for e in range(2) for q in range(2)) * 0.25
        face_y = sum(children(2, e, x + p, 0) for e in range(2) for p in range(2)) * 0.25
        face_z = sum(children(3, 0, x + p, q) for p in range(2) for q in range(2)) * 0.25
        for k, value in enumerate((absorb, face_x, face_y, face_z)):
            raw1[k, to, :] = value
            smc[big, pl.ds(k * NY1, NY1), :] = value
        return carry

    lax.fori_loop(0, NX1, coarsen1, 0)

    def mid_sends(group, src, near, wide):
        waits = []
        for n, offset in enumerate(MIDS):
            s_sem, r_sem = mids_s.at[group, n], mids_r.at[group, n]
            if n < 8:
                waits.append(send(src, near.at[n], s_sem, r_sem, offset))
            else:
                cut = pl.ds(2 if offset[0] > 0 else 0, 2)
                waits.append(send(src.at[cut], wide.at[n - 8], s_sem, r_sem, offset))
        return waits

    waits_mc = mid_sends(0, smc, rmc, rmcw)

    def mid_unpack(near, wide, store):
        for n, (sx, sy) in enumerate(MIDS):
            planes = range(4) if n < 8 else (range(2, 4) if sx > 0 else range(2))
            for i, x in enumerate(planes):
                value = near[n, i] if n < 8 else wide[n - 8, i]
                store(row1(x - sx * NX1, -sy * NY1), value)

    def both(v):
        return v + pltpu.roll(v, HALF, 1)

    for big in range(NX2):
        grand = lambda k, x, q: raw1[k, pl.ds(row1(x, q), NY2, stride=2), :]
        x = 2 * big
        absorb = both(sum(grand(0, x + p, q) for p in range(2) for q in range(2))) * 0.125
        face_x = both(sum(grand(1, x, q) for q in range(2))) * 0.25
        face_y = both(sum(grand(2, x + p, 0) for p in range(2))) * 0.25
        face_z = sum(grand(3, x + p, q) for p in range(2) for q in range(2)) * 0.25
        low = lanes((NY2, LANES)) < HALF
        face_z = jnp.where(low, face_z, pltpu.roll(face_z, HALF, 1))
        for k, value in enumerate((absorb, face_x, face_y, face_z)):
            raw2[k, pl.ds(row2(big, 0), NY2), :] = value
        s2c[pl.ds(big * NY2, NY2), :] = jnp.where(low, absorb, face_x)
        s2c[pl.ds(8 + big * NY2, NY2), :] = jnp.where(low, face_y, face_z)

    for wait in waits_a:
        wait.wait_recv()
    unpack(fine, 0, 8, rxa, rya, rca, 4, DEPTH)
    extra_in(fine, 2, rxa, 512, (0,))
    for wait in waits_b:
        wait.wait_recv()
    unpack(fine, 8, 4, rxb, ryb, rcb, 4, DEPTH)
    extra_in(fine, 10, rxb, 256, (0, 1))
    level0.build(-4, 16, -4, 24, (fine, 8))
    weights = chebyshev_weights(SWEEPS)
    level0.sweep(weights[0], (fine, 10), (fine_a, 0), -4, 16, -4, 24)
    level0.sweep(weights[1], (fine_a, 0), (fine_b, 0), -3, 14, -4, 24)
    level0.sweep(weights[2], (fine_b, 0), (fine_a, 0), -2, 12, -4, 24)
    level0.sweep(weights[3], (fine_a, 0), (fine_b, 0), -1, 10, -4, 24, last=True)

    def rest_fine(x):
        at_row = row0(x, 0)
        steps, _ = level0.residual((fine_b, 0), at_row, NY0)
        for e in range(2):
            rest0[e, pl.ds(x * NY0, NY0), :] = steps[e] * diag0[e, pl.ds(at_row, NY0), :]

    plane_loop(0, NX0, rest_fine)

    face_x = sum(children(1, e, NX0, q) for e in range(2) for q in range(2)) * 0.25
    raw1[1, pl.ds(row1(NX1, 0), NY1), :] = face_x
    for wait in waits_mc:
        wait.wait_recv()

    def store_raw(to, value):
        for k in range(4):
            raw1[k, pl.ds(to, NY1), :] = value[k * NY1 : (k + 1) * NY1]

    mid_unpack(rmc, rmcw, store_raw)
    level1.build(-5, 14, -8, 24)
    for big in range(NX1):
        total = sum(
            rest0[e, pl.ds((2 * big + p) * NY0 + q, NY1, stride=2), :]
            for e in range(2) for p in range(2) for q in range(2)
        )
        value = total * 0.125 / diag1[0, pl.ds(row1(big, 0), NY1), :]
        rhs1[0, pl.ds(row1(big, 0), NY1), :] = value
        sg1[big] = value

    waits_g1 = mid_sends(1, sg1, rg1, rg1w)
    waits_2c = [send(s2c, r2c.at[n], ball_s.at[0, n], ball_r.at[0, n], o) for n, o in enumerate(BALL)]

    x = NX1
    grand = lambda k, x, y: raw1[k, pl.ds(row1(x, y), NY2, stride=2), :]
    raw2[1, pl.ds(row2(NX2, 0), NY2), :] = both(grand(1, x, 0) + grand(1, x, 1)) * 0.25
    for big in range(NX2):
        above = both(sum(grand(2, 2 * big + p, NY1) for p in range(2))) * 0.25
        raw2[2, pl.ds(row2(big, NY2), 1), :] = above[0:1]
    diag_own2 = [level2.own_diagonal(big, 0, NY2)[0] for big in range(NX2)]

    def store_rhs1(to, value):
        rhs1[0, pl.ds(to, NY1), :] = value

    for wait in waits_g1:
        wait.wait_recv()
    mid_unpack(rg1, rg1w, store_rhs1)
    level1.first_from_zero(weights[0], (it1_a, 0), -4, 12, -4, 16)
    level1.sweep(weights[1], (it1_a, 0), (it1_b, 0), -3, 10, -4, 16)
    level1.sweep(weights[2], (it1_b, 0), (it1_a, 0), -2, 8, -4, 16)
    level1.sweep(weights[3], (it1_a, 0), (it1_b, 0), -1, 6, -4, 16, last=True)

    def rest_mid(x):
        at_row = row1(x, 0)
        steps, centre = level1.residual((it1_b, 0), at_row, NY1)
        rest1[pl.ds(x * NY1, NY1), :] = steps[0] * diag1[0, pl.ds(at_row, NY1), :]
        sx1[x] = centre[0]

    plane_loop(0, NX1, rest_mid)
    for big in range(NX2):
        total = sum(rest1[pl.ds((2 * big + p) * NY1 + q, NY2, stride=2), :] for p in range(2) for q in range(2))
        value = both(total) * 0.125 / diag_own2[big]
        rhs2[0, pl.ds(row2(big, 0), NY2), :] = value
        sg2[pl.ds(big * NY2, NY2), :] = value

    waits_g2 = [send(sg2, rg2.at[n], ball_s.at[1, n], ball_r.at[1, n], o) for n, o in enumerate(BALL)]
    waits_x1 = mid_sends(2, sx1, rx1, rx1w)
    pack(fine_b, 0, 2, sxu, syu, scu, 4, 4)
    waits_x0 = near_sends(2, sxu, syu, scu, rxu, ryu, rcu, (128, 128))

    for wait in waits_2c:
        wait.wait_recv()
    low8 = lanes((8, LANES)) < HALF
    for n, (i, j) in enumerate(BALL):
        for part in range(2):
            value = r2c[n, pl.ds(8 * part, 8), :]
            other = pltpu.roll(value, HALF, 1)
            for k, full in enumerate((jnp.where(low8, value, other), jnp.where(low8, other, value))):
                for p in range(NX2):
                    to = pl.ds(row2(p - 2 * i, -4 * j), NY2)
                    raw2[2 * part + k, to, :] = full[p * NY2 : (p + 1) * NY2]
    level2.build(-9, 20, -10, 24)
    for wait in waits_g2:
        wait.wait_recv()
    for n, (i, j) in enumerate(BALL):
        for p in range(NX2):
            rhs2[0, pl.ds(row2(p - 2 * i, -4 * j), NY2), :] = rg2[n, pl.ds(p * NY2, NY2), :]
    coarse = chebyshev_weights(COARSE_SWEEPS)
    level2.first_from_zero(coarse[0], (it2_a, 0), -10, 22, -10, 24)
    src, dst = it2_a, it2_b
    for sweep in range(1, COARSE_SWEEPS):
        reach = COARSE_SWEEPS - 1 - sweep
        first_y, rows = (-10, 24) if reach > 3 else (-6, 16)
        level2.sweep(coarse[sweep], (src, 0), (dst, 0), -3 - reach, 8 + 2 * reach, first_y, rows, last=reach == 0)
        src, dst = dst, src

    def store_it1(to, value):
        it1_b[0, pl.ds(to, NY1), :] = value

    for wait in waits_x1:
        wait.wait_recv()
    mid_unpack(rx1, rx1w, store_it1)

    def lift1(big):
        for y in (-3, -1):
            value = src[0, pl.ds(row2(big, y), 8), :]
            for p in range(2):
                for q in range(2):
                    to = pl.ds(row1(2 * big + p, 2 * y + q), 8, stride=2)
                    it1_a[0, to, :] = it1_b[0, to, :] + value

    plane_loop(-3, 8, lift1)
    level1.sweep(weights[0], (it1_a, 0), (it1_b, 0), -5, 14, -8, 24)
    level1.sweep(weights[1], (it1_b, 0), (it1_a, 0), -4, 12, -8, 24)
    level1.sweep(weights[2], (it1_a, 0), (it1_b, 0), -3, 10, -4, 16)
    level1.sweep(weights[3], (it1_b, 0), (it1_a, 0), -2, 8, -4, 16, last=True)

    for wait in waits_x0:
        wait.wait_recv()
    unpack(fine_b, 0, 2, rxu, ryu, rcu, 4, 4)

    def lift0(big):
        for y in (-2, 2):
            value = it1_a[0, pl.ds(row1(big, y), 8), :]
            for e in range(2):
                for p in range(2):
                    for q in range(2):
                        to = pl.ds(row0(2 * big + p, 2 * y + q), 8, stride=2)
                        fine_a[e, to, :] = fine_b[e, to, :] + value

    plane_loop(-2, 8, lift0)
    level0.sweep(weights[0], (fine_a, 0), (fine_b, 0), -3, 14, -4, 24)
    level0.sweep(weights[1], (fine_b, 0), (fine_a, 0), -2, 12, -4, 24)
    level0.sweep(weights[2], (fine_a, 0), (fine_b, 0), -1, 10, -4, 24)
    back = HALF * ((at // 2) % 2) + at // 4
    even = (at % 2) == 0

    def emit(x, news):
        for half in range(2):
            pick = back + 32 * half
            lower = jnp.take_along_axis(news[0], pick, axis=1, mode="promise_in_bounds")
            upper = jnp.take_along_axis(news[1], pick, axis=1, mode="promise_in_bounds")
            out_v[x, :, half * LANES : (half + 1) * LANES] = jnp.where(even, lower, upper)

    level0.sweep(weights[3], (fine_b, 0), None, 0, 8, 0, NY0, last=True, emit=emit)
    store = pltpu.make_async_copy(out_v, out_hbm, out_sem.at[0])
    store.start()
    for copy in started:
        copy.wait_send()
    store.wait()


def solution(mesh):
    counts = (mesh.shape["gx"], mesh.shape["gy"])

    def local(source, initial, absorption, beta_x, beta_y, beta_z):
        f32 = jnp.float32
        v = lambda *shape: pltpu.VMEM(shape, f32)
        scratch = [
            v(6, NX0, NY0, 256), v(12, ROWS0, LANES), v(2, ROWS0, LANES), v(2, ROWS0, LANES),
            v(12, ROWS0, LANES), v(2, ROWS0, LANES), v(2, ROWS0, LANES), v(2, ROWS0, LANES), v(2, 128, LANES),
            v(4, ROWS1, LANES), v(6, ROWS1, LANES), v(1, ROWS1, LANES), v(1, ROWS1, LANES), v(1, ROWS1, LANES),
            v(1, ROWS1, LANES), v(1, ROWS1, LANES), v(32, LANES),
            v(4, ROWS2, LANES), v(6, ROWS2, LANES), v(1, ROWS2, LANES), v(1, ROWS2, LANES), v(1, ROWS2, LANES),
            v(1, ROWS2, LANES), v(1, ROWS2, LANES),
            v(2, 544, LANES), v(2, 320, LANES), v(4, 80, LANES),
            v(2, 544, LANES), v(2, 320, LANES), v(4, 80, LANES),
            v(2, 288, LANES), v(2, 160, LANES), v(4, 40, LANES),
            v(2, 288, LANES), v(2, 160, LANES), v(4, 40, LANES),
            v(4, 32, LANES), v(8, 4, 32, LANES), v(6, 2, 32, LANES),
            v(4, 8, LANES), v(8, 4, 8, LANES), v(6, 2, 8, LANES),
            v(4, 8, LANES), v(8, 4, 8, LANES), v(6, 2, 8, LANES),
            v(16, LANES), v(len(BALL), 16, LANES), v(8, LANES), v(len(BALL), 8, LANES),
            v(2, 128, LANES), v(2, 64, LANES), v(4, 16, LANES),
            v(2, 128, LANES), v(2, 64, LANES), v(4, 16, LANES),
            v(NX0, NY0, 256),
            pltpu.SemaphoreType.DMA((6,)), pltpu.SemaphoreType.DMA((1,)),
            pltpu.SemaphoreType.DMA((3, 8)), pltpu.SemaphoreType.DMA((3, 8)),
            pltpu.SemaphoreType.DMA((3, len(MIDS))), pltpu.SemaphoreType.DMA((3, len(MIDS))),
            pltpu.SemaphoreType.DMA((2, len(BALL))), pltpu.SemaphoreType.DMA((2, len(BALL))),
        ]
        call = pl.pallas_call(
            lambda *refs: kernel(counts, *refs),
            out_shape=jax.ShapeDtypeStruct((NX0, NY0, 256), f32),
            in_specs=[pl.BlockSpec(memory_space=pl.ANY)] * 6,
            out_specs=pl.BlockSpec(memory_space=pl.ANY),
            scratch_shapes=scratch,
            compiler_params=pltpu.CompilerParams(
                collective_id=0, has_side_effects=True, vmem_limit_bytes=56 * 2**20
            ),
            name="vcycle",
        )
        return call(absorption, beta_x, beta_y, beta_z, source, initial)

    return jax.shard_map(
        local,
        mesh=mesh,
        in_specs=(P("gx", "gy", None),) * 6,
        out_specs=P("gx", "gy", None),
        check_vma=False,
    )
```

```python
import jax
import jax.numpy as jnp
from jax import lax
from jax.experimental import pallas as pl
from jax.experimental.pallas import tpu as pltpu
from jax.sharding import PartitionSpec as P

SWEEPS = 4
COARSE_SWEEPS = 8
LANES = 128
HALF = 64
GROUP = 4
MESH = pl.DeviceIdType.MESH

NX0, NY0, HX0, HY0, YP0 = 8, 16, 5, 5, 26
NX1, NY1, HX1, HY1, YP1 = 4, 8, 6, 9, 26
NX2, NY2, HX2, HY2, YP2 = 2, 4, 10, 12, 28
ROWS0 = 472
ROWS1 = 416
ROWS2 = 616

DEPTH = 5
NEAR = [(-1, 0), (1, 0), (0, -1), (0, 1), (-1, -1), (-1, 1), (1, -1), (1, 1)]
WIDE = [(-2, 0), (2, 0), (-2, -1), (-2, 1), (2, -1), (2, 1)]
MIDS = NEAR + WIDE


def ball_offsets():
    offsets = []
    for i in range(-5, 6):
        for j in range(-3, 4):
            far_x = 2 * abs(i) - 1 if i else 0
            far_y = 4 * abs(j) - 3 if j else 0
            if (i, j) != (0, 0) and far_x + far_y <= (11 if i and j else 10):
                offsets.append((i, j))
    return offsets


BALL = ball_offsets()


def chebyshev_weights(sweeps):
    cheb_theta = 1.125
    cheb_delta = 0.875
    cheb_sigma = cheb_theta / cheb_delta
    rho_old = 1.0 / cheb_sigma
    weights = [(0.0, 1.0 / cheb_theta)]
    for sweep in range(1, sweeps):
        rho_new = 1.0 / (2.0 * cheb_sigma - rho_old)
        weights.append((rho_new * rho_old, 2.0 * rho_new / cheb_delta))
        rho_old = rho_new
    return weights


def row0(x, y):
    return (x + HX0) * YP0 + y + HY0


def row1(x, y):
    return (x + HX1) * YP1 + y + HY1


def row2(x, y):
    return (x + HX2) * YP2 + y + HY2


def lanes(shape):
    return lax.broadcasted_iota(jnp.int32, shape, len(shape) - 1)


def shift_down(v):
    return jnp.where(lanes(v.shape) < HALF, pltpu.roll(v, HALF + 1, 1), pltpu.roll(v, HALF, 1))


def shift_up(v):
    return jnp.where(lanes(v.shape) < HALF, pltpu.roll(v, HALF, 1), pltpu.roll(v, HALF - 1, 1))


def z_neighbours(values, level):
    if level == 0:
        return (shift_down(values[1]), values[0]), (values[1], shift_up(values[0]))
    if level == 1:
        return (shift_down(values[0]),), (shift_up(values[0]),)
    return (pltpu.roll(values[0], 1, 1),), (pltpu.roll(values[0], LANES - 1, 1),)


def z_ends(shape, level, half):
    at = lanes(shape)
    if level == 0:
        return (at == 0) if half == 0 else None, (at == LANES - 1) if half == 1 else None
    if level == 1:
        return at == 0, at == LANES - 1
    return (at % HALF) == 0, (at % HALF) == HALF - 1


def plane_loop(first, count, body, group=GROUP):
    def several(start, n):
        stores = []
        for i in range(n):
            stores += body(start + i)
        for ref, index, value in stores:
            ref[index] = value

    def step(i, carry):
        several(first + group * i, group)
        return carry

    if count // group > 1:
        lax.fori_loop(0, count // group, step, 0)
        done = count // group * group
    else:
        done = 0
    if done < count:
        several(first + done, count - done)


class Level:
    def __init__(self, number, halves, row, pitch, raw, coef, diag, rhs, update):
        self.number, self.halves, self.row, self.pitch = number, halves, row, pitch
        self.raw, self.coef, self.diag, self.rhs, self.update = raw, coef, diag, rhs, update
        self.scale = 0.25**number

    def faces(self, at, rows):
        n, raw = self.halves, self.raw
        take = lambda k, e, shift=0: raw[k * n + e, pl.ds(at + shift, rows), :]
        low_z = [take(3, e) for e in range(n)]
        _, high_z = z_neighbours(low_z, self.number)
        out = []
        for e in range(n):
            _, top = z_ends((rows, LANES), self.number, e)
            upper = high_z[e] if top is None else jnp.where(top, 0.0, high_z[e])
            faces = [take(1, e), take(1, e, self.pitch), take(2, e), take(2, e, 1), low_z[e], upper]
            total = (faces[0] + faces[1]) + (faces[2] + faces[3]) + (faces[4] + faces[5])
            out.append((faces, take(0, e) + self.scale * total))
        return out

    def own_diagonal(self, x, y, rows):
        return [d for _, d in self.faces(self.row(x, y), rows)]

    def build(self, first_x, count, first_y, rows, source=None):
        n = self.halves

        def body(x):
            at = self.row(x, first_y)
            stores = []
            for e, (faces, diagonal) in enumerate(self.faces(at, rows)):
                inverse = 1.0 / diagonal
                low, _ = z_ends((rows, LANES), self.number, e)
                if low is not None:
                    faces[4] = jnp.where(low, 0.0, faces[4])
                scaled = self.scale * inverse
                for c in range(6):
                    stores.append((self.coef, (c * n + e, pl.ds(at, rows)), faces[c] * scaled))
                stores.append((self.diag, (e, pl.ds(at, rows)), diagonal))
                if source is not None:
                    ref, base = source
                    stores.append((self.rhs, (e, pl.ds(at, rows)), ref[base + e, pl.ds(at, rows), :] * inverse))
            return stores

        plane_loop(first_x, count, body)

    def residual(self, src, at, rows):
        n = self.halves
        ref, base = src
        take = lambda e, shift=0: ref[base + e, pl.ds(at + shift, rows), :]
        centre = [take(e) for e in range(n)]
        below, above = z_neighbours(centre, self.number)
        out = []
        for e in range(n):
            c = lambda k: self.coef[k * n + e, pl.ds(at, rows), :]
            t = self.rhs[e, pl.ds(at, rows), :] - centre[e]
            t_x = c(0) * take(e, -self.pitch) + c(1) * take(e, self.pitch)
            t_y = c(2) * take(e, -1) + c(3) * take(e, 1)
            t_z = c(4) * below[e] + c(5) * above[e]
            out.append(t + (t_x + t_y) + t_z)
        return out, centre

    def sweep(self, pair, src, dst, first_x, count, first_y, rows, last=False, emit=None):
        def body(x):
            at = self.row(x, first_y)
            steps, centre = self.residual(src, at, rows)
            news, stores = [], []
            for e in range(self.halves):
                new = pair[1] * steps[e]
                if pair[0] != 0.0:
                    new = pair[0] * self.update[e, pl.ds(at, rows), :] + new
                if not last:
                    stores.append((self.update, (e, pl.ds(at, rows)), new))
                news.append(centre[e] + new)
            if emit is not None:
                return emit(x, news)
            ref, base = dst
            return stores + [(ref, (base + e, pl.ds(at, rows)), news[e]) for e in range(self.halves)]

        plane_loop(first_x, count, body)

    def first_from_zero(self, pair, dst, first_x, count, first_y, rows):
        def body(x):
            at = self.row(x, first_y)
            ref, base = dst
            stores = []
            for e in range(self.halves):
                new = pair[1] * self.rhs[e, pl.ds(at, rows), :]
                stores.append((self.update, (e, pl.ds(at, rows)), new))
                stores.append((ref, (base + e, pl.ds(at, rows)), new))
            return stores

        plane_loop(first_x, count, body)


def corner_pieces(sx, sy, depth):
    pieces = []
    for dx in range(1, depth):
        rows = depth - dx
        pieces.append((NX0 - dx if sx > 0 else dx - 1, NY0 - rows if sy > 0 else 0, rows))
    return pieces


def side_plane(sx, dx):
    return NX0 - dx if sx > 0 else dx - 1


def side_row(sy, dy):
    return NY0 - dy if sy > 0 else dy - 1


def near_plan(fields, planes, depth, extra=(0, 0)):
    sizes = [fields * planes * NY0 + extra[0], fields * planes * NY0 + extra[1]]
    sizes += [fields * depth * NX0] * 2 + [-(-fields * corner_rows(depth) // 8) * 8] * 4
    starts = [sum(sizes[:n]) for n in range(8)]
    return list(zip(starts, sizes)), sum(sizes)


def corner_rows(depth):
    return depth * (depth - 1) // 2


RAW_A, RAW_B, MID_COEF, LOW_COEF, MID_RHS, LOW_RHS, MID_ITER, FINE_ITER = range(8)
PLAN_A, SIZE_A = near_plan(8, 4, DEPTH, (32, 0))
PLAN_B, SIZE_B = near_plan(4, 4, DEPTH, (32, 32))
PLAN_U, SIZE_U = near_plan(2, 4, 4)


def kernel(counts, *refs):
    inputs, out_hbm = refs[:6], refs[6]
    (nat, fine, fine_a, fine_b, coef0, diag0, rhs0, upd0, rest0,
     raw1, coef1, diag1, rhs1, upd1, it1_a, it1_b, rest1,
     raw2, coef2, diag2, rhs2, upd2, it2_a, it2_b,
     sra, rra, srb, rrb, smc, rmc, sg1, rg1, sx1, rx1, s2c, r2c, sg2, rg2, siu, riu, out_v,
     in_sem, out_sem, sent, got) = refs[7:]
    count_x, count_y = counts
    me_x, me_y = lax.axis_index("gx"), lax.axis_index("gy")

    def device(offset):
        return (lax.rem(me_x + offset[0] + count_x, count_x), lax.rem(me_y + offset[1] + count_y, count_y))

    loads = [pltpu.make_async_copy(inputs[k], nat.at[k], in_sem.at[k]) for k in range(6)]
    for load in loads:
        load.start()
    barrier = pltpu.get_barrier_semaphore()
    for offset in NEAR + [o for o in BALL if o not in NEAR]:
        pl.semaphore_signal(barrier, inc=1, device_id=device(offset), device_id_type=MESH)

    def send(group, src, dst, offset):
        pltpu.make_async_remote_copy(
            src_ref=src, dst_ref=dst, send_sem=sent.at[group], recv_sem=got.at[group],
            device_id=device(offset), device_id_type=MESH,
        ).start()

    def arrived(group, landing):
        pltpu.make_async_copy(landing, landing, got.at[group]).wait()

    def departed(group, landing):
        pltpu.make_async_copy(landing, landing, sent.at[group]).wait()

    level0 = Level(0, 2, row0, YP0, fine, coef0, diag0, rhs0, upd0)
    level1 = Level(1, 1, row1, YP1, raw1, coef1, diag1, rhs1, upd1)
    level2 = Level(2, 1, row2, YP2, raw2, coef2, diag2, rhs2, upd2)

    at = lanes((NY0, LANES))
    cell = 4 * (at % HALF) + 2 * (at // HALF)
    from_first = (at % HALF) < HALF // 2
    picks = [(cell + e) % LANES for e in range(2)]

    def permute(k):
        def body(x):
            first = nat[k, x, :, 0:LANES]
            second = nat[k, x, :, LANES : 2 * LANES]
            stores = []
            for e in range(2):
                low = jnp.take_along_axis(first, picks[e], axis=1, mode="promise_in_bounds")
                high = jnp.take_along_axis(second, picks[e], axis=1, mode="promise_in_bounds")
                stores.append((fine, (2 * k + e, pl.ds(row0(x, 0), NY0)), jnp.where(from_first, low, high)))
            return stores

        plane_loop(0, NX0, body)

    def near_rows(i, plan, planes, depth):
        for n, (sx, sy) in enumerate(NEAR):
            shift = -(sx * NX0 * YP0 + sy * NY0)
            start = plan[n][0]
            if n < 2:
                for dx in range(1, planes + 1):
                    at_buffer = pl.multiple_of(start + (i * planes + dx - 1) * NY0, 8)
                    yield row0(side_plane(sx, dx), 0), NY0, None, shift, at_buffer
            elif n < 4:
                for dy in range(1, depth + 1):
                    at_buffer = pl.multiple_of(start + (i * depth + dy - 1) * NX0, 8)
                    yield row0(0, side_row(sy, dy)), NX0, YP0, shift, at_buffer
            else:
                at_buffer = start + i * corner_rows(depth)
                for x, y, rows in corner_pieces(sx, sy, depth):
                    yield row0(x, y), rows, None, shift, at_buffer
                    at_buffer = at_buffer + rows

    def pack(field, first, count, out, plan, planes, depth):
        def body(i, carry):
            values = []
            for row, rows, stride, _, to in near_rows(i, plan, planes, depth):
                values.append((to, rows, field[first + i, pl.ds(row, rows, stride=stride), :]))
            for to, rows, value in values:
                out[pl.ds(to, rows), :] = value
            return carry

        lax.fori_loop(0, count, body, 0)

    def unpack(field, first, count, landing, plan, planes, depth):
        def body(i, carry):
            values = []
            for row, rows, stride, shift, at_buffer in near_rows(i, plan, planes, depth):
                values.append((pl.ds(row + shift, rows, stride=stride), landing[pl.ds(at_buffer, rows), :]))
            for to, value in values:
                field[first + i, to, :] = value
            return carry

        lax.fori_loop(0, count, body, 0)

    def extra_pieces(k, plan, base, sides):
        for side in sides:
            sx = NEAR[side][0]
            for e in range(2):
                row = row0(side_plane(sx, DEPTH), 0)
                yield k + e, row, row - sx * NX0 * YP0, plan[side][0] + base + e * NY0

    def extra_out(field, k, out, plan, base, sides):
        for f, row, _, to in extra_pieces(k, plan, base, sides):
            out[pl.ds(to, NY0), :] = field[f, pl.ds(row, NY0), :]

    def extra_in(field, k, landing, plan, base, sides):
        for f, _, row, at_buffer in extra_pieces(k, plan, base, sides):
            field[f, pl.ds(row, NY0), :] = landing[pl.ds(at_buffer, NY0), :]

    def near_sends(group, out, landing, plan):
        for (start, rows), offset in zip(plan, NEAR):
            cut = pl.ds(start, rows)
            send(group, out.at[cut], landing.at[cut], offset)

    for k in range(4):
        loads[k].wait()
        permute(k)
    pack(fine, 0, 8, sra, PLAN_A, 4, DEPTH)
    extra_out(fine, 2, sra, PLAN_A, 512, (0,))
    pl.semaphore_wait(barrier, len(BALL))
    near_sends(RAW_A, sra, rra, PLAN_A)
    for k in (4, 5):
        loads[k].wait()
        permute(k)
    pack(fine, 8, 4, srb, PLAN_B, 4, DEPTH)
    extra_out(fine, 10, srb, PLAN_B, 256, (0, 1))
    near_sends(RAW_B, srb, rrb, PLAN_B)

    def children(k, e, x, y_step):
        return fine[2 * k + e, pl.ds(row0(x, y_step), NY1, stride=2), :]

    def coarsen1(big):
        to = pl.ds(row1(big, 0), NY1)
        x = 2 * big
        absorb = sum(children(0, e, x + p, q) for e in range(2) for p in range(2) for q in range(2)) * 0.125
        face_x = sum(children(1, e, x, q) for e in range(2) for q in range(2)) * 0.25
        face_y = sum(children(2, e, x + p, 0) for e in range(2) for p in range(2)) * 0.25
        face_z = sum(children(3, 0, x + p, q) for p in range(2) for q in range(2)) * 0.25
        for k, value in enumerate((absorb, face_x, face_y, face_z)):
            raw1[k, to, :] = value
            smc[big, pl.ds(k * NY1, NY1), :] = value

    for big in range(NX1):
        coarsen1(big)

    def mid_sends(group, src, landing):
        for n, offset in enumerate(MIDS):
            if n < 8:
                send(group, src, landing.at[pl.ds(4 * n, 4)], offset)
            else:
                cut = pl.ds(2 if offset[0] > 0 else 0, 2)
                send(group, src.at[cut], landing.at[pl.ds(16 + 2 * n, 2)], offset)

    mid_sends(MID_COEF, smc, rmc)

    def mid_unpack(landing, store):
        for n, (sx, sy) in enumerate(MIDS):
            planes = range(4) if n < 8 else (range(2, 4) if sx > 0 else range(2))
            first = 4 * n if n < 8 else 16 + 2 * n
            for i, x in enumerate(planes):
                store(row1(x - sx * NX1, -sy * NY1), landing[first + i])

    def both(v):
        return v + pltpu.roll(v, HALF, 1)

    for big in range(NX2):
        grand = lambda k, x, q: raw1[k, pl.ds(row1(x, q), NY2, stride=2), :]
        x = 2 * big
        absorb = both(sum(grand(0, x + p, q) for p in range(2) for q in range(2))) * 0.125
        face_x = both(sum(grand(1, x, q) for q in range(2))) * 0.25
        face_y = both(sum(grand(2, x + p, 0) for p in range(2))) * 0.25
        face_z = sum(grand(3, x + p, q) for p in range(2) for q in range(2)) * 0.25
        low = lanes((NY2, LANES)) < HALF
        face_z = jnp.where(low, face_z, pltpu.roll(face_z, HALF, 1))
        for k, value in enumerate((absorb, face_x, face_y, face_z)):
            raw2[k, pl.ds(row2(big, 0), NY2), :] = value
        s2c[pl.ds(big * NY2, NY2), :] = jnp.where(low, absorb, face_x)
        s2c[pl.ds(8 + big * NY2, NY2), :] = jnp.where(low, face_y, face_z)

    def ball_sends(group, src, landing):
        for n, offset in enumerate(BALL):
            send(group, src, landing.at[n], offset)

    ball_sends(LOW_COEF, s2c, r2c)

    arrived(RAW_A, rra)
    unpack(fine, 0, 8, rra, PLAN_A, 4, DEPTH)
    extra_in(fine, 2, rra, PLAN_A, 512, (0,))
    arrived(RAW_B, rrb)
    unpack(fine, 8, 4, rrb, PLAN_B, 4, DEPTH)
    extra_in(fine, 10, rrb, PLAN_B, 256, (0, 1))
    level0.build(-4, 16, -4, 24, (fine, 8))
    weights = chebyshev_weights(SWEEPS)
    level0.sweep(weights[0], (fine, 10), (fine_a, 0), -4, 16, -4, 24)
    level0.sweep(weights[1], (fine_a, 0), (fine_b, 0), -3, 14, -4, 24)
    level0.sweep(weights[2], (fine_b, 0), (fine_a, 0), -2, 12, -4, 24)
    level0.sweep(weights[3], (fine_a, 0), (fine_b, 0), -1, 10, -4, 24, last=True)

    def rest_fine(x):
        at_row = row0(x, 0)
        steps, _ = level0.residual((fine_b, 0), at_row, NY0)
        return [
            (rest0, (e, pl.ds(x * NY0, NY0)), steps[e] * diag0[e, pl.ds(at_row, NY0), :]) for e in range(2)
        ]

    plane_loop(0, NX0, rest_fine)

    face_x = sum(children(1, e, NX0, q) for e in range(2) for q in range(2)) * 0.25
    raw1[1, pl.ds(row1(NX1, 0), NY1), :] = face_x
    arrived(MID_COEF, rmc)

    def store_raw(to, value):
        for k in range(4):
            raw1[k, pl.ds(to, NY1), :] = value[k * NY1 : (k + 1) * NY1]

    mid_unpack(rmc, store_raw)
    level1.build(-5, 14, -8, 24)
    for big in range(NX1):
        total = sum(
            rest0[e, pl.ds((2 * big + p) * NY0 + q, NY1, stride=2), :]
            for e in range(2) for p in range(2) for q in range(2)
        )
        value = total * 0.125 / diag1[0, pl.ds(row1(big, 0), NY1), :]
        rhs1[0, pl.ds(row1(big, 0), NY1), :] = value
        sg1[big] = value

    mid_sends(MID_RHS, sg1, rg1)

    x = NX1
    grand = lambda k, x, y: raw1[k, pl.ds(row1(x, y), NY2, stride=2), :]
    raw2[1, pl.ds(row2(NX2, 0), NY2), :] = both(grand(1, x, 0) + grand(1, x, 1)) * 0.25
    for big in range(NX2):
        above = both(sum(grand(2, 2 * big + p, NY1) for p in range(2))) * 0.25
        raw2[2, pl.ds(row2(big, NY2), 1), :] = above[0:1]
    diag_own2 = [level2.own_diagonal(big, 0, NY2)[0] for big in range(NX2)]

    def store_rhs1(to, value):
        rhs1[0, pl.ds(to, NY1), :] = value

    arrived(MID_RHS, rg1)
    mid_unpack(rg1, store_rhs1)
    level1.first_from_zero(weights[0], (it1_a, 0), -4, 12, -4, 16)
    level1.sweep(weights[1], (it1_a, 0), (it1_b, 0), -3, 10, -4, 16)
    level1.sweep(weights[2], (it1_b, 0), (it1_a, 0), -2, 8, -4, 16)
    level1.sweep(weights[3], (it1_a, 0), (it1_b, 0), -1, 6, -4, 16, last=True)

    def rest_mid(x):
        at_row = row1(x, 0)
        steps, centre = level1.residual((it1_b, 0), at_row, NY1)
        return [
            (rest1, (pl.ds(x * NY1, NY1),), steps[0] * diag1[0, pl.ds(at_row, NY1), :]),
            (sx1, (x,), centre[0]),
        ]

    plane_loop(0, NX1, rest_mid)
    for big in range(NX2):
        total = sum(rest1[pl.ds((2 * big + p) * NY1 + q, NY2, stride=2), :] for p in range(2) for q in range(2))
        value = both(total) * 0.125 / diag_own2[big]
        rhs2[0, pl.ds(row2(big, 0), NY2), :] = value
        sg2[pl.ds(big * NY2, NY2), :] = value

    ball_sends(LOW_RHS, sg2, rg2)
    mid_sends(MID_ITER, sx1, rx1)
    pack(fine_b, 0, 2, siu, PLAN_U, 4, 4)
    near_sends(FINE_ITER, siu, riu, PLAN_U)

    arrived(LOW_COEF, r2c)
    low8 = lanes((8, LANES)) < HALF
    for n, (i, j) in enumerate(BALL):
        for part in range(2):
            value = r2c[n, pl.ds(8 * part, 8), :]
            other = pltpu.roll(value, HALF, 1)
            for k, full in enumerate((jnp.where(low8, value, other), jnp.where(low8, other, value))):
                for p in range(NX2):
                    to = pl.ds(row2(p - 2 * i, -4 * j), NY2)
                    raw2[2 * part + k, to, :] = full[p * NY2 : (p + 1) * NY2]
    level2.build(-9, 20, -10, 24)
    arrived(LOW_RHS, rg2)
    for n, (i, j) in enumerate(BALL):
        for p in range(NX2):
            rhs2[0, pl.ds(row2(p - 2 * i, -4 * j), NY2), :] = rg2[n, pl.ds(p * NY2, NY2), :]
    coarse = chebyshev_weights(COARSE_SWEEPS)
    level2.first_from_zero(coarse[0], (it2_a, 0), -10, 22, -10, 24)
    src, dst = it2_a, it2_b
    for sweep in range(1, COARSE_SWEEPS):
        reach = COARSE_SWEEPS - 1 - sweep
        first_y, rows = (-10, 24) if reach > 3 else (-6, 16)
        level2.sweep(coarse[sweep], (src, 0), (dst, 0), -3 - reach, 8 + 2 * reach, first_y, rows, last=reach == 0)
        src, dst = dst, src

    def store_it1(to, value):
        it1_b[0, pl.ds(to, NY1), :] = value

    arrived(MID_ITER, rx1)
    mid_unpack(rx1, store_it1)

    def lift1(big):
        stores = []
        for y in (-3, -1):
            value = src[0, pl.ds(row2(big, y), 8), :]
            for p in range(2):
                for q in range(2):
                    to = pl.ds(row1(2 * big + p, 2 * y + q), 8, stride=2)
                    stores.append((it1_a, (0, to), it1_b[0, to, :] + value))
        return stores

    plane_loop(-3, 8, lift1)
    level1.sweep(weights[0], (it1_a, 0), (it1_b, 0), -5, 14, -8, 24)
    level1.sweep(weights[1], (it1_b, 0), (it1_a, 0), -4, 12, -8, 24)
    level1.sweep(weights[2], (it1_a, 0), (it1_b, 0), -3, 10, -4, 16)
    level1.sweep(weights[3], (it1_b, 0), (it1_a, 0), -2, 8, -4, 16, last=True)

    arrived(FINE_ITER, riu)
    unpack(fine_b, 0, 2, riu, PLAN_U, 4, 4)

    def lift0(big):
        stores = []
        for y in (-2, 2):
            value = it1_a[0, pl.ds(row1(big, y), 8), :]
            for e in range(2):
                for p in range(2):
                    for q in range(2):
                        to = pl.ds(row0(2 * big + p, 2 * y + q), 8, stride=2)
                        stores.append((fine_a, (e, to), fine_b[e, to, :] + value))
        return stores

    plane_loop(-2, 8, lift0)
    level0.sweep(weights[0], (fine_a, 0), (fine_b, 0), -3, 14, -4, 24)
    level0.sweep(weights[1], (fine_b, 0), (fine_a, 0), -2, 12, -4, 24)
    level0.sweep(weights[2], (fine_a, 0), (fine_b, 0), -1, 10, -4, 24)
    back = HALF * ((at // 2) % 2) + at // 4
    even = (at % 2) == 0

    def emit(x, news):
        stores = []
        for half in range(2):
            pick = back + 32 * half
            lower = jnp.take_along_axis(news[0], pick, axis=1, mode="promise_in_bounds")
            upper = jnp.take_along_axis(news[1], pick, axis=1, mode="promise_in_bounds")
            stores.append((out_v, (x, slice(None), slice(half * LANES, (half + 1) * LANES)), jnp.where(even, lower, upper)))
        return stores

    level0.sweep(weights[3], (fine_b, 0), None, 0, 8, 0, NY0, last=True, emit=emit)
    store = pltpu.make_async_copy(out_v, out_hbm, out_sem.at[0])
    store.start()
    for group, landing in enumerate((rra, rrb, rmc, r2c, rg1, rg2, rx1, riu)):
        departed(group, landing)
    store.wait()


def solution(mesh):
    counts = (mesh.shape["gx"], mesh.shape["gy"])

    def local(source, initial, absorption, beta_x, beta_y, beta_z):
        f32 = jnp.float32
        v = lambda *shape: pltpu.VMEM(shape, f32)
        scratch = [
            v(6, NX0, NY0, 256), v(12, ROWS0, LANES), v(2, ROWS0, LANES), v(2, ROWS0, LANES),
            v(12, ROWS0, LANES), v(2, ROWS0, LANES), v(2, ROWS0, LANES), v(2, ROWS0, LANES), v(2, 128, LANES),
            v(4, ROWS1, LANES), v(6, ROWS1, LANES), v(1, ROWS1, LANES), v(1, ROWS1, LANES), v(1, ROWS1, LANES),
            v(1, ROWS1, LANES), v(1, ROWS1, LANES), v(32, LANES),
            v(4, ROWS2, LANES), v(6, ROWS2, LANES), v(1, ROWS2, LANES), v(1, ROWS2, LANES), v(1, ROWS2, LANES),
            v(1, ROWS2, LANES), v(1, ROWS2, LANES),
            v(SIZE_A, LANES), v(SIZE_A, LANES), v(SIZE_B, LANES), v(SIZE_B, LANES),
            v(4, 32, LANES), v(44, 32, LANES), v(4, 8, LANES), v(44, 8, LANES), v(4, 8, LANES), v(44, 8, LANES),
            v(16, LANES), v(len(BALL), 16, LANES), v(8, LANES), v(len(BALL), 8, LANES),
            v(SIZE_U, LANES), v(SIZE_U, LANES), v(NX0, NY0, 256),
            pltpu.SemaphoreType.DMA((6,)), pltpu.SemaphoreType.DMA((1,)),
            pltpu.SemaphoreType.DMA((8,)), pltpu.SemaphoreType.DMA((8,)),
        ]
        call = pl.pallas_call(
            lambda *refs: kernel(counts, *refs),
            out_shape=jax.ShapeDtypeStruct((NX0, NY0, 256), f32),
            in_specs=[pl.BlockSpec(memory_space=pl.ANY)] * 6,
            out_specs=pl.BlockSpec(memory_space=pl.ANY),
            scratch_shapes=scratch,
            compiler_params=pltpu.CompilerParams(
                collective_id=0, has_side_effects=True, vmem_limit_bytes=56 * 2**20
            ),
            name="vcycle",
        )
        return call(absorption, beta_x, beta_y, beta_z, source, initial)

    return jax.shard_map(
        local,
        mesh=mesh,
        in_specs=(P("gx", "gy", None),) * 6,
        out_specs=P("gx", "gy", None),
        check_vma=False,
    )
```

```python
import jax
import jax.numpy as jnp
from jax import lax
from jax.experimental import pallas as pl
from jax.experimental.pallas import tpu as pltpu
from jax.sharding import PartitionSpec as P

SWEEPS = 4
COARSE_SWEEPS = 8
LANES = 128
HALF = 64
GROUP = 4
MESH = pl.DeviceIdType.MESH

NX0, NY0, HX0, HY0, YP0 = 8, 16, 5, 5, 26
NX1, NY1, HX1, HY1, YP1 = 4, 8, 6, 9, 26
NX2, NY2, HX2, HY2, YP2 = 2, 4, 10, 12, 28
ROWS0 = 472
ROWS1 = 416
ROWS2 = 616

DEPTH = 5
NEAR = [(-1, 0), (1, 0), (0, -1), (0, 1), (-1, -1), (-1, 1), (1, -1), (1, 1)]
WIDE = [(-2, 0), (2, 0), (-2, -1), (-2, 1), (2, -1), (2, 1)]
LINE = [1, -1, 2, -2, 3, -3, 4, -4, 5, -5]
COLUMNS = [(-1, 11), (1, 11), (-2, 7), (2, 7), (-3, 3), (3, 3)]


def ball_offsets():
    offsets = []
    for i in range(-5, 6):
        for j in range(-3, 4):
            far_x = 2 * abs(i) - 1 if i else 0
            far_y = 4 * abs(j) - 3 if j else 0
            if (i, j) != (0, 0) and far_x + far_y <= (11 if i and j else 10):
                offsets.append((i, j))
    return offsets


BALL = ball_offsets()


def chebyshev_weights(sweeps):
    cheb_theta = 1.125
    cheb_delta = 0.875
    cheb_sigma = cheb_theta / cheb_delta
    rho_old = 1.0 / cheb_sigma
    weights = [(0.0, 1.0 / cheb_theta)]
    for sweep in range(1, sweeps):
        rho_new = 1.0 / (2.0 * cheb_sigma - rho_old)
        weights.append((rho_new * rho_old, 2.0 * rho_new / cheb_delta))
        rho_old = rho_new
    return weights


def row0(x, y):
    return (x + HX0) * YP0 + y + HY0


def row1(x, y):
    return (x + HX1) * YP1 + y + HY1


def row2(x, y):
    return (x + HX2) * YP2 + y + HY2


def lanes(shape):
    return lax.broadcasted_iota(jnp.int32, shape, len(shape) - 1)


def shift_down(v):
    return jnp.where(lanes(v.shape) < HALF, pltpu.roll(v, HALF + 1, 1), pltpu.roll(v, HALF, 1))


def shift_up(v):
    return jnp.where(lanes(v.shape) < HALF, pltpu.roll(v, HALF, 1), pltpu.roll(v, HALF - 1, 1))


def z_neighbours(values, level):
    if level == 0:
        return (shift_down(values[1]), values[0]), (values[1], shift_up(values[0]))
    if level == 1:
        return (shift_down(values[0]),), (shift_up(values[0]),)
    return (pltpu.roll(values[0], 1, 1),), (pltpu.roll(values[0], LANES - 1, 1),)


def z_ends(shape, level, half):
    at = lanes(shape)
    if level == 0:
        return (at == 0) if half == 0 else None, (at == LANES - 1) if half == 1 else None
    if level == 1:
        return at == 0, at == LANES - 1
    return (at % HALF) == 0, (at % HALF) == HALF - 1


def plane_loop(first, count, body, group=GROUP):
    def several(start, n):
        stores = []
        for i in range(n):
            stores += body(start + i)
        for ref, index, value in stores:
            ref[index] = value

    def step(i, carry):
        several(first + group * i, group)
        return carry

    if count // group > 1:
        lax.fori_loop(0, count // group, step, 0)
        done = count // group * group
    else:
        done = 0
    if done < count:
        several(first + done, count - done)


class Level:
    def __init__(self, number, halves, row, pitch, raw, coef, diag, rhs, update):
        self.number, self.halves, self.row, self.pitch = number, halves, row, pitch
        self.raw, self.coef, self.diag, self.rhs, self.update = raw, coef, diag, rhs, update
        self.scale = 0.25**number

    def faces(self, at, rows):
        n, raw = self.halves, self.raw
        take = lambda k, e, shift=0: raw[k * n + e, pl.ds(at + shift, rows), :]
        low_z = [take(3, e) for e in range(n)]
        _, high_z = z_neighbours(low_z, self.number)
        out = []
        for e in range(n):
            _, top = z_ends((rows, LANES), self.number, e)
            upper = high_z[e] if top is None else jnp.where(top, 0.0, high_z[e])
            faces = [take(1, e), take(1, e, self.pitch), take(2, e), take(2, e, 1), low_z[e], upper]
            total = (faces[0] + faces[1]) + (faces[2] + faces[3]) + (faces[4] + faces[5])
            out.append((faces, take(0, e) + self.scale * total))
        return out

    def own_diagonal(self, x, y, rows):
        return [d for _, d in self.faces(self.row(x, y), rows)]

    def build(self, first_x, count, first_y, rows, source=None):
        n = self.halves

        def body(x):
            at = self.row(x, first_y)
            stores = []
            for e, (faces, diagonal) in enumerate(self.faces(at, rows)):
                inverse = 1.0 / diagonal
                low, _ = z_ends((rows, LANES), self.number, e)
                if low is not None:
                    faces[4] = jnp.where(low, 0.0, faces[4])
                scaled = self.scale * inverse
                for c in range(6):
                    stores.append((self.coef, (c * n + e, pl.ds(at, rows)), faces[c] * scaled))
                stores.append((self.diag, (e, pl.ds(at, rows)), diagonal))
                if source is not None:
                    ref, base = source
                    stores.append((self.rhs, (e, pl.ds(at, rows)), ref[base + e, pl.ds(at, rows), :] * inverse))
            return stores

        plane_loop(first_x, count, body)

    def residual(self, src, at, rows):
        n = self.halves
        ref, base = src
        take = lambda e, shift=0: ref[base + e, pl.ds(at + shift, rows), :]
        centre = [take(e) for e in range(n)]
        below, above = z_neighbours(centre, self.number)
        out = []
        for e in range(n):
            c = lambda k: self.coef[k * n + e, pl.ds(at, rows), :]
            t = self.rhs[e, pl.ds(at, rows), :] - centre[e]
            t_x = c(0) * take(e, -self.pitch) + c(1) * take(e, self.pitch)
            t_y = c(2) * take(e, -1) + c(3) * take(e, 1)
            t_z = c(4) * below[e] + c(5) * above[e]
            out.append(t + (t_x + t_y) + t_z)
        return out, centre

    def sweep(self, pair, src, dst, first_x, count, first_y, rows, last=False, emit=None):
        def body(x):
            at = self.row(x, first_y)
            steps, centre = self.residual(src, at, rows)
            news, stores = [], []
            for e in range(self.halves):
                new = pair[1] * steps[e]
                if pair[0] != 0.0:
                    new = pair[0] * self.update[e, pl.ds(at, rows), :] + new
                if not last:
                    stores.append((self.update, (e, pl.ds(at, rows)), new))
                news.append(centre[e] + new)
            if emit is not None:
                return emit(x, news)
            ref, base = dst
            return stores + [(ref, (base + e, pl.ds(at, rows)), news[e]) for e in range(self.halves)]

        plane_loop(first_x, count, body)

    def first_from_zero(self, pair, dst, first_x, count, first_y, rows):
        def body(x):
            at = self.row(x, first_y)
            ref, base = dst
            stores = []
            for e in range(self.halves):
                new = pair[1] * self.rhs[e, pl.ds(at, rows), :]
                stores.append((self.update, (e, pl.ds(at, rows)), new))
                stores.append((ref, (base + e, pl.ds(at, rows)), new))
            return stores

        plane_loop(first_x, count, body)


def corner_pieces(sx, sy, depth):
    pieces = []
    for dx in range(1, depth):
        rows = depth - dx
        pieces.append((NX0 - dx if sx > 0 else dx - 1, NY0 - rows if sy > 0 else 0, rows))
    return pieces


def side_plane(sx, dx):
    return NX0 - dx if sx > 0 else dx - 1


def side_row(sy, dy):
    return NY0 - dy if sy > 0 else dy - 1


def near_plan(fields, planes, depth, extra=(0, 0)):
    sizes = [fields * planes * NY0 + extra[0], fields * planes * NY0 + extra[1]]
    sizes += [fields * depth * NX0] * 2 + [-(-fields * corner_rows(depth) // 8) * 8] * 4
    starts = [sum(sizes[:n]) for n in range(8)]
    return list(zip(starts, sizes)), sum(sizes)


def corner_rows(depth):
    return depth * (depth - 1) // 2


def mid_corner(sx, sy):
    for dx in range(1, NX1 + 1):
        rows = 7 - dx
        yield (NX1 - dx if sx > 0 else dx - 1), (NY1 - rows if sy > 0 else 0), rows


def mid_plan(fields):
    sizes = [fields * NX1 * NY1] * 4 + [-(-fields * 18 // 8) * 8] * 4
    return list(zip([sum(sizes[:n]) for n in range(8)], sizes)), sum(sizes)


def wide_pieces(sx, sy):
    for dx in range(2):
        x = NX1 - 1 - dx if sx > 0 else dx
        if sy == 0:
            yield x, 0, NY1
        else:
            yield x, (NY1 - 2 if sy > 0 else 0), 2


WIDE_SIZES = [96, 96, 24, 24, 24, 24]
WIDE_STARTS = [sum(WIDE_SIZES[:n]) for n in range(6)]
RAW_A, RAW_B, LOW_LINE, MID_COEF, MID_RHS, LOW_COEF, LOW_RHS, MID_ITER, MID_WIDE, FINE_ITER = range(10)
PLAN_M4, SIZE_M4 = mid_plan(4)
PLAN_M1, SIZE_M1 = mid_plan(1)
PLAN_A, SIZE_A = near_plan(8, 4, DEPTH, (32, 0))
PLAN_B, SIZE_B = near_plan(4, 4, DEPTH, (32, 32))
PLAN_U, SIZE_U = near_plan(2, 4, 4)


def kernel(counts, *refs):
    inputs, out_hbm = refs[:6], refs[6]
    (nat, fine, fine_a, fine_b, coef0, diag0, rhs0, upd0, rest0,
     raw1, coef1, diag1, rhs1, upd1, it1_a, it1_b, rest1,
     raw2, coef2, diag2, rhs2, upd2, it2_a, it2_b,
     sra, rra, srb, rrb, smc, cmc, rmc, sg1, cg1, rg1, sx1, cx1, rx1, r2l, r2c, sg2, rg2, siu, riu, swi, rwi, out_v,
     in_sem, out_sem, sent, got) = refs[7:]
    count_x, count_y = counts
    me_x, me_y = lax.axis_index("gx"), lax.axis_index("gy")

    def device(offset):
        return (lax.rem(me_x + offset[0] + count_x, count_x), lax.rem(me_y + offset[1] + count_y, count_y))

    loads = [pltpu.make_async_copy(inputs[k], nat.at[k], in_sem.at[k]) for k in range(6)]
    for load in loads:
        load.start()
    barrier = pltpu.get_barrier_semaphore()
    for offset in NEAR + [o for o in BALL if o not in NEAR]:
        pl.semaphore_signal(barrier, inc=1, device_id=device(offset), device_id_type=MESH)

    def send(group, src, dst, offset):
        pltpu.make_async_remote_copy(
            src_ref=src, dst_ref=dst, send_sem=sent.at[group], recv_sem=got.at[group],
            device_id=device(offset), device_id_type=MESH,
        ).start()

    def arrived(group, landing):
        pltpu.make_async_copy(landing, landing, got.at[group]).wait()

    def departed(group, landing):
        pltpu.make_async_copy(landing, landing, sent.at[group]).wait()

    level0 = Level(0, 2, row0, YP0, fine, coef0, diag0, rhs0, upd0)
    level1 = Level(1, 1, row1, YP1, raw1, coef1, diag1, rhs1, upd1)
    level2 = Level(2, 1, row2, YP2, raw2, coef2, diag2, rhs2, upd2)

    at = lanes((NY0, LANES))
    cell = 4 * (at % HALF) + 2 * (at // HALF)
    from_first = (at % HALF) < HALF // 2
    picks = [(cell + e) % LANES for e in range(2)]

    def permute(k):
        def body(x):
            first = nat[k, x, :, 0:LANES]
            second = nat[k, x, :, LANES : 2 * LANES]
            stores = []
            for e in range(2):
                low = jnp.take_along_axis(first, picks[e], axis=1, mode="promise_in_bounds")
                high = jnp.take_along_axis(second, picks[e], axis=1, mode="promise_in_bounds")
                stores.append((fine, (2 * k + e, pl.ds(row0(x, 0), NY0)), jnp.where(from_first, low, high)))
            return stores

        plane_loop(0, NX0, body)

    def near_rows(i, plan, planes, depth):
        for n, (sx, sy) in enumerate(NEAR):
            shift = -(sx * NX0 * YP0 + sy * NY0)
            start = plan[n][0]
            if n < 2:
                for dx in range(1, planes + 1):
                    at_buffer = pl.multiple_of(start + (i * planes + dx - 1) * NY0, 8)
                    yield row0(side_plane(sx, dx), 0), NY0, None, shift, at_buffer
            elif n < 4:
                for dy in range(1, depth + 1):
                    at_buffer = pl.multiple_of(start + (i * depth + dy - 1) * NX0, 8)
                    yield row0(0, side_row(sy, dy)), NX0, YP0, shift, at_buffer
            else:
                at_buffer = start + i * corner_rows(depth)
                for x, y, rows in corner_pieces(sx, sy, depth):
                    yield row0(x, y), rows, None, shift, at_buffer
                    at_buffer = at_buffer + rows

    def pack(field, first, count, out, plan, planes, depth):
        def body(i, carry):
            values = []
            for row, rows, stride, _, to in near_rows(i, plan, planes, depth):
                values.append((to, rows, field[first + i, pl.ds(row, rows, stride=stride), :]))
            for to, rows, value in values:
                out[pl.ds(to, rows), :] = value
            return carry

        lax.fori_loop(0, count, body, 0)

    def unpack(field, first, count, landing, plan, planes, depth):
        def body(i, carry):
            values = []
            for row, rows, stride, shift, at_buffer in near_rows(i, plan, planes, depth):
                values.append((pl.ds(row + shift, rows, stride=stride), landing[pl.ds(at_buffer, rows), :]))
            for to, value in values:
                field[first + i, to, :] = value
            return carry

        lax.fori_loop(0, count, body, 0)

    def extra_pieces(k, plan, base, sides):
        for side in sides:
            sx = NEAR[side][0]
            for e in range(2):
                row = row0(side_plane(sx, DEPTH), 0)
                yield k + e, row, row - sx * NX0 * YP0, plan[side][0] + base + e * NY0

    def extra_out(field, k, out, plan, base, sides):
        for f, row, _, to in extra_pieces(k, plan, base, sides):
            out[pl.ds(to, NY0), :] = field[f, pl.ds(row, NY0), :]

    def extra_in(field, k, landing, plan, base, sides):
        for f, _, row, at_buffer in extra_pieces(k, plan, base, sides):
            field[f, pl.ds(row, NY0), :] = landing[pl.ds(at_buffer, NY0), :]

    def near_sends(group, out, landing, plan):
        for (start, rows), offset in zip(plan, NEAR):
            cut = pl.ds(start, rows)
            send(group, out.at[cut], landing.at[cut], offset)

    for k in range(4):
        loads[k].wait()
        permute(k)
    pack(fine, 0, 8, sra, PLAN_A, 4, DEPTH)
    extra_out(fine, 2, sra, PLAN_A, 512, (0,))
    pl.semaphore_wait(barrier, len(BALL))
    near_sends(RAW_A, sra, rra, PLAN_A)
    for k in (4, 5):
        loads[k].wait()
        permute(k)
    pack(fine, 8, 4, srb, PLAN_B, 4, DEPTH)
    extra_out(fine, 10, srb, PLAN_B, 256, (0, 1))
    near_sends(RAW_B, srb, rrb, PLAN_B)

    def children(k, e, x, y_step):
        return fine[2 * k + e, pl.ds(row0(x, y_step), NY1, stride=2), :]

    def coarsen1(big):
        to = pl.ds(row1(big, 0), NY1)
        x = 2 * big
        absorb = sum(children(0, e, x + p, q) for e in range(2) for p in range(2) for q in range(2)) * 0.125
        face_x = sum(children(1, e, x, q) for e in range(2) for q in range(2)) * 0.25
        face_y = sum(children(2, e, x + p, 0) for e in range(2) for p in range(2)) * 0.25
        face_z = sum(children(3, 0, x + p, q) for p in range(2) for q in range(2)) * 0.25
        for k, value in enumerate((absorb, face_x, face_y, face_z)):
            raw1[k, to, :] = value
            smc[pl.ds(k * 32 + big * NY1, NY1), :] = value

    for big in range(NX1):
        coarsen1(big)

    def mid_sends(group, own, corner, landing, plan, fields):
        for n, offset in enumerate(NEAR[4:]):
            to = 0
            for k in range(fields):
                for x, y, rows in mid_corner(*offset):
                    corner[n, pl.ds(to, rows), :] = own[pl.ds(k * 32 + x * NY1 + y, rows), :]
                    to += rows
        for n, ((start, rows), offset) in enumerate(zip(plan, NEAR)):
            send(group, own if n < 4 else corner.at[n - 4], landing.at[pl.ds(start, rows)], offset)

    def mid_unpack(landing, plan, fields, store):
        for n, ((start, _), (sx, sy)) in enumerate(zip(plan, NEAR)):
            for k in range(fields):
                pieces = mid_corner(sx, sy) if n >= 4 else ((x, 0, NY1) for x in range(NX1))
                for x, y, rows in pieces:
                    store(k, pl.ds(row1(x - sx * NX1, y - sy * NY1), rows), landing[pl.ds(start, rows), :])
                    start += rows

    def both(v):
        return v + pltpu.roll(v, HALF, 1)

    for big in range(NX2):
        grand = lambda k, x, q: raw1[k, pl.ds(row1(x, q), NY2, stride=2), :]
        x = 2 * big
        absorb = both(sum(grand(0, x + p, q) for p in range(2) for q in range(2))) * 0.125
        face_x = both(sum(grand(1, x, q) for q in range(2))) * 0.25
        face_y = both(sum(grand(2, x + p, 0) for p in range(2))) * 0.25
        face_z = sum(grand(3, x + p, q) for p in range(2) for q in range(2)) * 0.25
        low = lanes((NY2, LANES)) < HALF
        face_z = jnp.where(low, face_z, pltpu.roll(face_z, HALF, 1))
        for k, value in enumerate((absorb, face_x, face_y, face_z)):
            raw2[k, pl.ds(row2(big, 0), NY2), :] = value
        r2l[0, pl.ds(big * NY2, NY2), :] = jnp.where(low, absorb, face_x)
        r2l[0, pl.ds(8 + big * NY2, NY2), :] = jnp.where(low, face_y, face_z)

    def ball_sends(group, src, landing):
        for n, offset in enumerate(BALL):
            send(group, src, landing.at[n], offset)

    for n, i in enumerate(LINE):
        send(LOW_LINE, r2l.at[0], r2l.at[n + 1], (i, 0))
    mid_sends(MID_COEF, smc, cmc, rmc, PLAN_M4, 4)

    arrived(RAW_A, rra)
    unpack(fine, 0, 8, rra, PLAN_A, 4, DEPTH)
    extra_in(fine, 2, rra, PLAN_A, 512, (0,))
    arrived(RAW_B, rrb)
    unpack(fine, 8, 4, rrb, PLAN_B, 4, DEPTH)
    extra_in(fine, 10, rrb, PLAN_B, 256, (0, 1))
    level0.build(-4, 16, -4, 24, (fine, 8))
    weights = chebyshev_weights(SWEEPS)
    level0.sweep(weights[0], (fine, 10), (fine_a, 0), -4, 16, -4, 24)
    level0.sweep(weights[1], (fine_a, 0), (fine_b, 0), -3, 14, -4, 24)
    level0.sweep(weights[2], (fine_b, 0), (fine_a, 0), -2, 12, -4, 24)
    level0.sweep(weights[3], (fine_a, 0), (fine_b, 0), -1, 10, -4, 24, last=True)

    def rest_fine(x):
        at_row = row0(x, 0)
        steps, _ = level0.residual((fine_b, 0), at_row, NY0)
        return [
            (rest0, (e, pl.ds(x * NY0, NY0)), steps[e] * diag0[e, pl.ds(at_row, NY0), :]) for e in range(2)
        ]

    plane_loop(0, NX0, rest_fine)

    face_x = sum(children(1, e, NX0, q) for e in range(2) for q in range(2)) * 0.25
    raw1[1, pl.ds(row1(NX1, 0), NY1), :] = face_x
    arrived(MID_COEF, rmc)

    def store_raw(k, to, value):
        raw1[k, to, :] = value

    mid_unpack(rmc, PLAN_M4, 4, store_raw)
    level1.build(-4, 11, -8, 24)
    for big in range(NX1):
        total = sum(
            rest0[e, pl.ds((2 * big + p) * NY0 + q, NY1, stride=2), :]
            for e in range(2) for p in range(2) for q in range(2)
        )
        value = total * 0.125 / diag1[0, pl.ds(row1(big, 0), NY1), :]
        rhs1[0, pl.ds(row1(big, 0), NY1), :] = value
        sg1[pl.ds(big * NY1, NY1), :] = value

    mid_sends(MID_RHS, sg1, cg1, rg1, PLAN_M1, 1)
    arrived(LOW_LINE, r2l.at[pl.ds(1, 10)])
    start = 0
    for j, slots in COLUMNS:
        send(LOW_COEF, r2l.at[pl.ds(0, slots)], r2c.at[pl.ds(start, slots)], (0, j))
        start += slots

    x = NX1
    grand = lambda k, x, y: raw1[k, pl.ds(row1(x, y), NY2, stride=2), :]
    raw2[1, pl.ds(row2(NX2, 0), NY2), :] = both(grand(1, x, 0) + grand(1, x, 1)) * 0.25
    for big in range(NX2):
        above = both(sum(grand(2, 2 * big + p, NY1) for p in range(2))) * 0.25
        raw2[2, pl.ds(row2(big, NY2), 1), :] = above[0:1]
    diag_own2 = [level2.own_diagonal(big, 0, NY2)[0] for big in range(NX2)]

    def store_rhs1(k, to, value):
        rhs1[0, to, :] = value

    arrived(MID_RHS, rg1)
    mid_unpack(rg1, PLAN_M1, 1, store_rhs1)
    level1.first_from_zero(weights[0], (it1_a, 0), -4, 12, -4, 16)
    level1.sweep(weights[1], (it1_a, 0), (it1_b, 0), -3, 10, -4, 16)
    level1.sweep(weights[2], (it1_b, 0), (it1_a, 0), -2, 8, -4, 16)
    level1.sweep(weights[3], (it1_a, 0), (it1_b, 0), -1, 6, -4, 16, last=True)

    def rest_mid(x):
        at_row = row1(x, 0)
        steps, centre = level1.residual((it1_b, 0), at_row, NY1)
        return [
            (rest1, (pl.ds(x * NY1, NY1),), steps[0] * diag1[0, pl.ds(at_row, NY1), :]),
            (sx1, (pl.ds(x * NY1, NY1),), centre[0]),
        ]

    plane_loop(0, NX1, rest_mid)
    rhs_own2 = []
    for big in range(NX2):
        total = sum(rest1[pl.ds((2 * big + p) * NY1 + q, NY2, stride=2), :] for p in range(2) for q in range(2))
        rhs_own2.append(both(total) * 0.125 / diag_own2[big])
        rhs2[0, pl.ds(row2(big, 0), NY2), :] = rhs_own2[big]
    sg2[...] = jnp.where(low, rhs_own2[0], rhs_own2[1])

    ball_sends(LOW_RHS, sg2, rg2)
    mid_sends(MID_ITER, sx1, cx1, rx1, PLAN_M1, 1)
    pack(fine_b, 0, 2, siu, PLAN_U, 4, 4)
    near_sends(FINE_ITER, siu, riu, PLAN_U)
    for n, offset in enumerate(WIDE):
        to = WIDE_STARTS[n]
        for k in range(6):
            own, base = ((smc, 32 * k), (sg1, 0), (sx1, 0))[max(k - 3, 0)]
            for x, y, rows in wide_pieces(*offset):
                swi[pl.ds(to, rows), :] = own[pl.ds(base + x * NY1 + y, rows), :]
                to += rows
        cut = pl.ds(WIDE_STARTS[n], WIDE_SIZES[n])
        send(MID_WIDE, swi.at[cut], rwi.at[cut], offset)

    arrived(LOW_COEF, r2c)
    low8 = lanes((8, LANES)) < HALF

    def two_fields(value):
        other = pltpu.roll(value, HALF, 1)
        return jnp.where(low8, value, other), jnp.where(low8, other, value)

    def low_unpack(ref, slot, i, j):
        for part in range(2):
            for k, full in enumerate(two_fields(ref[slot, pl.ds(8 * part, 8), :])):
                for p in range(NX2):
                    to = pl.ds(row2(p - 2 * i, -4 * j), NY2)
                    raw2[2 * part + k, to, :] = full[p * NY2 : (p + 1) * NY2]

    for n, i in enumerate(LINE):
        low_unpack(r2l, n + 1, i, 0)
    start = 0
    for j, slots in COLUMNS:
        for n, i in enumerate(([0] + LINE)[:slots]):
            low_unpack(r2c, start + n, i, j)
        start += slots
    level2.build(-9, 20, -10, 24)
    arrived(LOW_RHS, rg2)
    for n, (i, j) in enumerate(BALL):
        value = rg2[n]
        other = pltpu.roll(value, HALF, 1)
        rhs2[0, pl.ds(row2(-2 * i, -4 * j), NY2), :] = jnp.where(low, value, other)
        rhs2[0, pl.ds(row2(1 - 2 * i, -4 * j), NY2), :] = jnp.where(low, other, value)
    coarse = chebyshev_weights(COARSE_SWEEPS)
    level2.first_from_zero(coarse[0], (it2_a, 0), -10, 22, -10, 24)
    src, dst = it2_a, it2_b
    for sweep in range(1, COARSE_SWEEPS):
        reach = COARSE_SWEEPS - 1 - sweep
        first_y, rows = (-10, 24) if reach > 3 else (-6, 16)
        level2.sweep(coarse[sweep], (src, 0), (dst, 0), -3 - reach, 8 + 2 * reach, first_y, rows, last=reach == 0)
        src, dst = dst, src

    def store_it1(k, to, value):
        it1_b[0, to, :] = value

    arrived(MID_ITER, rx1)
    mid_unpack(rx1, PLAN_M1, 1, store_it1)
    arrived(MID_WIDE, rwi)
    for n, (sx, sy) in enumerate(WIDE):
        start = WIDE_STARTS[n]
        for k in range(6):
            ref, field = (raw1, k) if k < 4 else ((rhs1, 0) if k == 4 else (it1_b, 0))
            for x, y, rows in wide_pieces(sx, sy):
                ref[field, pl.ds(row1(x - sx * NX1, y - sy * NY1), rows), :] = rwi[pl.ds(start, rows), :]
                start += rows
    level1.build(-5, 1, -8, 24)
    level1.build(7, 2, -8, 24)

    def lift1(big):
        stores = []
        for y in (-3, -1):
            value = src[0, pl.ds(row2(big, y), 8), :]
            for p in range(2):
                for q in range(2):
                    to = pl.ds(row1(2 * big + p, 2 * y + q), 8, stride=2)
                    stores.append((it1_a, (0, to), it1_b[0, to, :] + value))
        return stores

    plane_loop(-3, 8, lift1)
    level1.sweep(weights[0], (it1_a, 0), (it1_b, 0), -5, 14, -8, 24)
    level1.sweep(weights[1], (it1_b, 0), (it1_a, 0), -4, 12, -8, 24)
    level1.sweep(weights[2], (it1_a, 0), (it1_b, 0), -3, 10, -4, 16)
    level1.sweep(weights[3], (it1_b, 0), (it1_a, 0), -2, 8, -4, 16, last=True)

    arrived(FINE_ITER, riu)
    unpack(fine_b, 0, 2, riu, PLAN_U, 4, 4)

    def lift0(big):
        stores = []
        for y in (-2, 2):
            value = it1_a[0, pl.ds(row1(big, y), 8), :]
            for e in range(2):
                for p in range(2):
                    for q in range(2):
                        to = pl.ds(row0(2 * big + p, 2 * y + q), 8, stride=2)
                        stores.append((fine_a, (e, to), fine_b[e, to, :] + value))
        return stores

    plane_loop(-2, 8, lift0)
    level0.sweep(weights[0], (fine_a, 0), (fine_b, 0), -3, 14, -4, 24)
    level0.sweep(weights[1], (fine_b, 0), (fine_a, 0), -2, 12, -4, 24)
    level0.sweep(weights[2], (fine_a, 0), (fine_b, 0), -1, 10, -4, 24)
    back = HALF * ((at // 2) % 2) + at // 4
    even = (at % 2) == 0

    def emit(x, news):
        stores = []
        for half in range(2):
            pick = back + 32 * half
            lower = jnp.take_along_axis(news[0], pick, axis=1, mode="promise_in_bounds")
            upper = jnp.take_along_axis(news[1], pick, axis=1, mode="promise_in_bounds")
            stores.append((out_v, (x, slice(None), slice(half * LANES, (half + 1) * LANES)), jnp.where(even, lower, upper)))
        return stores

    level0.sweep(weights[3], (fine_b, 0), None, 0, 8, 0, NY0, last=True, emit=emit)
    store = pltpu.make_async_copy(out_v, out_hbm, out_sem.at[0])
    store.start()
    for group, landing in enumerate((rra, rrb, r2l.at[pl.ds(1, 10)], rmc, rg1, r2c, rg2, rx1, rwi, riu)):
        departed(group, landing)
    store.wait()


def solution(mesh):
    counts = (mesh.shape["gx"], mesh.shape["gy"])

    def local(source, initial, absorption, beta_x, beta_y, beta_z):
        f32 = jnp.float32
        v = lambda *shape: pltpu.VMEM(shape, f32)
        scratch = [
            v(6, NX0, NY0, 256), v(12, ROWS0, LANES), v(2, ROWS0, LANES), v(2, ROWS0, LANES),
            v(12, ROWS0, LANES), v(2, ROWS0, LANES), v(2, ROWS0, LANES), v(2, ROWS0, LANES), v(2, 128, LANES),
            v(4, ROWS1, LANES), v(6, ROWS1, LANES), v(1, ROWS1, LANES), v(1, ROWS1, LANES), v(1, ROWS1, LANES),
            v(1, ROWS1, LANES), v(1, ROWS1, LANES), v(32, LANES),
            v(4, ROWS2, LANES), v(6, ROWS2, LANES), v(1, ROWS2, LANES), v(1, ROWS2, LANES), v(1, ROWS2, LANES),
            v(1, ROWS2, LANES), v(1, ROWS2, LANES),
            v(SIZE_A, LANES), v(SIZE_A, LANES), v(SIZE_B, LANES), v(SIZE_B, LANES),
            v(128, LANES), v(4, 72, LANES), v(SIZE_M4, LANES),
            v(32, LANES), v(4, 24, LANES), v(SIZE_M1, LANES), v(32, LANES), v(4, 24, LANES), v(SIZE_M1, LANES),
            v(11, 16, LANES), v(42, 16, LANES), v(NY2, LANES), v(len(BALL), NY2, LANES),
            v(SIZE_U, LANES), v(SIZE_U, LANES), v(288, LANES), v(288, LANES), v(NX0, NY0, 256),
            pltpu.SemaphoreType.DMA((6,)), pltpu.SemaphoreType.DMA((1,)),
            pltpu.SemaphoreType.DMA((10,)), pltpu.SemaphoreType.DMA((10,)),
        ]
        call = pl.pallas_call(
            lambda *refs: kernel(counts, *refs),
            out_shape=jax.ShapeDtypeStruct((NX0, NY0, 256), f32),
            in_specs=[pl.BlockSpec(memory_space=pl.ANY)] * 6,
            out_specs=pl.BlockSpec(memory_space=pl.ANY),
            scratch_shapes=scratch,
            compiler_params=pltpu.CompilerParams(
                collective_id=0, has_side_effects=True, vmem_limit_bytes=56 * 2**20
            ),
            name="vcycle",
        )
        return call(absorption, beta_x, beta_y, beta_z, source, initial)

    return jax.shard_map(
        local,
        mesh=mesh,
        in_specs=(P("gx", "gy", None),) * 6,
        out_specs=P("gx", "gy", None),
        check_vma=False,
    )
```

```python
import jax
import jax.numpy as jnp
from jax import lax
from jax.experimental import pallas as pl
from jax.experimental.pallas import tpu as pltpu
from jax.sharding import PartitionSpec as P

SWEEPS = 4
COARSE_SWEEPS = 8
LANES = 128
HALF = 64
GROUP = 4
MESH = pl.DeviceIdType.MESH

NX0, NY0, HX0, HY0, YP0 = 8, 16, 5, 5, 26
NX1, NY1, HX1, HY1, YP1 = 4, 8, 6, 9, 26
NX2, NY2, HX2, HY2, YP2 = 2, 4, 10, 12, 28
ROWS0 = 472
ROWS1 = 416
ROWS2 = 616

DEPTH = 4
NEAR = [(-1, 0), (1, 0), (0, -1), (0, 1), (-1, -1), (-1, 1), (1, -1), (1, 1)]
WIDE = [(-2, 0), (2, 0), (-2, -1), (-2, 1), (2, -1), (2, 1)]
LINE = [1, -1, 2, -2, 3, -3, 4, -4, 5, -5]
COLUMNS = [(-1, 11), (1, 11), (-2, 7), (2, 7), (-3, 3), (3, 3)]


def ball_offsets():
    offsets = []
    for i in range(-5, 6):
        for j in range(-3, 4):
            far_x = 2 * abs(i) - 1 if i else 0
            far_y = 4 * abs(j) - 3 if j else 0
            if (i, j) != (0, 0) and far_x + far_y <= (11 if i and j else 10):
                offsets.append((i, j))
    return offsets


BALL = ball_offsets()


def chebyshev_weights(sweeps):
    cheb_theta = 1.125
    cheb_delta = 0.875
    cheb_sigma = cheb_theta / cheb_delta
    rho_old = 1.0 / cheb_sigma
    weights = [(0.0, 1.0 / cheb_theta)]
    for sweep in range(1, sweeps):
        rho_new = 1.0 / (2.0 * cheb_sigma - rho_old)
        weights.append((rho_new * rho_old, 2.0 * rho_new / cheb_delta))
        rho_old = rho_new
    return weights


def row0(x, y):
    return (x + HX0) * YP0 + y + HY0


def row1(x, y):
    return (x + HX1) * YP1 + y + HY1


def row2(x, y):
    return (x + HX2) * YP2 + y + HY2


def lanes(shape):
    return lax.broadcasted_iota(jnp.int32, shape, len(shape) - 1)


def shift_down(v):
    return jnp.where(lanes(v.shape) < HALF, pltpu.roll(v, HALF + 1, 1), pltpu.roll(v, HALF, 1))


def shift_up(v):
    return jnp.where(lanes(v.shape) < HALF, pltpu.roll(v, HALF, 1), pltpu.roll(v, HALF - 1, 1))


def z_neighbours(values, level):
    if level == 0:
        return (shift_down(values[1]), values[0]), (values[1], shift_up(values[0]))
    if level == 1:
        return (shift_down(values[0]),), (shift_up(values[0]),)
    return (pltpu.roll(values[0], 1, 1),), (pltpu.roll(values[0], LANES - 1, 1),)


def z_ends(shape, level, half):
    at = lanes(shape)
    if level == 0:
        return (at == 0) if half == 0 else None, (at == LANES - 1) if half == 1 else None
    if level == 1:
        return at == 0, at == LANES - 1
    return (at % HALF) == 0, (at % HALF) == HALF - 1


def plane_loop(first, count, body, group=GROUP):
    def several(start, n):
        stores = []
        for i in range(n):
            stores += body(start + i)
        for ref, index, value in stores:
            ref[index] = value

    def step(i, carry):
        several(first + group * i, group)
        return carry

    if count // group > 1:
        lax.fori_loop(0, count // group, step, 0)
        done = count // group * group
    else:
        done = 0
    if done < count:
        several(first + done, count - done)


class Level:
    def __init__(self, number, halves, row, pitch, raw, coef, diag, rhs, update):
        self.number, self.halves, self.row, self.pitch = number, halves, row, pitch
        self.raw, self.coef, self.diag, self.rhs, self.update = raw, coef, diag, rhs, update
        self.scale = 0.25**number

    def faces(self, at, rows):
        n, raw = self.halves, self.raw
        take = lambda k, e, shift=0: raw[k * n + e, pl.ds(at + shift, rows), :]
        low_z = [take(3, e) for e in range(n)]
        _, high_z = z_neighbours(low_z, self.number)
        out = []
        for e in range(n):
            _, top = z_ends((rows, LANES), self.number, e)
            upper = high_z[e] if top is None else jnp.where(top, 0.0, high_z[e])
            faces = [take(1, e), take(1, e, self.pitch), take(2, e), take(2, e, 1), low_z[e], upper]
            total = (faces[0] + faces[1]) + (faces[2] + faces[3]) + (faces[4] + faces[5])
            out.append((faces, take(0, e) + self.scale * total))
        return out

    def own_diagonal(self, x, y, rows):
        return [d for _, d in self.faces(self.row(x, y), rows)]

    def build(self, first_x, count, first_y, rows, source=None):
        n = self.halves

        def body(x):
            at = self.row(x, first_y)
            stores = []
            for e, (faces, diagonal) in enumerate(self.faces(at, rows)):
                inverse = 1.0 / diagonal
                low, _ = z_ends((rows, LANES), self.number, e)
                if low is not None:
                    faces[4] = jnp.where(low, 0.0, faces[4])
                scaled = self.scale * inverse
                for c in range(6):
                    stores.append((self.coef, (c * n + e, pl.ds(at, rows)), faces[c] * scaled))
                stores.append((self.diag, (e, pl.ds(at, rows)), diagonal))
                if source is not None:
                    ref, base = source
                    stores.append((self.rhs, (e, pl.ds(at, rows)), ref[base + e, pl.ds(at, rows), :] * inverse))
            return stores

        plane_loop(first_x, count, body)

    def stencil(self, src, at, rows):
        n = self.halves
        ref, base = src
        take = lambda e, shift=0: ref[base + e, pl.ds(at + shift, rows), :]
        centre = [take(e) for e in range(n)]
        below, above = z_neighbours(centre, self.number)
        out = []
        for e in range(n):
            c = lambda k: self.coef[k * n + e, pl.ds(at, rows), :]
            t_x = c(0) * take(e, -self.pitch) + c(1) * take(e, self.pitch)
            t_y = c(2) * take(e, -1) + c(3) * take(e, 1)
            t_z = c(4) * below[e] + c(5) * above[e]
            out.append((t_x + t_y) + t_z)
        return out, centre

    def residual(self, src, at, rows):
        sums, centre = self.stencil(src, at, rows)
        return [(self.rhs[e, pl.ds(at, rows), :] - centre[e]) + sums[e] for e in range(self.halves)], centre

    def advance(self, pair, src, dst, old, new, total, first_x, count, first_y, rows, lead=1.0, lift=False, emit=None):
        def body(x):
            at = self.row(x, first_y)
            here = pl.ds(at, rows)
            sums, centre = self.stencil((src, 0), at, rows)
            stores, news = [], []
            for e in range(self.halves):
                change = centre[e] - sums[e]
                rest = old[e, here, :] - (change if lead == 1.0 else lead * change)
                step = pair[1] * rest
                if pair[0] != 0.0:
                    step = (pair[0] * lead) * centre[e] + step
                iterate = total[e, here, :] + step
                if lift:
                    iterate = iterate + centre[e]
                news.append(iterate)
                if emit is None:
                    stores += [(new, (e, here), rest), (dst, (e, here), step), (total, (e, here), iterate)]
            return stores if emit is None else emit(x, news)

        plane_loop(first_x, count, body)

    def sweep(self, pair, src, dst, first_x, count, first_y, rows, last=False, emit=None):
        def body(x):
            at = self.row(x, first_y)
            steps, centre = self.residual(src, at, rows)
            news, stores = [], []
            for e in range(self.halves):
                new = pair[1] * steps[e]
                if pair[0] != 0.0:
                    new = pair[0] * self.update[e, pl.ds(at, rows), :] + new
                if not last:
                    stores.append((self.update, (e, pl.ds(at, rows)), new))
                news.append(centre[e] + new)
            if emit is not None:
                return emit(x, news)
            ref, base = dst
            return stores + [(ref, (base + e, pl.ds(at, rows)), news[e]) for e in range(self.halves)]

        plane_loop(first_x, count, body)

    def first_from_zero(self, pair, dst, first_x, count, first_y, rows):
        def body(x):
            at = self.row(x, first_y)
            ref, base = dst
            stores = []
            for e in range(self.halves):
                new = pair[1] * self.rhs[e, pl.ds(at, rows), :]
                stores.append((self.update, (e, pl.ds(at, rows)), new))
                stores.append((ref, (base + e, pl.ds(at, rows)), new))
            return stores

        plane_loop(first_x, count, body)


def corner_pieces(sx, sy, depth):
    pieces = []
    for dx in range(1, depth):
        rows = depth - dx
        pieces.append((NX0 - dx if sx > 0 else dx - 1, NY0 - rows if sy > 0 else 0, rows))
    return pieces


def side_plane(sx, dx):
    return NX0 - dx if sx > 0 else dx - 1


def side_row(sy, dy):
    return NY0 - dy if sy > 0 else dy - 1


def near_plan(fields, planes, depth, extra=(0, 0)):
    sizes = [fields * planes * NY0 + extra[0], fields * planes * NY0 + extra[1]]
    sizes += [fields * depth * NX0] * 2 + [-(-fields * corner_rows(depth) // 8) * 8] * 4
    starts = [sum(sizes[:n]) for n in range(8)]
    return list(zip(starts, sizes)), sum(sizes)


def corner_rows(depth):
    return depth * (depth - 1) // 2


def mid_corner(sx, sy):
    for dx in range(1, NX1 + 1):
        rows = 7 - dx
        yield (NX1 - dx if sx > 0 else dx - 1), (NY1 - rows if sy > 0 else 0), rows


def mid_plan(fields):
    sizes = [fields * NX1 * NY1] * 4 + [-(-fields * 18 // 8) * 8] * 4
    return list(zip([sum(sizes[:n]) for n in range(8)], sizes)), sum(sizes)


def wide_pieces(sx, sy):
    for dx in range(2):
        x = NX1 - 1 - dx if sx > 0 else dx
        if sy == 0:
            yield x, 0, NY1
        else:
            yield x, (NY1 - 2 if sy > 0 else 0), 2


WIDE_SIZES = [96, 96, 24, 24, 24, 24]
WIDE_STARTS = [sum(WIDE_SIZES[:n]) for n in range(6)]
FIRST, RAW, FINE_REST, LOW_LINE, MID_COEF, MID_RHS, LOW_COEF, LOW_RHS, MID_ITER, MID_WIDE, FINE_BACK = range(11)
PLAN_M4, SIZE_M4 = mid_plan(4)
PLAN_M1, SIZE_M1 = mid_plan(1)
PLAN_F, SIZE_F = [(0, 64), (64, 32), (96, 32), (128, 16)], 144
PLAN_A, SIZE_A = near_plan(8, 3, DEPTH, (32, 0))
PLAN_T, SIZE_T = near_plan(2, 4, DEPTH)
PLAN_U, SIZE_U = near_plan(2, 3, 3)


def kernel(counts, *refs):
    inputs, out_hbm = refs[:6], refs[6]
    (nat, fine, fine_a, fine_b, coef0, diag0, rhs0, rest_a, rest_b, total0, rest0,
     raw1, coef1, diag1, rhs1, upd1, it1_a, it1_b, rest1,
     raw2, coef2, diag2, rhs2, upd2, it2_a, it2_b,
     sfi, rfi, sra, rra, sta, rta, smc, cmc, rmc, sg1, cg1, rg1, sx1, cx1, rx1, r2l, r2c, sg2, rg2, siu, riu, swi, rwi, out_v,
     in_sem, out_sem, sent, got) = refs[7:]
    count_x, count_y = counts
    me_x, me_y = lax.axis_index("gx"), lax.axis_index("gy")

    def device(offset):
        return (lax.rem(me_x + offset[0] + count_x, count_x), lax.rem(me_y + offset[1] + count_y, count_y))

    loads = [pltpu.make_async_copy(inputs[k], nat.at[k], in_sem.at[k]) for k in range(6)]
    for load in loads:
        load.start()
    barrier = pltpu.get_barrier_semaphore()
    for offset in NEAR + [o for o in BALL if o not in NEAR]:
        pl.semaphore_signal(barrier, inc=1, device_id=device(offset), device_id_type=MESH)

    def send(group, src, dst, offset):
        pltpu.make_async_remote_copy(
            src_ref=src, dst_ref=dst, send_sem=sent.at[group], recv_sem=got.at[group],
            device_id=device(offset), device_id_type=MESH,
        ).start()

    def arrived(group, landing):
        pltpu.make_async_copy(landing, landing, got.at[group]).wait()

    def departed(group, landing):
        pltpu.make_async_copy(landing, landing, sent.at[group]).wait()

    level0 = Level(0, 2, row0, YP0, fine, coef0, diag0, rhs0, None)
    level1 = Level(1, 1, row1, YP1, raw1, coef1, diag1, rhs1, upd1)
    level2 = Level(2, 1, row2, YP2, raw2, coef2, diag2, rhs2, upd2)

    at = lanes((NY0, LANES))
    cell = 4 * (at % HALF) + 2 * (at // HALF)
    from_first = (at % HALF) < HALF // 2
    picks = [(cell + e) % LANES for e in range(2)]

    def permute(k):
        def body(x):
            first = nat[k, x, :, 0:LANES]
            second = nat[k, x, :, LANES : 2 * LANES]
            stores = []
            for e in range(2):
                low = jnp.take_along_axis(first, picks[e], axis=1, mode="promise_in_bounds")
                high = jnp.take_along_axis(second, picks[e], axis=1, mode="promise_in_bounds")
                stores.append((fine, (2 * k + e, pl.ds(row0(x, 0), NY0)), jnp.where(from_first, low, high)))
            return stores

        plane_loop(0, NX0, body)

    def near_rows(i, plan, planes, depth):
        for n, (sx, sy) in enumerate(NEAR):
            shift = -(sx * NX0 * YP0 + sy * NY0)
            start = plan[n][0]
            if n < 2:
                for dx in range(1, planes + 1):
                    at_buffer = pl.multiple_of(start + (i * planes + dx - 1) * NY0, 8)
                    yield row0(side_plane(sx, dx), 0), NY0, None, shift, at_buffer
            elif n < 4:
                for dy in range(1, depth + 1):
                    at_buffer = pl.multiple_of(start + (i * depth + dy - 1) * NX0, 8)
                    yield row0(0, side_row(sy, dy)), NX0, YP0, shift, at_buffer
            else:
                at_buffer = start + i * corner_rows(depth)
                for x, y, rows in corner_pieces(sx, sy, depth):
                    yield row0(x, y), rows, None, shift, at_buffer
                    at_buffer = at_buffer + rows

    def pack(field, first, count, out, plan, planes, depth):
        def body(i, carry):
            values = []
            for row, rows, stride, _, to in near_rows(i, plan, planes, depth):
                values.append((to, rows, field[first + i, pl.ds(row, rows, stride=stride), :]))
            for to, rows, value in values:
                out[pl.ds(to, rows), :] = value
            return carry

        lax.fori_loop(0, count, body, 0)

    def unpack(field, first, count, landing, plan, planes, depth):
        def body(i, carry):
            values = []
            for row, rows, stride, shift, at_buffer in near_rows(i, plan, planes, depth):
                values.append((pl.ds(row + shift, rows, stride=stride), landing[pl.ds(at_buffer, rows), :]))
            for to, value in values:
                field[first + i, to, :] = value
            return carry

        lax.fori_loop(0, count, body, 0)

    def extra_pieces(k, plan, base, sides):
        for side in sides:
            sx = NEAR[side][0]
            for e in range(2):
                row = row0(side_plane(sx, DEPTH), 0)
                yield k + e, row, row - sx * NX0 * YP0, plan[side][0] + base + e * NY0

    def extra_out(field, k, out, plan, base, sides):
        for f, row, _, to in extra_pieces(k, plan, base, sides):
            out[pl.ds(to, NY0), :] = field[f, pl.ds(row, NY0), :]

    def extra_in(field, k, landing, plan, base, sides):
        for f, _, row, at_buffer in extra_pieces(k, plan, base, sides):
            field[f, pl.ds(row, NY0), :] = landing[pl.ds(at_buffer, NY0), :]

    def near_sends(group, out, landing, plan):
        for (start, rows), offset in zip(plan, NEAR):
            cut = pl.ds(start, rows)
            send(group, out.at[cut], landing.at[cut], offset)

    def first_pieces():
        for n, (sx, sy) in enumerate(NEAR[:4]):
            fields = (10, 11) + ((2, 3) if n == 0 else (4, 5) if n == 2 else ())
            for i, k in enumerate(fields):
                shift = -(sx * NX0 * YP0 + sy * NY0)
                if n < 2:
                    yield k, row0(side_plane(sx, 1), 0), NY0, None, shift, PLAN_F[n][0] + i * NY0
                else:
                    yield k, row0(0, side_row(sy, 1)), NX0, YP0, shift, PLAN_F[n][0] + i * NX0

    weights = chebyshev_weights(SWEEPS)
    for k in (5, 1, 2):
        loads[k].wait()
        permute(k)
    for k, row, rows, stride, _, to in first_pieces():
        sfi[pl.ds(to, rows), :] = fine[k, pl.ds(row, rows, stride=stride), :]
    pl.semaphore_wait(barrier, len(BALL))
    near_sends(FIRST, sfi, rfi, PLAN_F)
    for k in (0, 3):
        loads[k].wait()
        permute(k)
    pack(fine, 0, 8, sra, PLAN_A, 3, DEPTH)
    extra_out(fine, 2, sra, PLAN_A, 384, (0,))
    near_sends(RAW, sra, rra, PLAN_A)
    loads[4].wait()
    permute(4)

    def children(k, e, x, y_step):
        return fine[2 * k + e, pl.ds(row0(x, y_step), NY1, stride=2), :]

    def coarsen1(big):
        to = pl.ds(row1(big, 0), NY1)
        x = 2 * big
        absorb = sum(children(0, e, x + p, q) for e in range(2) for p in range(2) for q in range(2)) * 0.125
        face_x = sum(children(1, e, x, q) for e in range(2) for q in range(2)) * 0.25
        face_y = sum(children(2, e, x + p, 0) for e in range(2) for p in range(2)) * 0.25
        face_z = sum(children(3, 0, x + p, q) for p in range(2) for q in range(2)) * 0.25
        for k, value in enumerate((absorb, face_x, face_y, face_z)):
            raw1[k, to, :] = value
            smc[pl.ds(k * 32 + big * NY1, NY1), :] = value

    for big in range(NX1):
        coarsen1(big)

    def mid_sends(group, own, corner, landing, plan, fields):
        for n, offset in enumerate(NEAR[4:]):
            to = 0
            for k in range(fields):
                for x, y, rows in mid_corner(*offset):
                    corner[n, pl.ds(to, rows), :] = own[pl.ds(k * 32 + x * NY1 + y, rows), :]
                    to += rows
        for n, ((start, rows), offset) in enumerate(zip(plan, NEAR)):
            send(group, own if n < 4 else corner.at[n - 4], landing.at[pl.ds(start, rows)], offset)

    def mid_unpack(landing, plan, fields, store):
        for n, ((start, _), (sx, sy)) in enumerate(zip(plan, NEAR)):
            for k in range(fields):
                pieces = mid_corner(sx, sy) if n >= 4 else ((x, 0, NY1) for x in range(NX1))
                for x, y, rows in pieces:
                    store(k, pl.ds(row1(x - sx * NX1, y - sy * NY1), rows), landing[pl.ds(start, rows), :])
                    start += rows

    def both(v):
        return v + pltpu.roll(v, HALF, 1)

    for big in range(NX2):
        grand = lambda k, x, q: raw1[k, pl.ds(row1(x, q), NY2, stride=2), :]
        x = 2 * big
        absorb = both(sum(grand(0, x + p, q) for p in range(2) for q in range(2))) * 0.125
        face_x = both(sum(grand(1, x, q) for q in range(2))) * 0.25
        face_y = both(sum(grand(2, x + p, 0) for p in range(2))) * 0.25
        face_z = sum(grand(3, x + p, q) for p in range(2) for q in range(2)) * 0.25
        low = lanes((NY2, LANES)) < HALF
        face_z = jnp.where(low, face_z, pltpu.roll(face_z, HALF, 1))
        for k, value in enumerate((absorb, face_x, face_y, face_z)):
            raw2[k, pl.ds(row2(big, 0), NY2), :] = value
        r2l[0, pl.ds(big * NY2, NY2), :] = jnp.where(low, absorb, face_x)
        r2l[0, pl.ds(8 + big * NY2, NY2), :] = jnp.where(low, face_y, face_z)

    def ball_sends(group, src, landing):
        for n, offset in enumerate(BALL):
            send(group, src, landing.at[n], offset)

    arrived(FIRST, rfi)
    for k, row, rows, stride, shift, at_buffer in first_pieces():
        fine[k, pl.ds(row + shift, rows, stride=stride), :] = rfi[pl.ds(at_buffer, rows), :]
    level0.build(0, NX0, 0, NY0, (fine, 8))

    def first_sweep(x):
        here = pl.ds(row0(x, 0), NY0)
        steps, centre = level0.residual((fine, 10), row0(x, 0), NY0)
        stores = []
        for e in range(2):
            stores.append((rest_a, (e, here), steps[e]))
            stores.append((total0, (e, here), centre[e] + weights[0][1] * steps[e]))
        return stores

    plane_loop(0, NX0, first_sweep)
    pack(rest_a, 0, 2, sta, PLAN_T, 4, DEPTH)
    near_sends(FINE_REST, sta, rta, PLAN_T)
    for n, i in enumerate(LINE):
        send(LOW_LINE, r2l.at[0], r2l.at[n + 1], (i, 0))
    mid_sends(MID_COEF, smc, cmc, rmc, PLAN_M4, 4)

    face_x = sum(children(1, e, NX0, q) for e in range(2) for q in range(2)) * 0.25
    raw1[1, pl.ds(row1(NX1, 0), NY1), :] = face_x
    face_y = sum(fine[4 + e, pl.ds(row0(p, NY0), NX1, stride=2 * YP0), :] for e in range(2) for p in range(2)) * 0.25
    raw1[2, pl.ds(row1(0, NY1), NX1, stride=YP1), :] = face_y
    diag_own1 = [level1.own_diagonal(big, 0, NY1)[0] for big in range(NX1)]
    x = NX1
    grand = lambda k, x, y: raw1[k, pl.ds(row1(x, y), NY2, stride=2), :]
    raw2[1, pl.ds(row2(NX2, 0), NY2), :] = both(grand(1, x, 0) + grand(1, x, 1)) * 0.25
    for big in range(NX2):
        above = both(sum(grand(2, 2 * big + p, NY1) for p in range(2))) * 0.25
        raw2[2, pl.ds(row2(big, NY2), 1), :] = above[0:1]
    diag_own2 = [level2.own_diagonal(big, 0, NY2)[0] for big in range(NX2)]

    arrived(RAW, rra)
    unpack(fine, 0, 8, rra, PLAN_A, 3, DEPTH)
    extra_in(fine, 2, rra, PLAN_A, 384, (0,))
    level0.build(-3, 14, -4, 24)
    arrived(FINE_REST, rta)
    unpack(rest_a, 0, 2, rta, PLAN_T, 4, DEPTH)
    level0.advance(weights[1], rest_a, fine_a, rest_a, rest_b, total0, -3, 14, -4, 24, lead=weights[0][1])
    level0.advance(weights[2], fine_a, fine_b, rest_b, rest_b, total0, -2, 12, -4, 24)
    level0.advance(weights[3], fine_b, fine_a, rest_b, rest_b, total0, -1, 10, -4, 24)

    def rest_fine(x):
        here = pl.ds(row0(x, 0), NY0)
        sums, centre = level0.stencil((fine_a, 0), row0(x, 0), NY0)
        stores = []
        for e in range(2):
            rest = rest_b[e, here, :] - (centre[e] - sums[e])
            stores.append((rest_b, (e, here), rest))
            stores.append((rest0, (e, pl.ds(x * NY0, NY0)), rest * diag0[e, here, :]))
        return stores

    plane_loop(0, NX0, rest_fine)
    for big in range(NX1):
        total = sum(
            rest0[e, pl.ds((2 * big + p) * NY0 + q, NY1, stride=2), :]
            for e in range(2) for p in range(2) for q in range(2)
        )
        value = total * 0.125 / diag_own1[big]
        rhs1[0, pl.ds(row1(big, 0), NY1), :] = value
        sg1[pl.ds(big * NY1, NY1), :] = value

    mid_sends(MID_RHS, sg1, cg1, rg1, PLAN_M1, 1)
    arrived(LOW_LINE, r2l.at[pl.ds(1, 10)])
    start = 0
    for j, slots in COLUMNS:
        send(LOW_COEF, r2l.at[pl.ds(0, slots)], r2c.at[pl.ds(start, slots)], (0, j))
        start += slots

    arrived(MID_COEF, rmc)

    def store_raw(k, to, value):
        raw1[k, to, :] = value

    mid_unpack(rmc, PLAN_M4, 4, store_raw)
    level1.build(-4, 11, -8, 24)

    def store_rhs1(k, to, value):
        rhs1[0, to, :] = value

    arrived(MID_RHS, rg1)
    mid_unpack(rg1, PLAN_M1, 1, store_rhs1)
    level1.first_from_zero(weights[0], (it1_a, 0), -4, 12, -4, 16)
    level1.sweep(weights[1], (it1_a, 0), (it1_b, 0), -3, 10, -4, 16)
    level1.sweep(weights[2], (it1_b, 0), (it1_a, 0), -2, 8, -4, 16)
    level1.sweep(weights[3], (it1_a, 0), (it1_b, 0), -1, 6, -4, 16, last=True)

    def rest_mid(x):
        at_row = row1(x, 0)
        steps, centre = level1.residual((it1_b, 0), at_row, NY1)
        return [
            (rest1, (pl.ds(x * NY1, NY1),), steps[0] * diag1[0, pl.ds(at_row, NY1), :]),
            (sx1, (pl.ds(x * NY1, NY1),), centre[0]),
        ]

    plane_loop(0, NX1, rest_mid)
    rhs_own2 = []
    for big in range(NX2):
        total = sum(rest1[pl.ds((2 * big + p) * NY1 + q, NY2, stride=2), :] for p in range(2) for q in range(2))
        rhs_own2.append(both(total) * 0.125 / diag_own2[big])
        rhs2[0, pl.ds(row2(big, 0), NY2), :] = rhs_own2[big]
    sg2[...] = jnp.where(low, rhs_own2[0], rhs_own2[1])

    ball_sends(LOW_RHS, sg2, rg2)
    mid_sends(MID_ITER, sx1, cx1, rx1, PLAN_M1, 1)
    pack(rest_b, 0, 2, siu, PLAN_U, 3, 3)
    near_sends(FINE_BACK, siu, riu, PLAN_U)
    for n, offset in enumerate(WIDE):
        to = WIDE_STARTS[n]
        for k in range(6):
            own, base = ((smc, 32 * k), (sg1, 0), (sx1, 0))[max(k - 3, 0)]
            for x, y, rows in wide_pieces(*offset):
                swi[pl.ds(to, rows), :] = own[pl.ds(base + x * NY1 + y, rows), :]
                to += rows
        cut = pl.ds(WIDE_STARTS[n], WIDE_SIZES[n])
        send(MID_WIDE, swi.at[cut], rwi.at[cut], offset)

    arrived(LOW_COEF, r2c)
    low8 = lanes((8, LANES)) < HALF

    def two_fields(value):
        other = pltpu.roll(value, HALF, 1)
        return jnp.where(low8, value, other), jnp.where(low8, other, value)

    def low_unpack(ref, slot, i, j):
        for part in range(2):
            for k, full in enumerate(two_fields(ref[slot, pl.ds(8 * part, 8), :])):
                for p in range(NX2):
                    to = pl.ds(row2(p - 2 * i, -4 * j), NY2)
                    raw2[2 * part + k, to, :] = full[p * NY2 : (p + 1) * NY2]

    for n, i in enumerate(LINE):
        low_unpack(r2l, n + 1, i, 0)
    start = 0
    for j, slots in COLUMNS:
        for n, i in enumerate(([0] + LINE)[:slots]):
            low_unpack(r2c, start + n, i, j)
        start += slots
    level2.build(-9, 20, -10, 24)
    arrived(LOW_RHS, rg2)
    for n, (i, j) in enumerate(BALL):
        value = rg2[n]
        other = pltpu.roll(value, HALF, 1)
        rhs2[0, pl.ds(row2(-2 * i, -4 * j), NY2), :] = jnp.where(low, value, other)
        rhs2[0, pl.ds(row2(1 - 2 * i, -4 * j), NY2), :] = jnp.where(low, other, value)
    coarse = chebyshev_weights(COARSE_SWEEPS)
    level2.first_from_zero(coarse[0], (it2_a, 0), -10, 22, -10, 24)
    src, dst = it2_a, it2_b
    for sweep in range(1, COARSE_SWEEPS):
        reach = COARSE_SWEEPS - 1 - sweep
        first_y, rows = (-10, 24) if reach > 3 else (-6, 16)
        level2.sweep(coarse[sweep], (src, 0), (dst, 0), -3 - reach, 8 + 2 * reach, first_y, rows, last=reach == 0)
        src, dst = dst, src

    def store_it1(k, to, value):
        it1_b[0, to, :] = value

    arrived(MID_ITER, rx1)
    mid_unpack(rx1, PLAN_M1, 1, store_it1)
    arrived(MID_WIDE, rwi)
    for n, (sx, sy) in enumerate(WIDE):
        start = WIDE_STARTS[n]
        for k in range(6):
            ref, field = (raw1, k) if k < 4 else ((rhs1, 0) if k == 4 else (it1_b, 0))
            for x, y, rows in wide_pieces(sx, sy):
                ref[field, pl.ds(row1(x - sx * NX1, y - sy * NY1), rows), :] = rwi[pl.ds(start, rows), :]
                start += rows
    level1.build(-5, 1, -8, 24)
    level1.build(7, 2, -8, 24)

    def lift1(big):
        stores = []
        for y in (-3, -1):
            value = src[0, pl.ds(row2(big, y), 8), :]
            for p in range(2):
                for q in range(2):
                    to = pl.ds(row1(2 * big + p, 2 * y + q), 8, stride=2)
                    stores.append((it1_a, (0, to), it1_b[0, to, :] + value))
        return stores

    plane_loop(-3, 8, lift1)
    level1.sweep(weights[0], (it1_a, 0), (it1_b, 0), -5, 14, -8, 24)
    level1.sweep(weights[1], (it1_b, 0), (it1_a, 0), -4, 12, -8, 24)
    level1.sweep(weights[2], (it1_a, 0), (it1_b, 0), -3, 10, -4, 16)
    level1.sweep(weights[3], (it1_b, 0), (it1_a, 0), -2, 8, -4, 16, last=True)

    arrived(FINE_BACK, riu)
    unpack(rest_b, 0, 2, riu, PLAN_U, 3, 3)

    def lift0(big):
        stores = []
        for y in (-2, 2):
            value = it1_a[0, pl.ds(row1(big, y), 8), :]
            for e in range(2):
                for p in range(2):
                    for q in range(2):
                        to = pl.ds(row0(2 * big + p, 2 * y + q), 8, stride=2)
                        stores.append((fine_b, (e, to), value))
        return stores

    plane_loop(-2, 8, lift0)
    level0.advance((0.0, weights[0][1]), fine_b, fine_a, rest_b, rest_b, total0, -3, 14, -4, 24, lift=True)
    level0.advance(weights[1], fine_a, fine_b, rest_b, rest_b, total0, -2, 12, -4, 24)
    level0.advance(weights[2], fine_b, fine_a, rest_b, rest_b, total0, -1, 10, -4, 24)
    back = HALF * ((at // 2) % 2) + at // 4
    even = (at % 2) == 0

    def emit(x, news):
        stores = []
        for half in range(2):
            pick = back + 32 * half
            lower = jnp.take_along_axis(news[0], pick, axis=1, mode="promise_in_bounds")
            upper = jnp.take_along_axis(news[1], pick, axis=1, mode="promise_in_bounds")
            stores.append((out_v, (x, slice(None), slice(half * LANES, (half + 1) * LANES)), jnp.where(even, lower, upper)))
        return stores

    level0.advance(weights[3], fine_a, None, rest_b, None, total0, 0, 8, 0, NY0, emit=emit)
    store = pltpu.make_async_copy(out_v, out_hbm, out_sem.at[0])
    store.start()
    for group, landing in enumerate((rfi, rra, rta, r2l.at[pl.ds(1, 10)], rmc, rg1, r2c, rg2, rx1, rwi, riu)):
        departed(group, landing)
    store.wait()


def solution(mesh):
    counts = (mesh.shape["gx"], mesh.shape["gy"])

    def local(source, initial, absorption, beta_x, beta_y, beta_z):
        f32 = jnp.float32
        v = lambda *shape: pltpu.VMEM(shape, f32)
        scratch = [
            v(6, NX0, NY0, 256), v(12, ROWS0, LANES), v(2, ROWS0, LANES), v(2, ROWS0, LANES),
            v(12, ROWS0, LANES), v(2, ROWS0, LANES), v(2, ROWS0, LANES), v(2, ROWS0, LANES), v(2, ROWS0, LANES), v(2, ROWS0, LANES),
            v(2, 128, LANES),
            v(4, ROWS1, LANES), v(6, ROWS1, LANES), v(1, ROWS1, LANES), v(1, ROWS1, LANES), v(1, ROWS1, LANES),
            v(1, ROWS1, LANES), v(1, ROWS1, LANES), v(32, LANES),
            v(4, ROWS2, LANES), v(6, ROWS2, LANES), v(1, ROWS2, LANES), v(1, ROWS2, LANES), v(1, ROWS2, LANES),
            v(1, ROWS2, LANES), v(1, ROWS2, LANES),
            v(SIZE_F, LANES), v(SIZE_F, LANES), v(SIZE_A, LANES), v(SIZE_A, LANES), v(SIZE_T, LANES), v(SIZE_T, LANES),
            v(128, LANES), v(4, 72, LANES), v(SIZE_M4, LANES),
            v(32, LANES), v(4, 24, LANES), v(SIZE_M1, LANES), v(32, LANES), v(4, 24, LANES), v(SIZE_M1, LANES),
            v(11, 16, LANES), v(42, 16, LANES), v(NY2, LANES), v(len(BALL), NY2, LANES),
            v(SIZE_U, LANES), v(SIZE_U, LANES), v(288, LANES), v(288, LANES), v(NX0, NY0, 256),
            pltpu.SemaphoreType.DMA((6,)), pltpu.SemaphoreType.DMA((1,)),
            pltpu.SemaphoreType.DMA((11,)), pltpu.SemaphoreType.DMA((11,)),
        ]
        call = pl.pallas_call(
            lambda *refs: kernel(counts, *refs),
            out_shape=jax.ShapeDtypeStruct((NX0, NY0, 256), f32),
            in_specs=[pl.BlockSpec(memory_space=pl.ANY)] * 6,
            out_specs=pl.BlockSpec(memory_space=pl.ANY),
            scratch_shapes=scratch,
            compiler_params=pltpu.CompilerParams(
                collective_id=0, has_side_effects=True, vmem_limit_bytes=56 * 2**20
            ),
            name="vcycle",
        )
        return call(absorption, beta_x, beta_y, beta_z, source, initial)

    return jax.shard_map(
        local,
        mesh=mesh,
        in_specs=(P("gx", "gy", None),) * 6,
        out_specs=P("gx", "gy", None),
        check_vma=False,
    )
```

```python
import jax
import jax.numpy as jnp
from jax import lax
from jax.experimental import pallas as pl
from jax.experimental.pallas import tpu as pltpu
from jax.sharding import PartitionSpec as P

SWEEPS = 4
COARSE_SWEEPS = 8
LANES = 128
HALF = 64
GROUP = 8
MESH = pl.DeviceIdType.MESH

NX0, NY0, HX0, HY0, YP0 = 8, 16, 5, 5, 26
NX1, NY1, HX1, HY1, YP1 = 4, 8, 6, 9, 26
NX2, NY2, HX2, HY2, YP2 = 2, 4, 10, 12, 28
ROWS0 = 472
ROWS1 = 416
ROWS2 = 616

DEPTH = 4
NEAR = [(-1, 0), (1, 0), (0, -1), (0, 1), (-1, -1), (-1, 1), (1, -1), (1, 1)]
WIDE = [(-2, 0), (2, 0), (-2, -1), (-2, 1), (2, -1), (2, 1)]
LINE = [1, -1, 2, -2, 3, -3, 4, -4, 5, -5]
COLUMNS = [(-1, 11), (1, 11), (-2, 7), (2, 7), (-3, 3), (3, 3)]


def ball_offsets():
    offsets = []
    for i in range(-5, 6):
        for j in range(-3, 4):
            far_x = 2 * abs(i) - 1 if i else 0
            far_y = 4 * abs(j) - 3 if j else 0
            if (i, j) != (0, 0) and far_x + far_y <= (11 if i and j else 10):
                offsets.append((i, j))
    return offsets


BALL = ball_offsets()


def chebyshev_weights(sweeps):
    cheb_theta = 1.125
    cheb_delta = 0.875
    cheb_sigma = cheb_theta / cheb_delta
    rho_old = 1.0 / cheb_sigma
    weights = [(0.0, 1.0 / cheb_theta)]
    for sweep in range(1, sweeps):
        rho_new = 1.0 / (2.0 * cheb_sigma - rho_old)
        weights.append((rho_new * rho_old, 2.0 * rho_new / cheb_delta))
        rho_old = rho_new
    return weights


def row0(x, y):
    return (x + HX0) * YP0 + y + HY0


def row1(x, y):
    return (x + HX1) * YP1 + y + HY1


def row2(x, y):
    return (x + HX2) * YP2 + y + HY2


def lanes(shape):
    return lax.broadcasted_iota(jnp.int32, shape, len(shape) - 1)


def shift_down(v):
    return jnp.where(lanes(v.shape) < HALF, pltpu.roll(v, HALF + 1, 1), pltpu.roll(v, HALF, 1))


def shift_up(v):
    return jnp.where(lanes(v.shape) < HALF, pltpu.roll(v, HALF, 1), pltpu.roll(v, HALF - 1, 1))


def z_neighbours(values, level):
    if level == 0:
        return (shift_down(values[1]), values[0]), (values[1], shift_up(values[0]))
    if level == 1:
        return (shift_down(values[0]),), (shift_up(values[0]),)
    return (pltpu.roll(values[0], 1, 1),), (pltpu.roll(values[0], LANES - 1, 1),)


def z_ends(shape, level, half):
    at = lanes(shape)
    if level == 0:
        return (at == 0) if half == 0 else None, (at == LANES - 1) if half == 1 else None
    if level == 1:
        return at == 0, at == LANES - 1
    return (at % HALF) == 0, (at % HALF) == HALF - 1


def plane_loop(first, count, body, group=GROUP):
    def several(start, n):
        stores = []
        for i in range(n):
            stores += body(start + i)
        for ref, index, value in stores:
            ref[index] = value

    def step(i, carry):
        several(first + group * i, group)
        return carry

    if count // group > 1:
        lax.fori_loop(0, count // group, step, 0)
        done = count // group * group
    else:
        done = 0
    if done < count:
        several(first + done, count - done)


class Level:
    def __init__(self, number, halves, row, pitch, raw, coef, diag, rhs, update):
        self.number, self.halves, self.row, self.pitch = number, halves, row, pitch
        self.raw, self.coef, self.diag, self.rhs, self.update = raw, coef, diag, rhs, update
        self.scale = 0.25**number

    def faces(self, at, rows):
        n, raw = self.halves, self.raw
        take = lambda k, e, shift=0: raw[k * n + e, pl.ds(at + shift, rows), :]
        low_z = [take(3, e) for e in range(n)]
        _, high_z = z_neighbours(low_z, self.number)
        out = []
        for e in range(n):
            _, top = z_ends((rows, LANES), self.number, e)
            upper = high_z[e] if top is None else jnp.where(top, 0.0, high_z[e])
            faces = [take(1, e), take(1, e, self.pitch), take(2, e), take(2, e, 1), low_z[e], upper]
            total = (faces[0] + faces[1]) + (faces[2] + faces[3]) + (faces[4] + faces[5])
            out.append((faces, take(0, e) + self.scale * total))
        return out

    def own_diagonal(self, x, y, rows):
        return [d for _, d in self.faces(self.row(x, y), rows)]

    def build(self, first_x, count, first_y, rows, source=None):
        n = self.halves

        def body(x):
            at = self.row(x, first_y)
            stores = []
            for e, (faces, diagonal) in enumerate(self.faces(at, rows)):
                inverse = 1.0 / diagonal
                low, _ = z_ends((rows, LANES), self.number, e)
                if low is not None:
                    faces[4] = jnp.where(low, 0.0, faces[4])
                scaled = self.scale * inverse
                for c in range(6):
                    stores.append((self.coef, (c * n + e, pl.ds(at, rows)), faces[c] * scaled))
                stores.append((self.diag, (e, pl.ds(at, rows)), diagonal))
                if source is not None:
                    ref, base = source
                    stores.append((self.rhs, (e, pl.ds(at, rows)), ref[base + e, pl.ds(at, rows), :] * inverse))
            return stores

        plane_loop(first_x, count, body)

    def stencil(self, src, at, rows):
        n = self.halves
        ref, base = src
        take = lambda e, shift=0: ref[base + e, pl.ds(at + shift, rows), :]
        centre = [take(e) for e in range(n)]
        below, above = z_neighbours(centre, self.number)
        out = []
        for e in range(n):
            c = lambda k: self.coef[k * n + e, pl.ds(at, rows), :]
            t_x = c(0) * take(e, -self.pitch) + c(1) * take(e, self.pitch)
            t_y = c(2) * take(e, -1) + c(3) * take(e, 1)
            t_z = c(4) * below[e] + c(5) * above[e]
            out.append((t_x + t_y) + t_z)
        return out, centre

    def residual(self, src, at, rows):
        sums, centre = self.stencil(src, at, rows)
        return [(self.rhs[e, pl.ds(at, rows), :] - centre[e]) + sums[e] for e in range(self.halves)], centre

    def advance(self, pair, src, dst, old, new, total, first_x, count, first_y, rows, lead=1.0, lift=False, emit=None):
        def body(x):
            at = self.row(x, first_y)
            here = pl.ds(at, rows)
            sums, centre = self.stencil((src, 0), at, rows)
            stores, news = [], []
            for e in range(self.halves):
                change = centre[e] - sums[e]
                rest = old[e, here, :] - (change if lead == 1.0 else lead * change)
                step = pair[1] * rest
                if pair[0] != 0.0:
                    step = (pair[0] * lead) * centre[e] + step
                iterate = total[e, here, :] + step
                if lift:
                    iterate = iterate + centre[e]
                news.append(iterate)
                if emit is None:
                    stores += [(new, (e, here), rest), (dst, (e, here), step), (total, (e, here), iterate)]
            return stores if emit is None else emit(x, news)

        plane_loop(first_x, count, body)

    def sweep(self, pair, src, dst, first_x, count, first_y, rows, last=False, emit=None):
        def body(x):
            at = self.row(x, first_y)
            steps, centre = self.residual(src, at, rows)
            news, stores = [], []
            for e in range(self.halves):
                new = pair[1] * steps[e]
                if pair[0] != 0.0:
                    new = pair[0] * self.update[e, pl.ds(at, rows), :] + new
                if not last:
                    stores.append((self.update, (e, pl.ds(at, rows)), new))
                news.append(centre[e] + new)
            if emit is not None:
                return emit(x, news)
            ref, base = dst
            return stores + [(ref, (base + e, pl.ds(at, rows)), news[e]) for e in range(self.halves)]

        plane_loop(first_x, count, body)

    def first_from_zero(self, pair, dst, first_x, count, first_y, rows):
        def body(x):
            at = self.row(x, first_y)
            ref, base = dst
            stores = []
            for e in range(self.halves):
                new = pair[1] * self.rhs[e, pl.ds(at, rows), :]
                stores.append((self.update, (e, pl.ds(at, rows)), new))
                stores.append((ref, (base + e, pl.ds(at, rows)), new))
            return stores

        plane_loop(first_x, count, body)


def corner_pieces(sx, sy, depth):
    pieces = []
    for dx in range(1, depth):
        rows = depth - dx
        pieces.append((NX0 - dx if sx > 0 else dx - 1, NY0 - rows if sy > 0 else 0, rows))
    return pieces


def side_plane(sx, dx):
    return NX0 - dx if sx > 0 else dx - 1


def side_row(sy, dy):
    return NY0 - dy if sy > 0 else dy - 1


def near_plan(fields, planes, depth, extra=(0, 0)):
    sizes = [fields * planes * NY0 + extra[0], fields * planes * NY0 + extra[1]]
    sizes += [fields * depth * NX0] * 2 + [-(-fields * corner_rows(depth) // 8) * 8] * 4
    starts = [sum(sizes[:n]) for n in range(8)]
    return list(zip(starts, sizes)), sum(sizes)


def corner_rows(depth):
    return depth * (depth - 1) // 2


def mid_corner(sx, sy):
    for dx in range(1, NX1 + 1):
        rows = 7 - dx
        yield (NX1 - dx if sx > 0 else dx - 1), (NY1 - rows if sy > 0 else 0), rows


def mid_plan(fields):
    sizes = [fields * NX1 * NY1] * 4 + [-(-fields * 18 // 8) * 8] * 4
    return list(zip([sum(sizes[:n]) for n in range(8)], sizes)), sum(sizes)


def wide_pieces(sx, sy):
    for dx in range(2):
        x = NX1 - 1 - dx if sx > 0 else dx
        if sy == 0:
            yield x, 0, NY1
        else:
            yield x, (NY1 - 2 if sy > 0 else 0), 2


WIDE_SIZES = [96, 96, 24, 24, 24, 24]
WIDE_STARTS = [sum(WIDE_SIZES[:n]) for n in range(6)]
FIRST, RAW, FINE_REST, LOW_LINE, MID_COEF, MID_RHS, LOW_COEF, LOW_RHS, MID_ITER, MID_WIDE, FINE_BACK = range(11)
PLAN_M4, SIZE_M4 = mid_plan(4)
PLAN_M1, SIZE_M1 = mid_plan(1)
PLAN_F, SIZE_F = [(0, 64), (64, 32), (96, 32), (128, 16)], 144
PLAN_A, SIZE_A = near_plan(8, 3, DEPTH, (32, 0))
PLAN_T, SIZE_T = near_plan(2, 4, DEPTH)
PLAN_U, SIZE_U = near_plan(2, 3, 3)


def kernel(counts, *refs):
    inputs, out_hbm = refs[:6], refs[6]
    (nat, fine, fine_a, fine_b, coef0, diag0, rhs0, rest_a, rest_b, total0, rest0,
     raw1, coef1, diag1, rhs1, upd1, it1_a, it1_b, rest1,
     raw2, coef2, diag2, rhs2, upd2, it2_a, it2_b,
     sfi, rfi, sra, rra, sta, rta, smc, cmc, rmc, sg1, cg1, rg1, sx1, cx1, rx1, r2l, r2c, sg2, rg2, siu, riu, swi, rwi, out_v,
     in_sem, out_sem, sent, got) = refs[7:]
    count_x, count_y = counts
    me_x, me_y = lax.axis_index("gx"), lax.axis_index("gy")

    def device(offset):
        return (lax.rem(me_x + offset[0] + count_x, count_x), lax.rem(me_y + offset[1] + count_y, count_y))

    loads = [pltpu.make_async_copy(inputs[k], nat.at[k], in_sem.at[k]) for k in range(6)]
    for load in loads:
        load.start()
    barrier = pltpu.get_barrier_semaphore()
    for offset in NEAR + [o for o in BALL if o not in NEAR]:
        pl.semaphore_signal(barrier, inc=1, device_id=device(offset), device_id_type=MESH)

    def send(group, src, dst, offset):
        pltpu.make_async_remote_copy(
            src_ref=src, dst_ref=dst, send_sem=sent.at[group], recv_sem=got.at[group],
            device_id=device(offset), device_id_type=MESH,
        ).start()

    def arrived(group, landing):
        pltpu.make_async_copy(landing, landing, got.at[group]).wait()

    def departed(group, landing):
        pltpu.make_async_copy(landing, landing, sent.at[group]).wait()

    level0 = Level(0, 2, row0, YP0, fine, coef0, diag0, rhs0, None)
    level1 = Level(1, 1, row1, YP1, raw1, coef1, diag1, rhs1, upd1)
    level2 = Level(2, 1, row2, YP2, raw2, coef2, diag2, rhs2, upd2)

    at = lanes((NY0, LANES))
    cell = 4 * (at % HALF) + 2 * (at // HALF)
    from_first = (at % HALF) < HALF // 2
    picks = [(cell + e) % LANES for e in range(2)]

    def permute(k):
        def body(x):
            first = nat[k, x, :, 0:LANES]
            second = nat[k, x, :, LANES : 2 * LANES]
            stores = []
            for e in range(2):
                low = jnp.take_along_axis(first, picks[e], axis=1, mode="promise_in_bounds")
                high = jnp.take_along_axis(second, picks[e], axis=1, mode="promise_in_bounds")
                stores.append((fine, (2 * k + e, pl.ds(row0(x, 0), NY0)), jnp.where(from_first, low, high)))
            return stores

        plane_loop(0, NX0, body)

    def near_rows(i, plan, planes, depth):
        for n, (sx, sy) in enumerate(NEAR):
            shift = -(sx * NX0 * YP0 + sy * NY0)
            start = plan[n][0]
            if n < 2:
                for dx in range(1, planes + 1):
                    at_buffer = pl.multiple_of(start + (i * planes + dx - 1) * NY0, 8)
                    yield row0(side_plane(sx, dx), 0), NY0, None, shift, at_buffer
            elif n < 4:
                for dy in range(1, depth + 1):
                    at_buffer = pl.multiple_of(start + (i * depth + dy - 1) * NX0, 8)
                    yield row0(0, side_row(sy, dy)), NX0, YP0, shift, at_buffer
            else:
                at_buffer = start + i * corner_rows(depth)
                for x, y, rows in corner_pieces(sx, sy, depth):
                    yield row0(x, y), rows, None, shift, at_buffer
                    at_buffer = at_buffer + rows

    def pack(field, first, count, out, plan, planes, depth):
        def body(i, carry):
            values = []
            for row, rows, stride, _, to in near_rows(i, plan, planes, depth):
                values.append((to, rows, field[first + i, pl.ds(row, rows, stride=stride), :]))
            for to, rows, value in values:
                out[pl.ds(to, rows), :] = value
            return carry

        lax.fori_loop(0, count, body, 0)

    def unpack(field, first, count, landing, plan, planes, depth):
        def body(i, carry):
            values = []
            for row, rows, stride, shift, at_buffer in near_rows(i, plan, planes, depth):
                values.append((pl.ds(row + shift, rows, stride=stride), landing[pl.ds(at_buffer, rows), :]))
            for to, value in values:
                field[first + i, to, :] = value
            return carry

        lax.fori_loop(0, count, body, 0)

    def extra_pieces(k, plan, base, sides):
        for side in sides:
            sx = NEAR[side][0]
            for e in range(2):
                row = row0(side_plane(sx, DEPTH), 0)
                yield k + e, row, row - sx * NX0 * YP0, plan[side][0] + base + e * NY0

    def extra_out(field, k, out, plan, base, sides):
        for f, row, _, to in extra_pieces(k, plan, base, sides):
            out[pl.ds(to, NY0), :] = field[f, pl.ds(row, NY0), :]

    def extra_in(field, k, landing, plan, base, sides):
        for f, _, row, at_buffer in extra_pieces(k, plan, base, sides):
            field[f, pl.ds(row, NY0), :] = landing[pl.ds(at_buffer, NY0), :]

    def near_sends(group, out, landing, plan):
        for (start, rows), offset in zip(plan, NEAR):
            cut = pl.ds(start, rows)
            send(group, out.at[cut], landing.at[cut], offset)

    def first_pieces():
        for n, (sx, sy) in enumerate(NEAR[:4]):
            fields = (10, 11) + ((2, 3) if n == 0 else (4, 5) if n == 2 else ())
            for i, k in enumerate(fields):
                shift = -(sx * NX0 * YP0 + sy * NY0)
                if n < 2:
                    yield k, row0(side_plane(sx, 1), 0), NY0, None, shift, PLAN_F[n][0] + i * NY0
                else:
                    yield k, row0(0, side_row(sy, 1)), NX0, YP0, shift, PLAN_F[n][0] + i * NX0

    weights = chebyshev_weights(SWEEPS)
    for k in (5, 1, 2):
        loads[k].wait()
        permute(k)
    for k, row, rows, stride, _, to in first_pieces():
        sfi[pl.ds(to, rows), :] = fine[k, pl.ds(row, rows, stride=stride), :]
    pl.semaphore_wait(barrier, len(BALL))
    near_sends(FIRST, sfi, rfi, PLAN_F)
    for k in (0, 3):
        loads[k].wait()
        permute(k)
    pack(fine, 0, 8, sra, PLAN_A, 3, DEPTH)
    extra_out(fine, 2, sra, PLAN_A, 384, (0,))
    near_sends(RAW, sra, rra, PLAN_A)
    loads[4].wait()
    permute(4)

    def children(k, e, x, y_step):
        return fine[2 * k + e, pl.ds(row0(x, y_step), NY1, stride=2), :]

    def coarsen1(big):
        to = pl.ds(row1(big, 0), NY1)
        x = 2 * big
        absorb = sum(children(0, e, x + p, q) for e in range(2) for p in range(2) for q in range(2)) * 0.125
        face_x = sum(children(1, e, x, q) for e in range(2) for q in range(2)) * 0.25
        face_y = sum(children(2, e, x + p, 0) for e in range(2) for p in range(2)) * 0.25
        face_z = sum(children(3, 0, x + p, q) for p in range(2) for q in range(2)) * 0.25
        for k, value in enumerate((absorb, face_x, face_y, face_z)):
            raw1[k, to, :] = value
            smc[pl.ds(k * 32 + big * NY1, NY1), :] = value

    for big in range(NX1):
        coarsen1(big)

    def mid_sends(group, own, corner, landing, plan, fields):
        for n, offset in enumerate(NEAR[4:]):
            to = 0
            for k in range(fields):
                for x, y, rows in mid_corner(*offset):
                    corner[n, pl.ds(to, rows), :] = own[pl.ds(k * 32 + x * NY1 + y, rows), :]
                    to += rows
        for n, ((start, rows), offset) in enumerate(zip(plan, NEAR)):
            send(group, own if n < 4 else corner.at[n - 4], landing.at[pl.ds(start, rows)], offset)

    def mid_unpack(landing, plan, fields, store):
        for n, ((start, _), (sx, sy)) in enumerate(zip(plan, NEAR)):
            for k in range(fields):
                pieces = mid_corner(sx, sy) if n >= 4 else ((x, 0, NY1) for x in range(NX1))
                for x, y, rows in pieces:
                    store(k, pl.ds(row1(x - sx * NX1, y - sy * NY1), rows), landing[pl.ds(start, rows), :])
                    start += rows

    def both(v):
        return v + pltpu.roll(v, HALF, 1)

    for big in range(NX2):
        grand = lambda k, x, q: raw1[k, pl.ds(row1(x, q), NY2, stride=2), :]
        x = 2 * big
        absorb = both(sum(grand(0, x + p, q) for p in range(2) for q in range(2))) * 0.125
        face_x = both(sum(grand(1, x, q) for q in range(2))) * 0.25
        face_y = both(sum(grand(2, x + p, 0) for p in range(2))) * 0.25
        face_z = sum(grand(3, x + p, q) for p in range(2) for q in range(2)) * 0.25
        low = lanes((NY2, LANES)) < HALF
        face_z = jnp.where(low, face_z, pltpu.roll(face_z, HALF, 1))
        for k, value in enumerate((absorb, face_x, face_y, face_z)):
            raw2[k, pl.ds(row2(big, 0), NY2), :] = value
        r2l[0, pl.ds(big * NY2, NY2), :] = jnp.where(low, absorb, face_x)
        r2l[0, pl.ds(8 + big * NY2, NY2), :] = jnp.where(low, face_y, face_z)

    def ball_sends(group, src, landing):
        for n, offset in enumerate(BALL):
            send(group, src, landing.at[n], offset)

    arrived(FIRST, rfi)
    for k, row, rows, stride, shift, at_buffer in first_pieces():
        fine[k, pl.ds(row + shift, rows, stride=stride), :] = rfi[pl.ds(at_buffer, rows), :]
    level0.build(0, NX0, 0, NY0, (fine, 8))

    def first_sweep(x):
        here = pl.ds(row0(x, 0), NY0)
        steps, centre = level0.residual((fine, 10), row0(x, 0), NY0)
        stores = []
        for e in range(2):
            stores.append((rest_a, (e, here), steps[e]))
            stores.append((total0, (e, here), centre[e] + weights[0][1] * steps[e]))
        return stores

    plane_loop(0, NX0, first_sweep)
    pack(rest_a, 0, 2, sta, PLAN_T, 4, DEPTH)
    near_sends(FINE_REST, sta, rta, PLAN_T)
    for n, i in enumerate(LINE):
        send(LOW_LINE, r2l.at[0], r2l.at[n + 1], (i, 0))
    mid_sends(MID_COEF, smc, cmc, rmc, PLAN_M4, 4)

    face_x = sum(children(1, e, NX0, q) for e in range(2) for q in range(2)) * 0.25
    raw1[1, pl.ds(row1(NX1, 0), NY1), :] = face_x
    face_y = sum(fine[4 + e, pl.ds(row0(p, NY0), NX1, stride=2 * YP0), :] for e in range(2) for p in range(2)) * 0.25
    raw1[2, pl.ds(row1(0, NY1), NX1, stride=YP1), :] = face_y
    diag_own1 = [level1.own_diagonal(big, 0, NY1)[0] for big in range(NX1)]
    x = NX1
    grand = lambda k, x, y: raw1[k, pl.ds(row1(x, y), NY2, stride=2), :]
    raw2[1, pl.ds(row2(NX2, 0), NY2), :] = both(grand(1, x, 0) + grand(1, x, 1)) * 0.25
    for big in range(NX2):
        above = both(sum(grand(2, 2 * big + p, NY1) for p in range(2))) * 0.25
        raw2[2, pl.ds(row2(big, NY2), 1), :] = above[0:1]
    diag_own2 = [level2.own_diagonal(big, 0, NY2)[0] for big in range(NX2)]

    arrived(RAW, rra)
    unpack(fine, 0, 8, rra, PLAN_A, 3, DEPTH)
    extra_in(fine, 2, rra, PLAN_A, 384, (0,))
    level0.build(-3, 14, -4, 24)
    arrived(FINE_REST, rta)
    unpack(rest_a, 0, 2, rta, PLAN_T, 4, DEPTH)
    level0.advance(weights[1], rest_a, fine_a, rest_a, rest_b, total0, -3, 14, -4, 24, lead=weights[0][1])
    level0.advance(weights[2], fine_a, fine_b, rest_b, rest_b, total0, -2, 12, -4, 24)
    level0.advance(weights[3], fine_b, fine_a, rest_b, rest_b, total0, -1, 10, -4, 24)

    def rest_fine(x):
        here = pl.ds(row0(x, 0), NY0)
        sums, centre = level0.stencil((fine_a, 0), row0(x, 0), NY0)
        stores = []
        for e in range(2):
            rest = rest_b[e, here, :] - (centre[e] - sums[e])
            stores.append((rest_b, (e, here), rest))
            stores.append((rest0, (e, pl.ds(x * NY0, NY0)), rest * diag0[e, here, :]))
        return stores

    plane_loop(0, NX0, rest_fine)
    for big in range(NX1):
        total = sum(
            rest0[e, pl.ds((2 * big + p) * NY0 + q, NY1, stride=2), :]
            for e in range(2) for p in range(2) for q in range(2)
        )
        value = total * 0.125 / diag_own1[big]
        rhs1[0, pl.ds(row1(big, 0), NY1), :] = value
        sg1[pl.ds(big * NY1, NY1), :] = value

    mid_sends(MID_RHS, sg1, cg1, rg1, PLAN_M1, 1)
    arrived(LOW_LINE, r2l.at[pl.ds(1, 10)])
    start = 0
    for j, slots in COLUMNS:
        send(LOW_COEF, r2l.at[pl.ds(0, slots)], r2c.at[pl.ds(start, slots)], (0, j))
        start += slots

    pack(rest_b, 0, 2, siu, PLAN_U, 3, 3)
    near_sends(FINE_BACK, siu, riu, PLAN_U)
    arrived(MID_COEF, rmc)

    def store_raw(k, to, value):
        raw1[k, to, :] = value

    mid_unpack(rmc, PLAN_M4, 4, store_raw)
    level1.build(-4, 11, -8, 24)

    def store_rhs1(k, to, value):
        rhs1[0, to, :] = value

    arrived(MID_RHS, rg1)
    mid_unpack(rg1, PLAN_M1, 1, store_rhs1)
    level1.first_from_zero(weights[0], (it1_a, 0), -4, 12, -4, 16)
    level1.sweep(weights[1], (it1_a, 0), (it1_b, 0), -3, 10, -4, 16)
    level1.sweep(weights[2], (it1_b, 0), (it1_a, 0), -2, 8, -4, 16)
    level1.sweep(weights[3], (it1_a, 0), (it1_b, 0), -1, 6, -4, 16, last=True)

    def rest_mid(x):
        at_row = row1(x, 0)
        steps, centre = level1.residual((it1_b, 0), at_row, NY1)
        return [
            (rest1, (pl.ds(x * NY1, NY1),), steps[0] * diag1[0, pl.ds(at_row, NY1), :]),
            (sx1, (pl.ds(x * NY1, NY1),), centre[0]),
        ]

    plane_loop(0, NX1, rest_mid)
    rhs_own2 = []
    for big in range(NX2):
        total = sum(rest1[pl.ds((2 * big + p) * NY1 + q, NY2, stride=2), :] for p in range(2) for q in range(2))
        rhs_own2.append(both(total) * 0.125 / diag_own2[big])
        rhs2[0, pl.ds(row2(big, 0), NY2), :] = rhs_own2[big]
    sg2[...] = jnp.where(low, rhs_own2[0], rhs_own2[1])

    ball_sends(LOW_RHS, sg2, rg2)
    mid_sends(MID_ITER, sx1, cx1, rx1, PLAN_M1, 1)
    for n, offset in enumerate(WIDE):
        to = WIDE_STARTS[n]
        for k in range(6):
            own, base = ((smc, 32 * k), (sg1, 0), (sx1, 0))[max(k - 3, 0)]
            for x, y, rows in wide_pieces(*offset):
                swi[pl.ds(to, rows), :] = own[pl.ds(base + x * NY1 + y, rows), :]
                to += rows
        cut = pl.ds(WIDE_STARTS[n], WIDE_SIZES[n])
        send(MID_WIDE, swi.at[cut], rwi.at[cut], offset)

    arrived(LOW_COEF, r2c)
    low8 = lanes((8, LANES)) < HALF

    def two_fields(value):
        other = pltpu.roll(value, HALF, 1)
        return jnp.where(low8, value, other), jnp.where(low8, other, value)

    def low_unpack(ref, slot, i, j):
        for part in range(2):
            for k, full in enumerate(two_fields(ref[slot, pl.ds(8 * part, 8), :])):
                for p in range(NX2):
                    to = pl.ds(row2(p - 2 * i, -4 * j), NY2)
                    raw2[2 * part + k, to, :] = full[p * NY2 : (p + 1) * NY2]

    for n, i in enumerate(LINE):
        low_unpack(r2l, n + 1, i, 0)
    start = 0
    for j, slots in COLUMNS:
        for n, i in enumerate(([0] + LINE)[:slots]):
            low_unpack(r2c, start + n, i, j)
        start += slots
    level2.build(-9, 20, -10, 24)
    arrived(LOW_RHS, rg2)
    for n, (i, j) in enumerate(BALL):
        value = rg2[n]
        other = pltpu.roll(value, HALF, 1)
        rhs2[0, pl.ds(row2(-2 * i, -4 * j), NY2), :] = jnp.where(low, value, other)
        rhs2[0, pl.ds(row2(1 - 2 * i, -4 * j), NY2), :] = jnp.where(low, other, value)
    coarse = chebyshev_weights(COARSE_SWEEPS)
    level2.first_from_zero(coarse[0], (it2_a, 0), -10, 22, -10, 24)
    src, dst = it2_a, it2_b
    for sweep in range(1, COARSE_SWEEPS):
        reach = COARSE_SWEEPS - 1 - sweep
        first_y, rows = (-10, 24) if reach > 3 else (-6, 16)
        level2.sweep(coarse[sweep], (src, 0), (dst, 0), -3 - reach, 8 + 2 * reach, first_y, rows, last=reach == 0)
        src, dst = dst, src

    def store_it1(k, to, value):
        it1_b[0, to, :] = value

    arrived(MID_ITER, rx1)
    mid_unpack(rx1, PLAN_M1, 1, store_it1)
    arrived(MID_WIDE, rwi)
    for n, (sx, sy) in enumerate(WIDE):
        start = WIDE_STARTS[n]
        for k in range(6):
            ref, field = (raw1, k) if k < 4 else ((rhs1, 0) if k == 4 else (it1_b, 0))
            for x, y, rows in wide_pieces(sx, sy):
                ref[field, pl.ds(row1(x - sx * NX1, y - sy * NY1), rows), :] = rwi[pl.ds(start, rows), :]
                start += rows
    level1.build(-5, 1, -8, 24)
    level1.build(7, 2, -8, 24)

    def lift1(big):
        stores = []
        for y in (-3, -1):
            value = src[0, pl.ds(row2(big, y), 8), :]
            for p in range(2):
                for q in range(2):
                    to = pl.ds(row1(2 * big + p, 2 * y + q), 8, stride=2)
                    stores.append((it1_a, (0, to), it1_b[0, to, :] + value))
        return stores

    plane_loop(-3, 8, lift1)
    level1.sweep(weights[0], (it1_a, 0), (it1_b, 0), -5, 14, -8, 24)
    level1.sweep(weights[1], (it1_b, 0), (it1_a, 0), -4, 12, -8, 24)
    level1.sweep(weights[2], (it1_a, 0), (it1_b, 0), -3, 10, -4, 16)
    level1.sweep(weights[3], (it1_b, 0), (it1_a, 0), -2, 8, -4, 16, last=True)

    arrived(FINE_BACK, riu)
    unpack(rest_b, 0, 2, riu, PLAN_U, 3, 3)

    def lift0(big):
        stores = []
        for y in (-2, 2):
            value = it1_a[0, pl.ds(row1(big, y), 8), :]
            for e in range(2):
                for p in range(2):
                    for q in range(2):
                        to = pl.ds(row0(2 * big + p, 2 * y + q), 8, stride=2)
                        stores.append((fine_b, (e, to), value))
        return stores

    plane_loop(-2, 8, lift0)
    level0.advance((0.0, weights[0][1]), fine_b, fine_a, rest_b, rest_b, total0, -3, 14, -4, 24, lift=True)
    level0.advance(weights[1], fine_a, fine_b, rest_b, rest_b, total0, -2, 12, -4, 24)
    level0.advance(weights[2], fine_b, fine_a, rest_b, rest_b, total0, -1, 10, -4, 24)
    back = HALF * ((at // 2) % 2) + at // 4
    even = (at % 2) == 0

    def emit(x, news):
        stores = []
        for half in range(2):
            pick = back + 32 * half
            lower = jnp.take_along_axis(news[0], pick, axis=1, mode="promise_in_bounds")
            upper = jnp.take_along_axis(news[1], pick, axis=1, mode="promise_in_bounds")
            stores.append((out_v, (x, slice(None), slice(half * LANES, (half + 1) * LANES)), jnp.where(even, lower, upper)))
        return stores

    level0.advance(weights[3], fine_a, None, rest_b, None, total0, 0, 8, 0, NY0, emit=emit)
    store = pltpu.make_async_copy(out_v, out_hbm, out_sem.at[0])
    store.start()
    for group, landing in enumerate((rfi, rra, rta, r2l.at[pl.ds(1, 10)], rmc, rg1, r2c, rg2, rx1, rwi, riu)):
        departed(group, landing)
    store.wait()


def solution(mesh):
    counts = (mesh.shape["gx"], mesh.shape["gy"])

    def local(source, initial, absorption, beta_x, beta_y, beta_z):
        f32 = jnp.float32
        v = lambda *shape: pltpu.VMEM(shape, f32)
        scratch = [
            v(6, NX0, NY0, 256), v(12, ROWS0, LANES), v(2, ROWS0, LANES), v(2, ROWS0, LANES),
            v(12, ROWS0, LANES), v(2, ROWS0, LANES), v(2, ROWS0, LANES), v(2, ROWS0, LANES), v(2, ROWS0, LANES), v(2, ROWS0, LANES),
            v(2, 128, LANES),
            v(4, ROWS1, LANES), v(6, ROWS1, LANES), v(1, ROWS1, LANES), v(1, ROWS1, LANES), v(1, ROWS1, LANES),
            v(1, ROWS1, LANES), v(1, ROWS1, LANES), v(32, LANES),
            v(4, ROWS2, LANES), v(6, ROWS2, LANES), v(1, ROWS2, LANES), v(1, ROWS2, LANES), v(1, ROWS2, LANES),
            v(1, ROWS2, LANES), v(1, ROWS2, LANES),
            v(SIZE_F, LANES), v(SIZE_F, LANES), v(SIZE_A, LANES), v(SIZE_A, LANES), v(SIZE_T, LANES), v(SIZE_T, LANES),
            v(128, LANES), v(4, 72, LANES), v(SIZE_M4, LANES),
            v(32, LANES), v(4, 24, LANES), v(SIZE_M1, LANES), v(32, LANES), v(4, 24, LANES), v(SIZE_M1, LANES),
            v(11, 16, LANES), v(42, 16, LANES), v(NY2, LANES), v(len(BALL), NY2, LANES),
            v(SIZE_U, LANES), v(SIZE_U, LANES), v(288, LANES), v(288, LANES), v(NX0, NY0, 256),
            pltpu.SemaphoreType.DMA((6,)), pltpu.SemaphoreType.DMA((1,)),
            pltpu.SemaphoreType.DMA((11,)), pltpu.SemaphoreType.DMA((11,)),
        ]
        call = pl.pallas_call(
            lambda *refs: kernel(counts, *refs),
            out_shape=jax.ShapeDtypeStruct((NX0, NY0, 256), f32),
            in_specs=[pl.BlockSpec(memory_space=pl.ANY)] * 6,
            out_specs=pl.BlockSpec(memory_space=pl.ANY),
            scratch_shapes=scratch,
            compiler_params=pltpu.CompilerParams(
                collective_id=0, has_side_effects=True, vmem_limit_bytes=56 * 2**20
            ),
            name="vcycle",
        )
        return call(absorption, beta_x, beta_y, beta_z, source, initial)

    return jax.shard_map(
        local,
        mesh=mesh,
        in_specs=(P("gx", "gy", None),) * 6,
        out_specs=P("gx", "gy", None),
        check_vma=False,
    )
```

```python
import jax
import jax.numpy as jnp
from jax import lax
from jax.experimental import pallas as pl
from jax.experimental.pallas import tpu as pltpu
from jax.sharding import PartitionSpec as P

SWEEPS = 4
COARSE_SWEEPS = 8
LANES = 128
HALF = 64
GROUP = 24
MESH = pl.DeviceIdType.MESH

NX0, NY0, HX0, HY0, YP0 = 8, 16, 5, 5, 26
NX1, NY1, HX1, HY1, YP1 = 4, 8, 6, 9, 26
NX2, NY2, HX2, HY2, YP2 = 2, 4, 10, 12, 28
ROWS0 = 472
ROWS1 = 416
ROWS2 = 616

DEPTH = 4
NEAR = [(-1, 0), (1, 0), (0, -1), (0, 1), (-1, -1), (-1, 1), (1, -1), (1, 1)]
WIDE = [(-2, 0), (2, 0), (-2, -1), (-2, 1), (2, -1), (2, 1)]
LINE = [1, -1, 2, -2, 3, -3, 4, -4, 5, -5]
COLUMNS = [(-1, 11), (1, 11), (-2, 7), (2, 7), (-3, 3), (3, 3)]


def ball_offsets():
    offsets = []
    for i in range(-5, 6):
        for j in range(-3, 4):
            far_x = 2 * abs(i) - 1 if i else 0
            far_y = 4 * abs(j) - 3 if j else 0
            if (i, j) != (0, 0) and far_x + far_y <= (11 if i and j else 10):
                offsets.append((i, j))
    return offsets


BALL = ball_offsets()


def chebyshev_weights(sweeps):
    cheb_theta = 1.125
    cheb_delta = 0.875
    cheb_sigma = cheb_theta / cheb_delta
    rho_old = 1.0 / cheb_sigma
    weights = [(0.0, 1.0 / cheb_theta)]
    for sweep in range(1, sweeps):
        rho_new = 1.0 / (2.0 * cheb_sigma - rho_old)
        weights.append((rho_new * rho_old, 2.0 * rho_new / cheb_delta))
        rho_old = rho_new
    return weights


def row0(x, y):
    return (x + HX0) * YP0 + y + HY0


def row1(x, y):
    return (x + HX1) * YP1 + y + HY1


def row2(x, y):
    return (x + HX2) * YP2 + y + HY2


def lanes(shape):
    return lax.broadcasted_iota(jnp.int32, shape, len(shape) - 1)


def shift_down(v):
    return jnp.where(lanes(v.shape) < HALF, pltpu.roll(v, HALF + 1, 1), pltpu.roll(v, HALF, 1))


def shift_up(v):
    return jnp.where(lanes(v.shape) < HALF, pltpu.roll(v, HALF, 1), pltpu.roll(v, HALF - 1, 1))


def z_neighbours(values, level):
    if level == 0:
        return (shift_down(values[1]), values[0]), (values[1], shift_up(values[0]))
    if level == 1:
        return (shift_down(values[0]),), (shift_up(values[0]),)
    return (pltpu.roll(values[0], 1, 1),), (pltpu.roll(values[0], LANES - 1, 1),)


def z_ends(shape, level, half):
    at = lanes(shape)
    if level == 0:
        return (at == 0) if half == 0 else None, (at == LANES - 1) if half == 1 else None
    if level == 1:
        return at == 0, at == LANES - 1
    return (at % HALF) == 0, (at % HALF) == HALF - 1


def plane_loop(first, count, body, group=GROUP):
    def several(start, n):
        stores = []
        for i in range(n):
            stores += body(start + i)
        for ref, index, value in stores:
            ref[index] = value

    def step(i, carry):
        several(first + group * i, group)
        return carry

    if count // group > 1:
        lax.fori_loop(0, count // group, step, 0)
        done = count // group * group
    else:
        done = 0
    if done < count:
        several(first + done, count - done)


class Level:
    def __init__(self, number, halves, row, pitch, raw, coef, diag, rhs, update):
        self.number, self.halves, self.row, self.pitch = number, halves, row, pitch
        self.raw, self.coef, self.diag, self.rhs, self.update = raw, coef, diag, rhs, update
        self.scale = 0.25**number

    def faces(self, at, rows):
        n, raw = self.halves, self.raw
        take = lambda k, e, shift=0: raw[k * n + e, pl.ds(at + shift, rows), :]
        low_z = [take(3, e) for e in range(n)]
        _, high_z = z_neighbours(low_z, self.number)
        out = []
        for e in range(n):
            _, top = z_ends((rows, LANES), self.number, e)
            upper = high_z[e] if top is None else jnp.where(top, 0.0, high_z[e])
            faces = [take(1, e), take(1, e, self.pitch), take(2, e), take(2, e, 1), low_z[e], upper]
            total = (faces[0] + faces[1]) + (faces[2] + faces[3]) + (faces[4] + faces[5])
            out.append((faces, take(0, e) + self.scale * total))
        return out

    def own_diagonal(self, x, y, rows):
        return [d for _, d in self.faces(self.row(x, y), rows)]

    def build(self, first_x, count, first_y, rows, source=None):
        n = self.halves

        def body(x):
            at = self.row(x, first_y)
            stores = []
            for e, (faces, diagonal) in enumerate(self.faces(at, rows)):
                inverse = 1.0 / diagonal
                low, _ = z_ends((rows, LANES), self.number, e)
                if low is not None:
                    faces[4] = jnp.where(low, 0.0, faces[4])
                scaled = self.scale * inverse
                for c in range(6):
                    stores.append((self.coef, (c * n + e, pl.ds(at, rows)), faces[c] * scaled))
                stores.append((self.diag, (e, pl.ds(at, rows)), diagonal))
                if source is not None:
                    ref, base = source
                    stores.append((self.rhs, (e, pl.ds(at, rows)), ref[base + e, pl.ds(at, rows), :] * inverse))
            return stores

        plane_loop(first_x, count, body)

    def stencil(self, src, at, rows):
        n = self.halves
        ref, base = src
        take = lambda e, shift=0: ref[base + e, pl.ds(at + shift, rows), :]
        centre = [take(e) for e in range(n)]
        below, above = z_neighbours(centre, self.number)
        out = []
        for e in range(n):
            c = lambda k: self.coef[k * n + e, pl.ds(at, rows), :]
            t_x = c(0) * take(e, -self.pitch) + c(1) * take(e, self.pitch)
            t_y = c(2) * take(e, -1) + c(3) * take(e, 1)
            t_z = c(4) * below[e] + c(5) * above[e]
            out.append((t_x + t_y) + t_z)
        return out, centre

    def residual(self, src, at, rows):
        sums, centre = self.stencil(src, at, rows)
        return [(self.rhs[e, pl.ds(at, rows), :] - centre[e]) + sums[e] for e in range(self.halves)], centre

    def advance(self, pair, src, dst, old, new, total, first_x, count, first_y, rows, lead=1.0, lift=False, emit=None):
        def body(x):
            at = self.row(x, first_y)
            here = pl.ds(at, rows)
            sums, centre = self.stencil((src, 0), at, rows)
            stores, news = [], []
            for e in range(self.halves):
                change = centre[e] - sums[e]
                rest = old[e, here, :] - (change if lead == 1.0 else lead * change)
                step = pair[1] * rest
                if pair[0] != 0.0:
                    step = (pair[0] * lead) * centre[e] + step
                iterate = total[e, here, :] + step
                if lift:
                    iterate = iterate + centre[e]
                news.append(iterate)
                if emit is None:
                    stores += [(new, (e, here), rest), (dst, (e, here), step), (total, (e, here), iterate)]
            return stores if emit is None else emit(x, news)

        plane_loop(first_x, count, body)

    def sweep(self, pair, src, dst, first_x, count, first_y, rows, last=False, emit=None):
        def body(x):
            at = self.row(x, first_y)
            steps, centre = self.residual(src, at, rows)
            news, stores = [], []
            for e in range(self.halves):
                new = pair[1] * steps[e]
                if pair[0] != 0.0:
                    new = pair[0] * self.update[e, pl.ds(at, rows), :] + new
                if not last:
                    stores.append((self.update, (e, pl.ds(at, rows)), new))
                news.append(centre[e] + new)
            if emit is not None:
                return emit(x, news)
            ref, base = dst
            return stores + [(ref, (base + e, pl.ds(at, rows)), news[e]) for e in range(self.halves)]

        plane_loop(first_x, count, body)

    def first_from_zero(self, pair, dst, first_x, count, first_y, rows):
        def body(x):
            at = self.row(x, first_y)
            ref, base = dst
            stores = []
            for e in range(self.halves):
                new = pair[1] * self.rhs[e, pl.ds(at, rows), :]
                stores.append((self.update, (e, pl.ds(at, rows)), new))
                stores.append((ref, (base + e, pl.ds(at, rows)), new))
            return stores

        plane_loop(first_x, count, body)


def corner_pieces(sx, sy, depth):
    pieces = []
    for dx in range(1, depth):
        rows = depth - dx
        pieces.append((NX0 - dx if sx > 0 else dx - 1, NY0 - rows if sy > 0 else 0, rows))
    return pieces


def side_plane(sx, dx):
    return NX0 - dx if sx > 0 else dx - 1


def side_row(sy, dy):
    return NY0 - dy if sy > 0 else dy - 1


def near_plan(fields, planes, depth, extra=(0, 0)):
    sizes = [fields * planes * NY0 + extra[0], fields * planes * NY0 + extra[1]]
    sizes += [fields * depth * NX0] * 2 + [-(-fields * corner_rows(depth) // 8) * 8] * 4
    starts = [sum(sizes[:n]) for n in range(8)]
    return list(zip(starts, sizes)), sum(sizes)


def corner_rows(depth):
    return depth * (depth - 1) // 2


def mid_corner(sx, sy):
    for dx in range(1, NX1 + 1):
        rows = 7 - dx
        yield (NX1 - dx if sx > 0 else dx - 1), (NY1 - rows if sy > 0 else 0), rows


def mid_plan(fields):
    sizes = [fields * NX1 * NY1] * 4 + [-(-fields * 18 // 8) * 8] * 4
    return list(zip([sum(sizes[:n]) for n in range(8)], sizes)), sum(sizes)


def wide_pieces(sx, sy):
    for dx in range(2):
        x = NX1 - 1 - dx if sx > 0 else dx
        if sy == 0:
            yield x, 0, NY1
        else:
            yield x, (NY1 - 2 if sy > 0 else 0), 2


WIDE_SIZES = [96, 96, 24, 24, 24, 24]
WIDE_STARTS = [sum(WIDE_SIZES[:n]) for n in range(6)]
FIRST, RAW, FINE_REST, LOW_LINE, MID_COEF, MID_RHS, LOW_COEF, LOW_RHS, MID_ITER, MID_WIDE, FINE_BACK = range(11)
PLAN_M4, SIZE_M4 = mid_plan(4)
PLAN_M1, SIZE_M1 = mid_plan(1)
PLAN_F, SIZE_F = [(0, 64), (64, 32), (96, 32), (128, 16)], 144
PLAN_A, SIZE_A = near_plan(8, 3, DEPTH, (32, 0))
PLAN_T, SIZE_T = near_plan(2, 4, DEPTH)
PLAN_U, SIZE_U = near_plan(2, 3, 3)


def kernel(counts, *refs):
    inputs, out_hbm = refs[:6], refs[6]
    (nat, fine, fine_a, fine_b, coef0, diag0, rhs0, rest_a, rest_b, total0, rest0,
     raw1, coef1, diag1, rhs1, upd1, it1_a, it1_b, rest1,
     raw2, coef2, diag2, rhs2, upd2, it2_a, it2_b,
     sfi, rfi, sra, rra, sta, rta, smc, cmc, rmc, sg1, cg1, rg1, sx1, cx1, rx1, r2l, r2c, sg2, rg2, siu, riu, swi, rwi, out_v,
     in_sem, out_sem, sent, got) = refs[7:]
    count_x, count_y = counts
    me_x, me_y = lax.axis_index("gx"), lax.axis_index("gy")

    def device(offset):
        return (lax.rem(me_x + offset[0] + count_x, count_x), lax.rem(me_y + offset[1] + count_y, count_y))

    loads = [pltpu.make_async_copy(inputs[k], nat.at[k], in_sem.at[k]) for k in range(6)]
    for load in loads:
        load.start()
    barrier = pltpu.get_barrier_semaphore()
    for offset in NEAR + [o for o in BALL if o not in NEAR]:
        pl.semaphore_signal(barrier, inc=1, device_id=device(offset), device_id_type=MESH)

    def send(group, src, dst, offset):
        pltpu.make_async_remote_copy(
            src_ref=src, dst_ref=dst, send_sem=sent.at[group], recv_sem=got.at[group],
            device_id=device(offset), device_id_type=MESH,
        ).start()

    def arrived(group, landing):
        pltpu.make_async_copy(landing, landing, got.at[group]).wait()

    def departed(group, landing):
        pltpu.make_async_copy(landing, landing, sent.at[group]).wait()

    level0 = Level(0, 2, row0, YP0, fine, coef0, diag0, rhs0, None)
    level1 = Level(1, 1, row1, YP1, raw1, coef1, diag1, rhs1, upd1)
    level2 = Level(2, 1, row2, YP2, raw2, coef2, diag2, rhs2, upd2)

    at = lanes((NY0, LANES))
    cell = 4 * (at % HALF) + 2 * (at // HALF)
    from_first = (at % HALF) < HALF // 2
    picks = [(cell + e) % LANES for e in range(2)]

    def permute(k):
        def body(x):
            first = nat[k, x, :, 0:LANES]
            second = nat[k, x, :, LANES : 2 * LANES]
            stores = []
            for e in range(2):
                low = jnp.take_along_axis(first, picks[e], axis=1, mode="promise_in_bounds")
                high = jnp.take_along_axis(second, picks[e], axis=1, mode="promise_in_bounds")
                stores.append((fine, (2 * k + e, pl.ds(row0(x, 0), NY0)), jnp.where(from_first, low, high)))
            return stores

        plane_loop(0, NX0, body)

    def near_rows(i, plan, planes, depth):
        for n, (sx, sy) in enumerate(NEAR):
            shift = -(sx * NX0 * YP0 + sy * NY0)
            start = plan[n][0]
            if n < 2:
                for dx in range(1, planes + 1):
                    at_buffer = pl.multiple_of(start + (i * planes + dx - 1) * NY0, 8)
                    yield row0(side_plane(sx, dx), 0), NY0, None, shift, at_buffer
            elif n < 4:
                for dy in range(1, depth + 1):
                    at_buffer = pl.multiple_of(start + (i * depth + dy - 1) * NX0, 8)
                    yield row0(0, side_row(sy, dy)), NX0, YP0, shift, at_buffer
            else:
                at_buffer = start + i * corner_rows(depth)
                for x, y, rows in corner_pieces(sx, sy, depth):
                    yield row0(x, y), rows, None, shift, at_buffer
                    at_buffer = at_buffer + rows

    def pack(field, first, count, out, plan, planes, depth):
        def body(i, carry):
            values = []
            for row, rows, stride, _, to in near_rows(i, plan, planes, depth):
                values.append((to, rows, field[first + i, pl.ds(row, rows, stride=stride), :]))
            for to, rows, value in values:
                out[pl.ds(to, rows), :] = value
            return carry

        lax.fori_loop(0, count, body, 0)

    def unpack(field, first, count, landing, plan, planes, depth):
        def body(i, carry):
            values = []
            for row, rows, stride, shift, at_buffer in near_rows(i, plan, planes, depth):
                values.append((pl.ds(row + shift, rows, stride=stride), landing[pl.ds(at_buffer, rows), :]))
            for to, value in values:
                field[first + i, to, :] = value
            return carry

        lax.fori_loop(0, count, body, 0)

    def extra_pieces(k, plan, base, sides):
        for side in sides:
            sx = NEAR[side][0]
            for e in range(2):
                row = row0(side_plane(sx, DEPTH), 0)
                yield k + e, row, row - sx * NX0 * YP0, plan[side][0] + base + e * NY0

    def extra_out(field, k, out, plan, base, sides):
        for f, row, _, to in extra_pieces(k, plan, base, sides):
            out[pl.ds(to, NY0), :] = field[f, pl.ds(row, NY0), :]

    def extra_in(field, k, landing, plan, base, sides):
        for f, _, row, at_buffer in extra_pieces(k, plan, base, sides):
            field[f, pl.ds(row, NY0), :] = landing[pl.ds(at_buffer, NY0), :]

    def near_sends(group, out, landing, plan):
        for (start, rows), offset in zip(plan, NEAR):
            cut = pl.ds(start, rows)
            send(group, out.at[cut], landing.at[cut], offset)

    def first_pieces():
        for n, (sx, sy) in enumerate(NEAR[:4]):
            fields = (10, 11) + ((2, 3) if n == 0 else (4, 5) if n == 2 else ())
            for i, k in enumerate(fields):
                shift = -(sx * NX0 * YP0 + sy * NY0)
                if n < 2:
                    yield k, row0(side_plane(sx, 1), 0), NY0, None, shift, PLAN_F[n][0] + i * NY0
                else:
                    yield k, row0(0, side_row(sy, 1)), NX0, YP0, shift, PLAN_F[n][0] + i * NX0

    weights = chebyshev_weights(SWEEPS)
    for k in (5, 1, 2):
        loads[k].wait()
        permute(k)
    for k, row, rows, stride, _, to in first_pieces():
        sfi[pl.ds(to, rows), :] = fine[k, pl.ds(row, rows, stride=stride), :]
    pl.semaphore_wait(barrier, len(BALL))
    near_sends(FIRST, sfi, rfi, PLAN_F)
    for k in (0, 3):
        loads[k].wait()
        permute(k)
    pack(fine, 0, 8, sra, PLAN_A, 3, DEPTH)
    extra_out(fine, 2, sra, PLAN_A, 384, (0,))
    near_sends(RAW, sra, rra, PLAN_A)
    loads[4].wait()
    permute(4)

    def children(k, e, x, y_step):
        return fine[2 * k + e, pl.ds(row0(x, y_step), NY1, stride=2), :]

    def coarsen1(big):
        to = pl.ds(row1(big, 0), NY1)
        x = 2 * big
        absorb = sum(children(0, e, x + p, q) for e in range(2) for p in range(2) for q in range(2)) * 0.125
        face_x = sum(children(1, e, x, q) for e in range(2) for q in range(2)) * 0.25
        face_y = sum(children(2, e, x + p, 0) for e in range(2) for p in range(2)) * 0.25
        face_z = sum(children(3, 0, x + p, q) for p in range(2) for q in range(2)) * 0.25
        for k, value in enumerate((absorb, face_x, face_y, face_z)):
            raw1[k, to, :] = value
            smc[pl.ds(k * 32 + big * NY1, NY1), :] = value

    for big in range(NX1):
        coarsen1(big)

    def mid_sends(group, own, corner, landing, plan, fields):
        for n, offset in enumerate(NEAR[4:]):
            to = 0
            for k in range(fields):
                for x, y, rows in mid_corner(*offset):
                    corner[n, pl.ds(to, rows), :] = own[pl.ds(k * 32 + x * NY1 + y, rows), :]
                    to += rows
        for n, ((start, rows), offset) in enumerate(zip(plan, NEAR)):
            send(group, own if n < 4 else corner.at[n - 4], landing.at[pl.ds(start, rows)], offset)

    def mid_unpack(landing, plan, fields, store):
        for n, ((start, _), (sx, sy)) in enumerate(zip(plan, NEAR)):
            for k in range(fields):
                pieces = mid_corner(sx, sy) if n >= 4 else ((x, 0, NY1) for x in range(NX1))
                for x, y, rows in pieces:
                    store(k, pl.ds(row1(x - sx * NX1, y - sy * NY1), rows), landing[pl.ds(start, rows), :])
                    start += rows

    def both(v):
        return v + pltpu.roll(v, HALF, 1)

    for big in range(NX2):
        grand = lambda k, x, q: raw1[k, pl.ds(row1(x, q), NY2, stride=2), :]
        x = 2 * big
        absorb = both(sum(grand(0, x + p, q) for p in range(2) for q in range(2))) * 0.125
        face_x = both(sum(grand(1, x, q) for q in range(2))) * 0.25
        face_y = both(sum(grand(2, x + p, 0) for p in range(2))) * 0.25
        face_z = sum(grand(3, x + p, q) for p in range(2) for q in range(2)) * 0.25
        low = lanes((NY2, LANES)) < HALF
        face_z = jnp.where(low, face_z, pltpu.roll(face_z, HALF, 1))
        for k, value in enumerate((absorb, face_x, face_y, face_z)):
            raw2[k, pl.ds(row2(big, 0), NY2), :] = value
        r2l[0, pl.ds(big * NY2, NY2), :] = jnp.where(low, absorb, face_x)
        r2l[0, pl.ds(8 + big * NY2, NY2), :] = jnp.where(low, face_y, face_z)

    def ball_sends(group, src, landing):
        for n, offset in enumerate(BALL):
            send(group, src, landing.at[n], offset)

    arrived(FIRST, rfi)
    for k, row, rows, stride, shift, at_buffer in first_pieces():
        fine[k, pl.ds(row + shift, rows, stride=stride), :] = rfi[pl.ds(at_buffer, rows), :]
    level0.build(0, NX0, 0, NY0, (fine, 8))

    def first_sweep(x):
        here = pl.ds(row0(x, 0), NY0)
        steps, centre = level0.residual((fine, 10), row0(x, 0), NY0)
        stores = []
        for e in range(2):
            stores.append((rest_a, (e, here), steps[e]))
            stores.append((total0, (e, here), centre[e] + weights[0][1] * steps[e]))
        return stores

    plane_loop(0, NX0, first_sweep)
    pack(rest_a, 0, 2, sta, PLAN_T, 4, DEPTH)
    near_sends(FINE_REST, sta, rta, PLAN_T)
    for n, i in enumerate(LINE):
        send(LOW_LINE, r2l.at[0], r2l.at[n + 1], (i, 0))
    mid_sends(MID_COEF, smc, cmc, rmc, PLAN_M4, 4)

    face_x = sum(children(1, e, NX0, q) for e in range(2) for q in range(2)) * 0.25
    raw1[1, pl.ds(row1(NX1, 0), NY1), :] = face_x
    face_y = sum(fine[4 + e, pl.ds(row0(p, NY0), NX1, stride=2 * YP0), :] for e in range(2) for p in range(2)) * 0.25
    raw1[2, pl.ds(row1(0, NY1), NX1, stride=YP1), :] = face_y
    diag_own1 = [level1.own_diagonal(big, 0, NY1)[0] for big in range(NX1)]
    x = NX1
    grand = lambda k, x, y: raw1[k, pl.ds(row1(x, y), NY2, stride=2), :]
    raw2[1, pl.ds(row2(NX2, 0), NY2), :] = both(grand(1, x, 0) + grand(1, x, 1)) * 0.25
    for big in range(NX2):
        above = both(sum(grand(2, 2 * big + p, NY1) for p in range(2))) * 0.25
        raw2[2, pl.ds(row2(big, NY2), 1), :] = above[0:1]
    diag_own2 = [level2.own_diagonal(big, 0, NY2)[0] for big in range(NX2)]

    arrived(RAW, rra)
    unpack(fine, 0, 8, rra, PLAN_A, 3, DEPTH)
    extra_in(fine, 2, rra, PLAN_A, 384, (0,))
    level0.build(-3, 14, -4, 24)
    arrived(FINE_REST, rta)
    unpack(rest_a, 0, 2, rta, PLAN_T, 4, DEPTH)
    level0.advance(weights[1], rest_a, fine_a, rest_a, rest_b, total0, -3, 14, -4, 24, lead=weights[0][1])
    level0.advance(weights[2], fine_a, fine_b, rest_b, rest_b, total0, -2, 12, -4, 24)
    level0.advance(weights[3], fine_b, fine_a, rest_b, rest_b, total0, -1, 10, -4, 24)

    def rest_fine(x):
        here = pl.ds(row0(x, 0), NY0)
        sums, centre = level0.stencil((fine_a, 0), row0(x, 0), NY0)
        stores = []
        for e in range(2):
            rest = rest_b[e, here, :] - (centre[e] - sums[e])
            stores.append((rest_b, (e, here), rest))
            stores.append((rest0, (e, pl.ds(x * NY0, NY0)), rest * diag0[e, here, :]))
        return stores

    plane_loop(0, NX0, rest_fine)
    for big in range(NX1):
        total = sum(
            rest0[e, pl.ds((2 * big + p) * NY0 + q, NY1, stride=2), :]
            for e in range(2) for p in range(2) for q in range(2)
        )
        value = total * 0.125 / diag_own1[big]
        rhs1[0, pl.ds(row1(big, 0), NY1), :] = value
        sg1[pl.ds(big * NY1, NY1), :] = value

    mid_sends(MID_RHS, sg1, cg1, rg1, PLAN_M1, 1)
    arrived(LOW_LINE, r2l.at[pl.ds(1, 10)])
    start = 0
    for j, slots in COLUMNS:
        send(LOW_COEF, r2l.at[pl.ds(0, slots)], r2c.at[pl.ds(start, slots)], (0, j))
        start += slots

    pack(rest_b, 0, 2, siu, PLAN_U, 3, 3)
    near_sends(FINE_BACK, siu, riu, PLAN_U)
    arrived(MID_COEF, rmc)

    def store_raw(k, to, value):
        raw1[k, to, :] = value

    mid_unpack(rmc, PLAN_M4, 4, store_raw)
    level1.build(-4, 11, -8, 24)

    def store_rhs1(k, to, value):
        rhs1[0, to, :] = value

    arrived(MID_RHS, rg1)
    mid_unpack(rg1, PLAN_M1, 1, store_rhs1)
    level1.first_from_zero(weights[0], (it1_a, 0), -4, 12, -4, 16)
    level1.sweep(weights[1], (it1_a, 0), (it1_b, 0), -3, 10, -4, 16)
    level1.sweep(weights[2], (it1_b, 0), (it1_a, 0), -2, 8, -4, 16)
    level1.sweep(weights[3], (it1_a, 0), (it1_b, 0), -1, 6, -4, 16, last=True)

    def rest_mid(x):
        at_row = row1(x, 0)
        steps, centre = level1.residual((it1_b, 0), at_row, NY1)
        return [
            (rest1, (pl.ds(x * NY1, NY1),), steps[0] * diag1[0, pl.ds(at_row, NY1), :]),
            (sx1, (pl.ds(x * NY1, NY1),), centre[0]),
        ]

    plane_loop(0, NX1, rest_mid)
    rhs_own2 = []
    for big in range(NX2):
        total = sum(rest1[pl.ds((2 * big + p) * NY1 + q, NY2, stride=2), :] for p in range(2) for q in range(2))
        rhs_own2.append(both(total) * 0.125 / diag_own2[big])
        rhs2[0, pl.ds(row2(big, 0), NY2), :] = rhs_own2[big]
    sg2[...] = jnp.where(low, rhs_own2[0], rhs_own2[1])

    ball_sends(LOW_RHS, sg2, rg2)
    mid_sends(MID_ITER, sx1, cx1, rx1, PLAN_M1, 1)
    for n, offset in enumerate(WIDE):
        to = WIDE_STARTS[n]
        for k in range(6):
            own, base = ((smc, 32 * k), (sg1, 0), (sx1, 0))[max(k - 3, 0)]
            for x, y, rows in wide_pieces(*offset):
                swi[pl.ds(to, rows), :] = own[pl.ds(base + x * NY1 + y, rows), :]
                to += rows
        cut = pl.ds(WIDE_STARTS[n], WIDE_SIZES[n])
        send(MID_WIDE, swi.at[cut], rwi.at[cut], offset)

    arrived(LOW_COEF, r2c)
    low8 = lanes((8, LANES)) < HALF

    def two_fields(value):
        other = pltpu.roll(value, HALF, 1)
        return jnp.where(low8, value, other), jnp.where(low8, other, value)

    def low_unpack(ref, slot, i, j):
        for part in range(2):
            for k, full in enumerate(two_fields(ref[slot, pl.ds(8 * part, 8), :])):
                for p in range(NX2):
                    to = pl.ds(row2(p - 2 * i, -4 * j), NY2)
                    raw2[2 * part + k, to, :] = full[p * NY2 : (p + 1) * NY2]

    for n, i in enumerate(LINE):
        low_unpack(r2l, n + 1, i, 0)
    start = 0
    for j, slots in COLUMNS:
        for n, i in enumerate(([0] + LINE)[:slots]):
            low_unpack(r2c, start + n, i, j)
        start += slots
    level2.build(-9, 20, -10, 24)
    arrived(LOW_RHS, rg2)
    for n, (i, j) in enumerate(BALL):
        value = rg2[n]
        other = pltpu.roll(value, HALF, 1)
        rhs2[0, pl.ds(row2(-2 * i, -4 * j), NY2), :] = jnp.where(low, value, other)
        rhs2[0, pl.ds(row2(1 - 2 * i, -4 * j), NY2), :] = jnp.where(low, other, value)
    coarse = chebyshev_weights(COARSE_SWEEPS)
    level2.first_from_zero(coarse[0], (it2_a, 0), -10, 22, -10, 24)
    src, dst = it2_a, it2_b
    for sweep in range(1, COARSE_SWEEPS):
        reach = COARSE_SWEEPS - 1 - sweep
        first_y, rows = (-10, 24) if reach > 3 else (-6, 16)
        level2.sweep(coarse[sweep], (src, 0), (dst, 0), -3 - reach, 8 + 2 * reach, first_y, rows, last=reach == 0)
        src, dst = dst, src

    def store_it1(k, to, value):
        it1_b[0, to, :] = value

    arrived(MID_ITER, rx1)
    mid_unpack(rx1, PLAN_M1, 1, store_it1)
    arrived(MID_WIDE, rwi)
    for n, (sx, sy) in enumerate(WIDE):
        start = WIDE_STARTS[n]
        for k in range(6):
            ref, field = (raw1, k) if k < 4 else ((rhs1, 0) if k == 4 else (it1_b, 0))
            for x, y, rows in wide_pieces(sx, sy):
                ref[field, pl.ds(row1(x - sx * NX1, y - sy * NY1), rows), :] = rwi[pl.ds(start, rows), :]
                start += rows
    level1.build(-5, 1, -8, 24)
    level1.build(7, 2, -8, 24)

    def lift1(big):
        stores = []
        for y in (-3, -1):
            value = src[0, pl.ds(row2(big, y), 8), :]
            for p in range(2):
                for q in range(2):
                    to = pl.ds(row1(2 * big + p, 2 * y + q), 8, stride=2)
                    stores.append((it1_a, (0, to), it1_b[0, to, :] + value))
        return stores

    plane_loop(-3, 8, lift1)
    level1.sweep(weights[0], (it1_a, 0), (it1_b, 0), -5, 14, -8, 24)
    level1.sweep(weights[1], (it1_b, 0), (it1_a, 0), -4, 12, -8, 24)
    level1.sweep(weights[2], (it1_a, 0), (it1_b, 0), -3, 10, -4, 16)
    level1.sweep(weights[3], (it1_b, 0), (it1_a, 0), -2, 8, -4, 16, last=True)

    arrived(FINE_BACK, riu)
    unpack(rest_b, 0, 2, riu, PLAN_U, 3, 3)

    def lift0(big):
        stores = []
        for y in (-2, 2):
            value = it1_a[0, pl.ds(row1(big, y), 8), :]
            for e in range(2):
                for p in range(2):
                    for q in range(2):
                        to = pl.ds(row0(2 * big + p, 2 * y + q), 8, stride=2)
                        stores.append((fine_b, (e, to), value))
        return stores

    plane_loop(-2, 8, lift0)
    level0.advance((0.0, weights[0][1]), fine_b, fine_a, rest_b, rest_b, total0, -3, 14, -4, 24, lift=True)
    level0.advance(weights[1], fine_a, fine_b, rest_b, rest_b, total0, -2, 12, -4, 24)
    level0.advance(weights[2], fine_b, fine_a, rest_b, rest_b, total0, -1, 10, -4, 24)
    back = HALF * ((at // 2) % 2) + at // 4
    even = (at % 2) == 0

    def emit(x, news):
        stores = []
        for half in range(2):
            pick = back + 32 * half
            lower = jnp.take_along_axis(news[0], pick, axis=1, mode="promise_in_bounds")
            upper = jnp.take_along_axis(news[1], pick, axis=1, mode="promise_in_bounds")
            stores.append((out_v, (x, slice(None), slice(half * LANES, (half + 1) * LANES)), jnp.where(even, lower, upper)))
        return stores

    level0.advance(weights[3], fine_a, None, rest_b, None, total0, 0, 8, 0, NY0, emit=emit)
    store = pltpu.make_async_copy(out_v, out_hbm, out_sem.at[0])
    store.start()
    for group, landing in enumerate((rfi, rra, rta, r2l.at[pl.ds(1, 10)], rmc, rg1, r2c, rg2, rx1, rwi, riu)):
        departed(group, landing)
    store.wait()


def solution(mesh):
    counts = (mesh.shape["gx"], mesh.shape["gy"])

    def local(source, initial, absorption, beta_x, beta_y, beta_z):
        f32 = jnp.float32
        v = lambda *shape: pltpu.VMEM(shape, f32)
        scratch = [
            v(6, NX0, NY0, 256), v(12, ROWS0, LANES), v(2, ROWS0, LANES), v(2, ROWS0, LANES),
            v(12, ROWS0, LANES), v(2, ROWS0, LANES), v(2, ROWS0, LANES), v(2, ROWS0, LANES), v(2, ROWS0, LANES), v(2, ROWS0, LANES),
            v(2, 128, LANES),
            v(4, ROWS1, LANES), v(6, ROWS1, LANES), v(1, ROWS1, LANES), v(1, ROWS1, LANES), v(1, ROWS1, LANES),
            v(1, ROWS1, LANES), v(1, ROWS1, LANES), v(32, LANES),
            v(4, ROWS2, LANES), v(6, ROWS2, LANES), v(1, ROWS2, LANES), v(1, ROWS2, LANES), v(1, ROWS2, LANES),
            v(1, ROWS2, LANES), v(1, ROWS2, LANES),
            v(SIZE_F, LANES), v(SIZE_F, LANES), v(SIZE_A, LANES), v(SIZE_A, LANES), v(SIZE_T, LANES), v(SIZE_T, LANES),
            v(128, LANES), v(4, 72, LANES), v(SIZE_M4, LANES),
            v(32, LANES), v(4, 24, LANES), v(SIZE_M1, LANES), v(32, LANES), v(4, 24, LANES), v(SIZE_M1, LANES),
            v(11, 16, LANES), v(42, 16, LANES), v(NY2, LANES), v(len(BALL), NY2, LANES),
            v(SIZE_U, LANES), v(SIZE_U, LANES), v(288, LANES), v(288, LANES), v(NX0, NY0, 256),
            pltpu.SemaphoreType.DMA((6,)), pltpu.SemaphoreType.DMA((1,)),
            pltpu.SemaphoreType.DMA((11,)), pltpu.SemaphoreType.DMA((11,)),
        ]
        call = pl.pallas_call(
            lambda *refs: kernel(counts, *refs),
            out_shape=jax.ShapeDtypeStruct((NX0, NY0, 256), f32),
            in_specs=[pl.BlockSpec(memory_space=pl.ANY)] * 6,
            out_specs=pl.BlockSpec(memory_space=pl.ANY),
            scratch_shapes=scratch,
            compiler_params=pltpu.CompilerParams(
                collective_id=0, has_side_effects=True, vmem_limit_bytes=56 * 2**20
            ),
            name="vcycle",
        )
        return call(absorption, beta_x, beta_y, beta_z, source, initial)

    return jax.shard_map(
        local,
        mesh=mesh,
        in_specs=(P("gx", "gy", None),) * 6,
        out_specs=P("gx", "gy", None),
        check_vma=False,
    )
```
